32 devices in a mesh: dp: 8 (over z, x), mx: 2 (over y), my: 2 (over core).
Axes of the slice: x: 2, y: 2, z: 4, core: 2. Of those that a mesh axis runs over, the one named last changes fastest.
Arguments:
- layer_input: bfloat16 [32768, 768], P(('dp', 'mx', 'my')), may hold values from -6 to 6
- w_qkv: bfloat16 [768, 2304], P('mx', 'my'), may hold values from -0.21875 to 0.21875
- b_qkv: bfloat16 [2304], P(('mx', 'my')), may hold values from -3 to 3
- w_out: bfloat16 [768, 768], P('mx', 'my'), may hold values from -0.875 to 0.875
- b_out: bfloat16 [768], P(('mx', 'my')), may hold values from -2 to 2
- ln1_gain: bfloat16 [768], P(('mx', 'my')), may hold values from 0.5 to 1.5
- ln1_bias: bfloat16 [768], P(('mx', 'my')), may hold values from -2 to 2
- w_up: bfloat16 [768, 3072], P('mx', 'my'), may hold values from -0.21875 to 0.21875
- b_up: bfloat16 [3072], P(('mx', 'my')), may hold values from -3 to 3
- w_down: bfloat16 [3072, 768], P('mx', 'my'), may hold values from -0.109375 to 0.109375
- b_down: bfloat16 [768], P(('mx', 'my')), may hold values from -2 to 2
- ln2_gain: bfloat16 [768], P(('mx', 'my')), may hold values from 0.5 to 1.5
- ln2_bias: bfloat16 [768], P(('mx', 'my')), may hold values from -2 to 2
- segment_ids: int32 [32768], P(('dp', 'mx', 'my')), may hold values from 0 to 7, as said below
- doc_lengths: int32 [32, 8], P(('dp', 'mx', 'my')), may hold values from 1 to 1017, as said below
- cotangent: bfloat16 [32768, 768], P(('dp', 'mx', 'my')), may hold values from -6 to 6
Outputs:
- block_out: bfloat16 [32768, 768], P(('dp', 'mx', 'my'))
- input_grad: bfloat16 [32768, 768], P(('dp', 'mx', 'my'))
- grad_w_qkv: float32 [768, 2304], P('mx', 'my')
- grad_b_qkv: float32 [2304], P(('mx', 'my'))
- grad_w_out: float32 [768, 768], P('mx', 'my')
- grad_b_out: float32 [768], P(('mx', 'my'))
- grad_ln1_gain: float32 [768], P(('mx', 'my'))
- grad_ln1_bias: float32 [768], P(('mx', 'my'))
- grad_w_up: float32 [768, 3072], P('mx', 'my')
- grad_b_up: float32 [3072], P(('mx', 'my'))
- grad_w_down: float32 [3072, 768], P('mx', 'my')
- grad_b_down: float32 [768], P(('mx', 'my'))
- grad_ln2_gain: float32 [768], P(('mx', 'my'))
- grad_ln2_bias: float32 [768], P(('mx', 'my'))
The draws below stay inside these ranges and needn't reach their ends.
Inputs may be any that keep to these rules, and one draw needn't show every extreme that they name: Each sequence of 1024 tokens holds exactly 8 documents back to back; segment_ids starts at 0 at each sequence's first token and rises by one at each document's first token. `doc_lengths`: A sequence's lengths sum to 1024 and are the lengths of its documents in order, as segment_ids lays them out.
All inputs are finite; a program needn't handle non-finite values.
Results may differ from the reference program's by a relative error of at most 0.018.
Values may be sent and summed in bfloat16 or wider, within the bound.
No kernel may reach another device: no remote copies, remote signals or barrier semaphores. Data moves between devices by JAX's collectives and lax.ppermute only.
A program may use at most 192 MiB of HBM per device.

```python
import math
import jax
import jax.numpy as jnp
from jax import lax

D = 768
FF = 3072
HEADS = 12
HD = 64
LEN = 1024
DOCS = 8
NSEQ = 32
TOKENS = 32768


def doc_table(key):
    table_key = jax.random.fold_in(key, 11)
    key_power, key_factor = jax.random.split(table_key)
    powers = jax.random.randint(key_power, (NSEQ, DOCS), 0, 7)
    factor = jax.random.randint(key_factor, (NSEQ, DOCS), 1, 4)
    weights = factor * jnp.left_shift(jnp.ones_like(powers), powers)
    leftover = LEN - DOCS
    shares = 1 + weights * leftover // jnp.sum(weights, axis=1, keepdims=True)
    missing = LEN - jnp.sum(shares, axis=1, keepdims=True)
    final_doc = (jnp.arange(DOCS) == DOCS - 1).astype(jnp.int32)
    drawn = shares + final_doc[None, :] * missing
    first_doc = (jnp.arange(DOCS) == 0).astype(jnp.int32)
    extreme = 1 + first_doc * (LEN - DOCS)
    first_seq = (jnp.arange(NSEQ) == 0)[:, None]
    return jnp.where(first_seq, extreme[None, :], drawn).astype(jnp.int32)


def draw_doc_lengths(key, part):
    return doc_table(key)


def draw_segment_ids(key, part):
    spans = doc_table(key)
    starts = jnp.cumsum(spans, axis=1) - spans
    places = jnp.arange(LEN, dtype=jnp.int32)
    passed = places[None, :, None] >= starts[:, None, 1:]
    return jnp.sum(passed.astype(jnp.int32), axis=-1).reshape(NSEQ * LEN).astype(jnp.int32)


def steps_of(rng, dims, cuts, low, top_value):
    def one(dim, parts):
        heights = jax.random.uniform(jax.random.fold_in(jax.random.fold_in(rng, 6), dim), (parts,), jnp.float32, low / len(cuts), top_value / len(cuts))
        return jnp.repeat(jnp.exp(heights), dims[dim] // parts).reshape((-1,) + (1,) * (len(dims) - dim - 1))

    loudness = one(*cuts[0])
    for cut in cuts[1:]:
        loudness = loudness * one(*cut)
    return loudness


def centred(rng, shape, scale, most, cuts=(), held_as=jnp.bfloat16):
    drawn = scale * jax.random.normal(rng, shape, jnp.float32)
    if cuts:
        drawn = drawn * steps_of(rng, shape, cuts, -0.22, 0.18)
    return jnp.clip(drawn, -most, most).astype(held_as)


def setup_inputs(seed: int = 0) -> dict:
    key_of = jax.random.split(jax.random.key(seed), 17)
    layer_input = centred(key_of[0], (TOKENS, D), 1.0, 6.0, ((0, 32),))
    w_qkv = centred(key_of[1], (D, 3 * D), D ** -0.5, 0.21875, ((0, 2), (1, 2)))
    b_qkv = centred(key_of[2], (3 * D,), 0.5, 3.0, ((0, 4),))
    w_out = centred(key_of[3], (D, D), (D // 16) ** -0.5, 0.875, ((0, 2), (1, 2)))
    b_out = centred(key_of[4], (D,), 0.3, 2.0, ((0, 4),))
    ln1_gain = jnp.clip(1.0 + 0.1 * jax.random.normal(key_of[5], (D,), jnp.float32), 0.5, 1.5).astype(jnp.bfloat16)
    ln1_bias = centred(key_of[6], (D,), 0.3, 2.0, ((0, 4),))
    w_up = centred(key_of[7], (D, FF), D ** -0.5, 0.21875, ((0, 2), (1, 2)))
    b_up = centred(key_of[8], (FF,), 0.5, 3.0, ((0, 4),))
    w_down = centred(key_of[9], (FF, D), FF ** -0.5, 0.109375, ((0, 2), (1, 2)))
    b_down = centred(key_of[10], (D,), 0.3, 2.0, ((0, 4),))
    ln2_gain = jnp.clip(1.0 + 0.1 * jax.random.normal(key_of[11], (D,), jnp.float32), 0.5, 1.5).astype(jnp.bfloat16)
    ln2_bias = centred(key_of[12], (D,), 0.3, 2.0, ((0, 4),))
    segment_ids = draw_segment_ids(jax.random.fold_in(key_of[16], 71), 0)
    doc_lengths = draw_doc_lengths(jax.random.fold_in(key_of[16], 71), 0)
    cotangent = centred(key_of[15], (TOKENS, D), 1.0, 6.0, ((0, 32),))
    return dict(layer_input=layer_input, w_qkv=w_qkv, b_qkv=b_qkv, w_out=w_out, b_out=b_out, ln1_gain=ln1_gain, ln1_bias=ln1_bias, w_up=w_up, b_up=b_up, w_down=w_down, b_down=b_down, ln2_gain=ln2_gain, ln2_bias=ln2_bias, segment_ids=segment_ids, doc_lengths=doc_lengths, cotangent=cotangent)


norm_eps = 1e-05
HIGH = lax.Precision.HIGHEST

@jax.custom_vjp
def low(v):
    return lax.optimization_barrier(v.astype(jnp.bfloat16)).astype(jnp.float32)

@jax.custom_vjp
def low_back(v):
    return v

def low_keep(v):
    return (low(v), None)

def low_pass(kept, grad):
    return (grad,)

def back_keep(v):
    return (v, None)

def back_low(kept, grad):
    return (low(grad),)
low.defvjp(low_keep, low_pass)
low_back.defvjp(back_keep, back_low)

def layer_norm(resid, gain, shift):
    center = resid - lax.optimization_barrier(jnp.mean(resid, axis=-1, keepdims=True))
    spread = lax.optimization_barrier(jnp.mean(center * center, axis=-1, keepdims=True))
    return center * lax.rsqrt(spread + norm_eps) * gain + shift

def geometry(segment, spans):
    doc_count = spans.shape[0]
    member = segment[:, None] == jnp.arange(doc_count, dtype=jnp.int32)[None, :]
    doc_span = lax.optimization_barrier(jnp.sum(jnp.where(member, spans[None, :], 0), axis=1)).astype(jnp.int32)
    length = segment.shape[0]
    places = jnp.arange(length, dtype=jnp.int32)
    angle = 0.5 * math.pi * places.astype(jnp.float32) / doc_span.astype(jnp.float32)
    causal = places[:, None] >= places[None, :]
    keep_mask = jnp.where((segment[:, None] == segment[None, :]) & causal, 1.0, 0.0).astype(jnp.float32)
    return (jnp.cos(angle), jnp.sin(angle), keep_mask)

def block_forward(inputs, w_qkv, b_qkv, w_out, b_out, ln1_gain, ln1_bias, w_up, b_up, w_down, b_down, ln2_gain, ln2_bias, cosine, sine, keep_mask):
    length = inputs.shape[0]
    proj = low_back(jnp.dot(inputs, w_qkv, precision=HIGH) + b_qkv)
    query = (jax.nn.relu(proj[:, :D]) * 0.125).reshape(length, HEADS, HD)
    keyed = jax.nn.relu(proj[:, D:2 * D]).reshape(length, HEADS, HD)
    valued = proj[:, 2 * D:].reshape(length, HEADS, HD)
    cos_col = cosine[:, None, None]
    sin_col = sine[:, None, None]
    q_feat = low(jnp.concatenate([query * cos_col, query * sin_col], axis=-1))
    k_feat = low(jnp.concatenate([keyed * cos_col, keyed * sin_col], axis=-1))
    v_bf = low(valued)
    scores = jnp.einsum('ihd,jhd->hij', q_feat, k_feat, precision=HIGH) * keep_mask[None]
    scores_kept = low_back(scores)
    denom = jnp.maximum(lax.optimization_barrier(jnp.sum(scores_kept, axis=-1)), 1.0)
    numer = low_back(jnp.einsum('hij,jhd->ihd', low(scores_kept), v_bf, precision=HIGH))
    attn = low((numer / jnp.transpose(denom)[:, :, None]).reshape(length, D))
    branch = low_back(jnp.dot(attn, w_out, precision=HIGH) + b_out)
    hidden = layer_norm(inputs + branch, ln1_gain, ln1_bias)
    upward = low_back(jnp.dot(low(hidden), w_up, precision=HIGH) + b_up)
    action = low(jax.nn.gelu(upward, approximate=False))
    downward = low_back(jnp.dot(action, w_down, precision=HIGH) + b_down)
    return layer_norm(hidden + downward, ln2_gain, ln2_bias)

def reference(layer_input, w_qkv, b_qkv, w_out, b_out, ln1_gain, ln1_bias, w_up, b_up, w_down, b_down, ln2_gain, ln2_bias, segment_ids, doc_lengths, cotangent):
    params = tuple((item.astype(jnp.float32) for item in (w_qkv, b_qkv, w_out, b_out, ln1_gain, ln1_bias, w_up, b_up, w_down, b_down, ln2_gain, ln2_bias)))
    seq_inputs = layer_input.astype(jnp.float32).reshape(NSEQ, LEN, D)
    seq_cots = cotangent.astype(jnp.float32).reshape(NSEQ, LEN, D)
    seq_segments = segment_ids.reshape(NSEQ, LEN)

    def one_sequence(totals, pieces):
        inputs, cots, segment, spans = pieces
        cosine, sine, keep_mask = geometry(segment, spans)

        def forward_fn(values, *weights):
            return block_forward(values, *weights, cosine, sine, keep_mask)
        result, pullback = jax.vjp(forward_fn, inputs, *params)
        grads = pullback(cots)
        totals = tuple((left_part + right_part for left_part, right_part in zip(totals, grads[1:])))
        return (totals, (result, grads[0]))
    start_totals = tuple((jnp.zeros_like(item) for item in params))
    totals, (results, input_grads) = lax.scan(one_sequence, start_totals, (seq_inputs, seq_cots, seq_segments, doc_lengths))
    return (results.reshape(TOKENS, D).astype(jnp.bfloat16), input_grads.reshape(TOKENS, D).astype(jnp.bfloat16), totals[0], totals[1], totals[2], totals[3], totals[4], totals[5], totals[6], totals[7], totals[8], totals[9], totals[10], totals[11])
```

```python
import functools
import math

import jax
import jax.numpy as jnp
from jax import lax
from jax.experimental import pallas as pl
from jax.experimental.pallas import tpu as pltpu
from jax.sharding import PartitionSpec as P

HD = 64
LANE = 128
TILE = 256
GROUPS = 3
MIB = 1 << 20
VMEM_MIB = 58
BLOCK = 768
VECTOR_ROWS = 64
SPLITS = (2, 1)
TURNS = (
    ((0,), (1,)),
    ((0,), (1,), (0,), (1,)),
    ((0,), (1,), (0,), (1,), (0,)),
)

BF = jnp.bfloat16
F32 = jnp.float32
norm_eps = 1e-05


def dot(left, right):
    return lax.dot_general(left, right, (((1,), (0,)), ((), ())), preferred_element_type=F32)


def dot_t(left, right):
    return lax.dot_general(left, right, (((1,), (1,)), ((), ())), preferred_element_type=F32)


def t_dot(left, right):
    return lax.dot_general(left, right, (((0,), (0,)), ((), ())), preferred_element_type=F32)


def low_half(shape):
    return lax.broadcasted_iota(jnp.int32, shape, 1) < HD


def params(limit, grid_dims=0):
    return pltpu.CompilerParams(
        dimension_semantics=("arbitrary",) * grid_dims if grid_dims else None,
        vmem_limit_bytes=limit * MIB,
    )


def cost(*_):
    return pl.CostEstimate(flops=1000, bytes_accessed=1000, transcendentals=0)


def hbm(shape, dtype):
    return pltpu.HBM(shape, dtype)


def vmem(shape, dtype):
    return jax.ShapeDtypeStruct(shape, dtype)


def full(shape):
    return pl.BlockSpec(shape, lambda *_: (0,) * len(shape))


ANY = pl.BlockSpec(memory_space=pl.ANY)


def shift(value, axis, step):
    size = lax.axis_size(axis)
    return lax.ppermute(value, axis, [(i, (i + step) % size) for i in range(size)])


def pair_swap(value, axis):
    size = lax.axis_size(axis)
    return lax.ppermute(value, axis, [(i, i ^ 1) for i in range(size)])


def flip(value, bit):
    size = lax.axis_size("dp")
    return lax.ppermute(value, "dp", [(i, i ^ bit) for i in range(size)])


def gate(value, deps):
    return lax.optimization_barrier((value,) + tuple(deps))[0]


def fetch_near(block):
    return [block, pair_swap(block, "my")]


def fetch_far(block, *deps):
    grid_rows = lax.axis_size("mx")
    block = gate(block, deps) if deps else block
    return [shift(block, "mx", step) for step in range(1, grid_rows)]


def fetch_rest(near, far, *deps):
    if deps:
        far = list(lax.optimization_barrier(tuple(far) + deps)[: len(far)])
    return near + far + [pair_swap(item, "my") for item in far]


def piece_places():
    grid_rows = lax.axis_size("mx")
    row = lax.axis_index("mx")
    col = lax.axis_index("my")
    places = [(row, col), (row, 1 - col)]
    for c in (col, 1 - col):
        for step in range(1, grid_rows):
            places.append(((row - step + grid_rows) % grid_rows, c))
    return jnp.stack([jnp.asarray(item, jnp.int32) for place in places for item in place])


def pack_kernel(*refs):
    out_ref = refs[-1]
    for index, ref in enumerate(refs[:-1]):
        size = ref.shape[0]
        out_ref[index : index + 1, 0:size] = ref[...].astype(F32).reshape(1, size)


def pack_vectors(vectors):
    wide = max(item.shape[0] for item in vectors)
    return pl.pallas_call(
        pack_kernel,
        out_shape=jax.ShapeDtypeStruct((len(vectors), wide), F32),
        compiler_params=params(VMEM_MIB),
        name="pack",
    )(*vectors)


def spread_kernel(sizes, grid_rows, chunk_count, places_ref, *refs):
    owners = grid_rows * 2
    qkv_ref, up_ref, rest_ref = refs[owners : owners + 3]
    scr = refs[owners + 3]
    rest = 0
    for index, size in enumerate(sizes):
        total = size * owners
        whole = jnp.zeros((1, total), F32)
        for owner in range(owners):
            place = places_ref[2 * owner] * 2 + places_ref[2 * owner + 1]
            scr[...] = jnp.zeros_like(scr)
            scr[:, 0:size] = refs[owner][index : index + 1, 0:size]
            whole = whole + pltpu.roll(scr[:, 0:total], place * size, 1)
        if index == 0:
            for unit in range(6 * GROUPS):
                part, pair = unit // (2 * GROUPS), unit % (2 * GROUPS)
                lane = (pair % GROUPS) * 6 * LANE + (2 * part + pair // GROUPS) * LANE
                qkv_ref[:, lane : lane + LANE] = whole[:, unit * LANE : (unit + 1) * LANE]
        elif index == 4:
            piece = total // grid_rows // chunk_count
            for i in range(grid_rows):
                for c in range(chunk_count):
                    src, dst = (i * chunk_count + c) * piece, (c * grid_rows + i) * piece
                    up_ref[:, dst : dst + piece] = whole[:, src : src + piece]
        else:
            rest_ref[rest : rest + 1, :] = whole
            rest += 1
    rest_ref[rest:8, :] = jnp.zeros((8 - rest, rest_ref.shape[1]), F32)


def spread_vectors(places, packs, sizes, chunk_count):
    grid_rows = lax.axis_size("mx")
    owners = grid_rows * 2
    wide = max(sizes) * owners
    return pl.pallas_call(
        functools.partial(spread_kernel, sizes, grid_rows, chunk_count),
        grid_spec=pltpu.PrefetchScalarGridSpec(
            num_scalar_prefetch=1,
            grid=(1,),
            in_specs=[full(item.shape) for item in packs],
            out_specs=[
                full((1, sizes[0] * owners)),
                full((1, sizes[4] * owners)),
                full((8, sizes[1] * owners)),
            ],
            scratch_shapes=[pltpu.VMEM((1, wide), F32)],
        ),
        out_shape=[
            jax.ShapeDtypeStruct((1, sizes[0] * owners), F32),
            jax.ShapeDtypeStruct((1, sizes[4] * owners), F32),
            jax.ShapeDtypeStruct((8, sizes[1] * owners), F32),
        ],
        compiler_params=params(VMEM_MIB, 1),
        name="spread",
    )(places, *packs)


def share_vectors(spot_ref, rows, groups, outs, grid_rows, chunk_count):
    owners = grid_rows * 2
    owner = spot_ref[0] * 2 + spot_ref[1]

    def pair(index):
        return [rows[2 * index : 2 * index + 1, :], rows[2 * index + 1 : 2 * index + 2, :]]

    qkv = []
    for unit in range(6 * GROUPS):
        part, place = unit // (2 * GROUPS), unit % (2 * GROUPS)
        lane = 2 * part + place // GROUPS
        row = groups[place % GROUPS][lane // 3 : lane // 3 + 1, :]
        qkv.append(row[:, (lane % 3) * LANE : (lane % 3 + 1) * LANE])
    wide = rows.shape[1]
    piece = outs[4].shape[0] * owners // grid_rows // chunk_count
    ups = []
    for i in range(grid_rows):
        for c in range(chunk_count):
            for part in range(piece // LANE):
                place = (c * grid_rows + i) * piece + part * LANE
                row, lane = 12 + place // wide, place % wide
                ups.append(rows[row : row + 1, lane : lane + LANE])
    for items, out_ref in zip(
        (qkv, pair(0), pair(1), pair(2), ups, pair(3), pair(4), pair(5)), outs
    ):
        size = out_ref.shape[0]
        total = size * owners
        whole = jnp.concatenate(items, axis=1)
        turned = pltpu.roll(whole, lax.rem(total - owner * size, total), 1)
        out_ref[...] = turned[:, 0:size].reshape(size)


def gates(values, dep):
    return list(lax.optimization_barrier(tuple(values) + (dep,))[:-1])


class Chain:
    def __init__(self, send, keep, plan):
        self.plan = plan
        self.stage = 0
        self.fresh = send
        self.terms = [(keep, 0), (pair_swap(send, "my"), 0)]
        self.rows = send.shape[1]
        self.split = True

    def part(self, first, rows, owner=None):
        result = None
        for array, start in self.terms:
            if array.ndim == 3:
                count = array.shape[0] if owner is None else 1
                at = (0 if owner is None else owner, start + first, 0)
                item = lax.dynamic_slice(array, at, (count, rows, array.shape[2]))
                item = item if owner is None else item[0]
            else:
                item = lax.dynamic_slice(array, (start + first, 0), (rows, array.shape[1]))
            if len(self.terms) > 2:
                item = item.astype(F32)
            result = item if result is None else result + item
        return result.astype(BF)

    def step(self, after=None):
        if self.stage == len(self.plan):
            return False
        kind, bit = self.plan[self.stage]
        self.stage += 1
        array, start = self.terms[-1]
        if after is not None:
            self.terms[-1] = (gate(array, [after]), start)
        owner = None if self.split else 0
        if kind == "mx":
            parts = [self.part(0, self.rows, i) for i in range(1, lax.axis_size("mx"))]
            self.fresh = parts[0]
            self.terms += [(shift(part, "mx", i + 1), 0) for i, part in enumerate(parts)]
            self.split = False
        elif kind == "halve":
            side = lax.axis_index("dp") // bit % 2
            self.rows //= 2
            self.fresh = self.part((1 - side) * self.rows, self.rows, owner)
            self.terms = [(array, start + side * self.rows) for array, start in self.terms]
            self.terms.append((flip(self.fresh, bit), 0))
        else:
            if kind == "join" and self.plan[self.stage - 2][0] == "join":
                self.fresh = jnp.concatenate([array for array, _ in self.terms], axis=0)
            else:
                self.fresh = self.part(0, self.rows, owner)
            self.terms = [(self.fresh, 0), (flip(self.fresh, bit), 0)]
        return True

    def finish(self):
        while self.step():
            pass
        return [array for array, _ in self.terms]


def plan(split):
    bits = []
    while 1 << len(bits) < lax.axis_size("dp"):
        bits.append(1 << len(bits))
    return (
        [("mx", None)]
        + [("halve", bit) for bit in bits[:split]]
        + [("whole", bit) for bit in bits[split:]]
        + [("join", bit) for bit in bits[:split][::-1]]
    )


def deep_sum(value):
    size = lax.axis_size("dp")
    groups = [list(range(start, size, 2)) for start in range(2)]
    return lax.psum(value, "dp", axis_index_groups=groups)


def place_copies(places_ref, refs, sems, put):
    copies = []
    for index, ref in enumerate(refs):
        copies += put(places_ref[2 * index], places_ref[2 * index + 1], ref)
    return [
        pltpu.make_async_copy(src, dst, sems.at[index]) for index, (src, dst) in enumerate(copies)
    ]


def aligned(value, size):
    return pl.multiple_of(value, size)


def attend_kernel(pieces, width, places_ref, *refs):
    x_ref = refs[0]
    w_refs = refs[1 : 1 + pieces]
    bias_ref, cs_ref, segc_ref, segr_ref, qm_ref, km_ref = refs[1 + pieces : 7 + pieces]
    qf_ref, kf_ref, vp_ref, out_a, out_b, rden_ref, wp_ref = refs[7 + pieces : 14 + pieces]
    w_scr, mask_scr, sems, out_sem = refs[14 + pieces :]
    step = pl.program_id(0)
    tokens = x_ref.shape[0]
    model = x_ref.shape[1]
    chunks = tokens // TILE
    units = width // LANE

    def put(row, col, ref):
        rows = ref.shape[0]
        start = row * rows
        start = aligned(start, 16)
        result = []
        for unit in range(units):
            where = col * units + unit
            part = where // (2 * GROUPS)
            pair = where % (2 * GROUPS)
            group = pair % GROUPS
            lane = aligned(part * (2 * LANE) + (pair // GROUPS) * LANE, LANE)
            result.append(
                (
                    ref.at[:, unit * LANE : (unit + 1) * LANE],
                    w_scr.at[group, pl.ds(start, rows), pl.ds(lane, LANE)],
                )
            )
        return result

    out_copy = pltpu.make_async_copy(w_scr, wp_ref, out_sem)

    @pl.when(step == 0)
    def _():
        copies = place_copies(places_ref, w_refs, sems, put)
        for copy in copies:
            copy.start()
        ii = lax.broadcasted_iota(jnp.int32, (TILE, TILE), 0)
        jj = lax.broadcasted_iota(jnp.int32, (TILE, TILE), 1)
        for c in range(chunks):
            rows = slice(c * TILE, (c + 1) * TILE)
            keep = (segc_ref[rows, :] == segr_ref[:, rows]) & (jj <= ii)
            mask_scr[c] = jnp.where(keep, 1.0, 0.0)
        for copy in copies:
            copy.wait()
        out_copy.start()

    low = low_half((TILE, LANE))
    for r in range(chunks):
        rows = slice(r * TILE, (r + 1) * TILE)
        acc = dot(x_ref[rows, :], w_scr[step]) + bias_ref[...]
        cs = cs_ref[rows, :]
        for a in range(2):
            q = jnp.maximum(acc[:, a * LANE : (a + 1) * LANE], 0.0) * 0.125
            k = jnp.maximum(acc[:, (2 + a) * LANE : (3 + a) * LANE], 0.0)
            v = acc[:, (4 + a) * LANE : (5 + a) * LANE]
            q_r = pltpu.roll(q, HD, 1)
            k_r = pltpu.roll(k, HD, 1)
            first = slice(2 * a * LANE, (2 * a + 1) * LANE)
            second = slice((2 * a + 1) * LANE, (2 * a + 2) * LANE)
            qf_ref[rows, first] = (jnp.where(low, q, q_r) * cs).astype(BF)
            qf_ref[rows, second] = (jnp.where(low, q_r, q) * cs).astype(BF)
            kf_ref[rows, first] = (jnp.where(low, k, k_r) * cs).astype(BF)
            kf_ref[rows, second] = (jnp.where(low, k_r, k) * cs).astype(BF)
            vp_ref[rows, first] = jnp.where(low, v, 1.0).astype(BF)
            vp_ref[rows, second] = jnp.where(low, 1.0, v).astype(BF)

    states = [None] * 4
    for c in range(chunks):
        rows = slice(c * TILE, (c + 1) * TILE)
        mask = mask_scr[c]
        qm = qm_ref[rows, :]
        km = km_ref[rows, :]
        for a in range(2):
            outs = []
            for h in (2 * a, 2 * a + 1):
                cols = slice(h * LANE, (h + 1) * LANE)
                q = qf_ref[rows, cols]
                k = kf_ref[rows, cols]
                v = vp_ref[rows, cols]
                scores = (dot_t(q, k) * mask).astype(BF)
                out = dot(scores, v)
                if c > 0:
                    out = out + qm * dot(q, states[h].astype(BF))
                outs.append(out)
                if c < chunks - 1:
                    grown = t_dot(k * km.astype(BF), v)
                    if c > 0:
                        grown = grown + states[h] * qm[TILE - 1 : TILE, :]
                    states[h] = grown
            numer = jnp.where(low, outs[0], outs[1])
            denom = pltpu.roll(jnp.where(low, outs[1], outs[0]), HD, 1)
            rden = 1.0 / jnp.maximum(denom, 1.0)
            rden_ref[rows, a * LANE : (a + 1) * LANE] = rden
            (out_a, out_b)[a][rows, :] = (numer * rden).astype(BF)

    @pl.when(step == GROUPS - 1)
    def _():
        out_copy.wait()


def attend(places, x, pieces, bias, cs, segc, segr, qm, km):
    tokens, model = x.shape
    count = len(pieces)
    width = 3 * model // 2
    group = 6 * LANE
    spec = pl.BlockSpec((tokens, 4 * LANE), lambda g, p: (0, g))
    half = pl.BlockSpec((tokens, LANE), lambda g, p: (0, g))
    return pl.pallas_call(
        functools.partial(attend_kernel, count, width),
        grid_spec=pltpu.PrefetchScalarGridSpec(
            num_scalar_prefetch=1,
            grid=(GROUPS,),
            in_specs=[full((tokens, model))]
            + [ANY] * count
            + [
                pl.BlockSpec((1, group), lambda g, p: (0, g)),
                full((tokens, LANE)),
                full((tokens, 1)),
                full((1, tokens)),
                full((tokens, LANE)),
                full((tokens, LANE)),
            ],
            out_specs=[
                spec,
                spec,
                spec,
                half,
                half,
                pl.BlockSpec((tokens, 2 * LANE), lambda g, p: (0, g)),
                ANY,
            ],
            scratch_shapes=[
                pltpu.VMEM((GROUPS, model, group), BF),
                pltpu.VMEM((tokens // TILE, TILE, TILE), F32),
                pltpu.SemaphoreType.DMA((count * (width // LANE),)),
                pltpu.SemaphoreType.DMA,
            ],
        ),
        out_shape=[hbm((tokens, GROUPS * 4 * LANE), BF)] * 3
        + [jax.ShapeDtypeStruct((tokens, GROUPS * LANE), BF)] * 2
        + [
            hbm((tokens, model), F32),
            hbm((GROUPS, model, group), BF),
        ],
        compiler_params=params(VMEM_MIB, 1),
        cost_estimate=cost(2 * tokens * model * 3 * model * 1.8, 20 * MIB),
        name="attend",
    )(places, x, *pieces, bias, cs, segc, segr, qm, km)


def rows_put(target, first):
    def put(row, col, ref):
        rows = ref.shape[0]
        width = ref.shape[1] - first
        start = row * rows
        return [
            (
                ref.at[:, first : first + width],
                target.at[pl.ds(aligned(start, 16), rows), pl.ds(aligned(col * width, LANE), width)],
            )
        ]

    return put


def join_kernel(pieces, places_ref, *refs):
    a_ref, b_ref, x_ref = refs[:3]
    w_refs = refs[3 : 3 + pieces]
    rest_ref = refs[3 + pieces]
    xhat_ref, rstd_ref, hb_ref, ht_ref, at_ref, wo_ref = refs[4 + pieces : 10 + pieces]
    w_scr, sems, out_sem = refs[10 + pieces :]
    step = pl.program_id(0)
    out_copy = pltpu.make_async_copy(w_scr, wo_ref, out_sem)

    @pl.when(step == 0)
    def _():
        copies = place_copies(places_ref, w_refs, sems, rows_put(w_scr, 3 * w_scr.shape[1] // 2))
        for copy in copies:
            copy.start()
        for copy in copies:
            copy.wait()
        out_copy.start()

    attn = jnp.concatenate([a_ref[...], b_ref[...]], axis=1)
    resid = x_ref[...].astype(F32) + dot(attn, w_scr[...]) + rest_ref[0:1, :]
    center = resid - jnp.mean(resid, axis=1, keepdims=True)
    rstd = lax.rsqrt(jnp.mean(center * center, axis=1, keepdims=True) + norm_eps)
    xhat = center * rstd
    hidden = xhat * rest_ref[1:2, :] + rest_ref[2:3, :]
    xhat_ref[...] = xhat
    rstd_ref[...] = jnp.broadcast_to(rstd, rstd_ref.shape)
    hb_ref[...] = hidden.astype(BF)
    ht_ref[...] = hidden.T.astype(BF)
    at_ref[...] = attn.astype(F32).T.astype(BF)

    @pl.when(step == pl.num_programs(0) - 1)
    def _():
        out_copy.wait()


def join(places, attn_a, attn_b, x, pieces, rest):
    tokens, model = x.shape
    count = len(pieces)
    row = pl.BlockSpec((TILE, model), lambda r, p: (r, 0))
    half = pl.BlockSpec((TILE, model // 2), lambda r, p: (r, 0))
    flip = pl.BlockSpec((model, TILE), lambda r, p: (0, r))
    return pl.pallas_call(
        functools.partial(join_kernel, count),
        grid_spec=pltpu.PrefetchScalarGridSpec(
            num_scalar_prefetch=1,
            grid=(tokens // TILE,),
            in_specs=[half, half, row] + [ANY] * count + [full((8, model))],
            out_specs=[row, pl.BlockSpec((TILE, LANE), lambda r, p: (r, 0)), row, flip, flip, ANY],
            scratch_shapes=[
                pltpu.VMEM((model, model), BF),
                pltpu.SemaphoreType.DMA((count,)),
                pltpu.SemaphoreType.DMA,
            ],
        ),
        out_shape=[
            hbm((tokens, model), F32),
            hbm((tokens, LANE), F32),
            vmem((tokens, model), BF),
            hbm((model, tokens), BF),
            hbm((model, tokens), BF),
            hbm((model, model), BF),
        ],
        compiler_params=params(VMEM_MIB, 1),
        cost_estimate=cost(2 * tokens * model * model, 14 * MIB),
        name="join",
    )(places, attn_a, attn_b, x, *pieces, rest)


def up_kernel(pieces, chunk_count, places_ref, *refs):
    h_ref = refs[0]
    w_refs = refs[1 : 1 + pieces]
    bias_ref = refs[1 + pieces]
    act_ref, slope_ref, wp_ref = refs[2 + pieces : 5 + pieces]
    w_scr, sems, out_sem = refs[5 + pieces :]
    step = pl.program_id(0)
    wide = w_scr.shape[2]
    out_copy = pltpu.make_async_copy(w_scr, wp_ref, out_sem)

    @pl.when(step == 0)
    def _():
        width = w_refs[0].shape[1]
        piece = wide // lax.axis_size("mx")
        blocks = width // (piece * chunk_count)

        def put(row, col, ref):
            rows = ref.shape[0]
            start = row * rows
            result = []
            for i in range(blocks):
                for c in range(chunk_count):
                    lane = aligned((col * blocks + i) * piece, LANE)
                    src = (i * chunk_count + c) * piece
                    result.append(
                        (
                            ref.at[:, src : src + piece],
                            w_scr.at[c, pl.ds(aligned(start, 16), rows), pl.ds(lane, piece)],
                        )
                    )
            return result

        copies = place_copies(places_ref, w_refs, sems, put)
        for copy in copies:
            copy.start()
        for copy in copies:
            copy.wait()
        out_copy.start()

    tokens = h_ref.shape[0]
    for r in range(tokens // TILE):
        rows = slice(r * TILE, (r + 1) * TILE)
        up = dot(h_ref[rows, :], w_scr[step]) + bias_ref[...]
        phi = lax.erf(up * math.sqrt(0.5)) * 0.5 + 0.5
        bell = jnp.exp(up * up * -0.5) * (1.0 / math.sqrt(2.0 * math.pi))
        act_ref[rows, :] = (up * phi).astype(BF)
        slope_ref[rows, :] = (phi + up * bell).astype(BF)

    @pl.when(step == pl.num_programs(0) - 1)
    def _():
        out_copy.wait()


def up_project(places, hidden, pieces, bias, chunk_count):
    tokens, model = hidden.shape
    count = len(pieces)
    hidden_units = pieces[0].shape[1] * 2
    wide = hidden_units // chunk_count
    piece = wide // lax.axis_size("mx")
    per = pieces[0].shape[1] // piece
    col = pl.BlockSpec((tokens, wide), lambda c, p: (0, c))
    return pl.pallas_call(
        functools.partial(up_kernel, count, chunk_count),
        grid_spec=pltpu.PrefetchScalarGridSpec(
            num_scalar_prefetch=1,
            grid=(chunk_count,),
            in_specs=[full((tokens, model))]
            + [ANY] * count
            + [pl.BlockSpec((1, wide), lambda c, p: (0, c))],
            out_specs=[col, col, ANY],
            scratch_shapes=[
                pltpu.VMEM((chunk_count, model, wide), BF),
                pltpu.SemaphoreType.DMA((count * per,)),
                pltpu.SemaphoreType.DMA,
            ],
        ),
        out_shape=[hbm((tokens, hidden_units), BF)] * 2 + [hbm((chunk_count, model, wide), BF)],
        compiler_params=params(VMEM_MIB, 1),
        cost_estimate=cost(
            2 * tokens * model * hidden_units, 24 * MIB, 2 * tokens * hidden_units
        ),
        name="up",
    )(places, hidden, *pieces, bias)


def once(shape):
    return pl.BlockSpec(shape, lambda *_: (0,) * len(shape), pipeline_mode=pl.Buffered(1))


def ffn_kernel(pieces, chunk_count, grid_rows, piece, tiles, places_ref, spot_ref, *refs):
    rowa_ref, xhat_ref, cot_ref = refs[:3]
    w_refs = refs[3 : 3 + pieces]
    rest_ref, ht_hbm, act_ref, slope_ref, wu_ref = refs[3 + pieces : 8 + pieces]
    outs = refs[8 + pieces :]
    out_ref, sums_ref, dh_ref, bsum_ref = outs[:4]
    keeps = outs[4 : 4 + chunk_count]
    sends = outs[4 + chunk_count : 4 + 2 * chunk_count]
    w_scr, dup_scr, dd_ref, ddt_ref, ht_ref, sems, ht_sem = outs[4 + 2 * chunk_count :]
    row, col = spot_ref[0], spot_ref[1]
    step = pl.program_id(0)
    wide = w_scr.shape[0] // chunk_count
    tokens, block = act_ref.shape
    model = dh_ref.shape[1]
    half, share = model // 2, model // grid_rows
    per = grid_rows // 2
    ht_copy = pltpu.make_async_copy(ht_hbm, ht_ref, ht_sem)

    @pl.when(step == 0)
    def _():
        def put(row, col, ref):
            width = ref.shape[1]
            lane = pl.ds(aligned(col * width, LANE), width)
            return [
                (
                    ref.at[c * piece : (c + 1) * piece, :],
                    w_scr.at[pl.ds(aligned(c * wide + row * piece, 16), piece), lane],
                )
                for c in range(chunk_count)
            ]

        copies = place_copies(places_ref, w_refs, sems, put)
        for copy in copies:
            copy.start()
        ht_copy.start()
        sums_ref[...] = jnp.zeros_like(sums_ref)
        for copy in copies:
            copy.wait()

    @pl.when(step < tiles)
    def _():
        rows = pl.ds(aligned(step * TILE, TILE), TILE)
        hidden = xhat_ref[...] * rest_ref[1:2, :] + rest_ref[2:3, :]
        resid = hidden + dot(rowa_ref[...], w_scr[...]) + rest_ref[3:4, :]
        center = resid - jnp.mean(resid, axis=1, keepdims=True)
        rstd = lax.rsqrt(jnp.mean(center * center, axis=1, keepdims=True) + norm_eps)
        xhat = center * rstd
        out_ref[...] = (xhat * rest_ref[4:5, :] + rest_ref[5:6, :]).astype(BF)
        g = cot_ref[...].astype(F32)
        e = g * rest_ref[4:5, :]
        d_res = rstd * (
            e
            - jnp.mean(e, axis=1, keepdims=True)
            - xhat * jnp.mean(e * xhat, axis=1, keepdims=True)
        )
        dh_ref[rows, :] = d_res
        d_down = d_res.astype(BF)
        dd_ref[rows, :] = d_down
        ddt_ref[:, rows] = d_down.T
        sums_ref[0:1, :] += jnp.sum(g * xhat, axis=0, keepdims=True)
        sums_ref[1:2, :] += jnp.sum(g, axis=0, keepdims=True)
        sums_ref[2:3, :] += jnp.sum(d_down.astype(F32), axis=0, keepdims=True)

    @pl.when(step == tiles)
    def _():
        ht_copy.wait()

    @pl.when(step >= tiles)
    def _():
        turn = step - tiles
        blocks = piece // block
        owner = lax.rem(turn // blocks, grid_rows)
        chunk = turn // (blocks * grid_rows)
        lane = pl.ds(aligned(lax.rem(turn, blocks) * block, LANE), block)
        wd = w_scr.at[pl.ds(aligned(turn * block, 16), block), :]
        total = jnp.zeros((1, block), F32)
        for r in range(tokens // TILE):
            rows = slice(r * TILE, (r + 1) * TILE)
            grad = (dot_t(dd_ref[rows, :], wd[...]) * slope_ref[rows, :].astype(F32)).astype(BF)
            dup_scr[rows, :] = grad
            total = total + jnp.sum(grad.astype(F32), axis=0, keepdims=True)
        bsum_ref[...] = jnp.broadcast_to(total, bsum_ref.shape)
        for r in range(tokens // TILE):
            rows = slice(r * TILE, (r + 1) * TILE)
            dh_ref[rows, :] += dot_t(dup_scr[rows, :], wu_ref[...])
        slot = lax.rem(owner - row + grid_rows, grid_rows)
        place = aligned(half + lax.rem(owner, per) * share, 16)
        down = dot(ddt_ref[pl.ds(aligned(col * half, 16), half), :], act_ref[...]).astype(BF)
        down_far = dot(
            ddt_ref[pl.ds(aligned((1 - col) * half, 16), half), :], act_ref[...]
        ).astype(BF)
        up = dot(ht_ref[...], dup_scr[...]).astype(BF)
        for c in range(chunk_count):

            @pl.when(chunk == c)
            def _():
                keeps[c][slot, 0:half, lane] = down
                sends[c][slot, 0:half, lane] = down_far
                for mine, target in ((True, keeps[c]), (False, sends[c])):

                    @pl.when((owner // per == col) == mine)
                    def _():
                        for i in range(grid_rows):
                            where = lax.rem(i - row + grid_rows, grid_rows)
                            target[where, pl.ds(place, share), lane] = up[
                                i * share : (i + 1) * share, :
                            ]


def ffn(places, spot, act, slope, xhat, cot, pieces, rest, hidden_t, w_up, chunk_count):
    tokens, hidden_units = act.shape
    model = xhat.shape[1]
    count = len(pieces)
    grid_rows = lax.axis_size("mx")
    wide = hidden_units // chunk_count
    piece = wide // grid_rows
    block = min(piece, BLOCK)
    message = (grid_rows, model, piece)
    tiles = tokens // TILE
    inner = wide // block

    def row(width):
        return pl.BlockSpec((TILE, width), lambda s, *_: (jnp.minimum(s, tiles - 1), 0))

    def late(s):
        return jnp.maximum(s - tiles, 0)

    pick = pl.BlockSpec((tokens, block), lambda s, *_: (0, late(s)))
    return pl.pallas_call(
        functools.partial(ffn_kernel, count, chunk_count, grid_rows, piece, tiles),
        grid_spec=pltpu.PrefetchScalarGridSpec(
            num_scalar_prefetch=2,
            grid=(tiles + hidden_units // block,),
            in_specs=[row(hidden_units), row(model), row(model)]
            + [ANY] * count
            + [
                once((8, model)),
                ANY,
                pick,
                pick,
                pl.BlockSpec(
                    (None, model, block), lambda s, *_: (late(s) // inner, 0, late(s) % inner)
                ),
            ],
            out_specs=[
                row(model),
                once((8, model)),
                once((tokens, model)),
                pl.BlockSpec((8, block), lambda s, *_: (0, late(s))),
            ]
            + [once(message)] * (2 * chunk_count),
            scratch_shapes=[
                pltpu.VMEM((hidden_units, model), BF),
                pltpu.VMEM((tokens, block), BF),
                pltpu.VMEM((tokens, model), BF),
                pltpu.VMEM((model, tokens), BF),
                pltpu.VMEM((model, tokens), BF),
                pltpu.SemaphoreType.DMA((count * chunk_count,)),
                pltpu.SemaphoreType.DMA,
            ],
        ),
        out_shape=[
            hbm((tokens, model), BF),
            vmem((8, model), F32),
            hbm((tokens, model), F32),
            vmem((8, hidden_units), F32),
        ]
        + [hbm(message, BF)] * (2 * chunk_count),
        compiler_params=params(VMEM_MIB, 1),
        cost_estimate=cost(),
        name="ffn",
    )(places, spot, act, xhat, cot, *pieces, rest, hidden_t, act, slope, w_up)


def norm_kernel(grid_rows, spot_ref, *refs):
    (
        dres_ref,
        xhat_ref,
        rstd_ref,
        a_ref,
        b_ref,
        rden_ref,
        wo_ref,
        gain_ref,
        at_ref,
        two_ref,
        up_ref,
    ) = refs[:11]
    dn_ref, dr_ref, keep_ref, send_ref, sums_ref, db_scr, msg_scr, ext_scr, sems = refs[11:]
    step = pl.program_id(0)
    model = dres_ref.shape[1]

    @pl.when(step == 0)
    def _():
        sums_ref[...] = jnp.zeros_like(sums_ref)

    d_hidden = dres_ref[...]
    xhat = xhat_ref[...]
    e = d_hidden * gain_ref[1:2, :]
    d_res = rstd_ref[:, 0:1] * (
        e
        - jnp.mean(e, axis=1, keepdims=True)
        - xhat * jnp.mean(e * xhat, axis=1, keepdims=True)
    )
    dr_ref[...] = d_res
    d_branch = d_res.astype(BF)
    db_scr[pl.ds(aligned(step * TILE, TILE), TILE), :] = d_branch
    sums_ref[0:1, :] += jnp.sum(d_hidden * xhat, axis=0, keepdims=True)
    sums_ref[1:2, :] += jnp.sum(d_hidden, axis=0, keepdims=True)
    sums_ref[2:3, :] += jnp.sum(d_branch.astype(F32), axis=0, keepdims=True)
    d_attn = dot_t(d_branch, wo_ref[...])
    low = low_half((TILE, LANE))
    li = lax.broadcasted_iota(jnp.int32, (LANE, LANE), 0) < HD
    lj = lax.broadcasted_iota(jnp.int32, (LANE, LANE), 1) < HD
    swap = jnp.where(li == lj, 0.0, 1.0 / HD).astype(BF)
    for pair in range(2 * GROUPS):
        a, g = pair // GROUPS, pair % GROUPS
        d_pair = d_attn[:, pair * LANE : (pair + 1) * LANE]
        attn = (a_ref, b_ref)[a][:, g * LANE : (g + 1) * LANE].astype(F32)
        rden = rden_ref[:, (2 * g + a) * LANE : (2 * g + a + 1) * LANE]
        prod = d_pair * attn
        high = prod.astype(BF)
        rest = (prod - high.astype(F32)).astype(BF)
        other = dot(high, swap) + dot(rest, swap)
        turned = pltpu.roll(rden, HD, 1)
        d_denom = jnp.where(turned < 1.0, -other * turned, 0.0)
        d_numer = d_pair * rden
        place = (4 * g + 2 * a) * LANE
        dn_ref[:, place : place + LANE] = jnp.where(low, d_numer, d_denom).astype(BF)
        dn_ref[:, place + LANE : place + 2 * LANE] = jnp.where(low, d_denom, d_numer).astype(BF)

    @pl.when(step == pl.num_programs(0) - 1)
    def _():
        row, col = spot_ref[0], spot_ref[1]
        half = model // 2
        share = model // grid_rows
        wide = ext_scr.shape[1]
        ext_scr[...] = jnp.zeros_like(ext_scr)
        for index, (ref, line) in enumerate(
            ((sums_ref, 2), (sums_ref, 0), (sums_ref, 1), (two_ref, 2), (two_ref, 0), (two_ref, 1))
        ):
            for part in range(2):
                ext_scr[2 * index + part : 2 * index + part + 1, :] = ref[
                    line : line + 1, part * wide : (part + 1) * wide
                ].astype(BF)
        for part in range(up_ref.shape[1] // wide):
            ext_scr[12 + part : 13 + part, :] = up_ref[
                0:1, part * wide : (part + 1) * wide
            ].astype(BF)
        message_out(
            row, col, grid_rows, at_ref, db_scr, msg_scr, ext_scr, keep_ref, send_ref, 0, 3, 0, sems
        )


def message_out(
    row, col, grid_rows, left_ref, right_ref, msg_scr, ext_scr, keep_ref, send_ref, place, parts,
    line, sems,
):
    share, half = msg_scr.shape[2:]
    count = ext_scr.shape[0]
    copies = []
    for index, (side, target) in enumerate(((1 - col, send_ref), (col, keep_ref))):
        right = right_ref[:, pl.ds(aligned(side * half, LANE), half)]
        grad = dot(left_ref[...], right).astype(BF)
        for i in range(grid_rows):
            slot = lax.rem(i - row + grid_rows, grid_rows)
            msg_scr[index, slot] = grad[i * share : (i + 1) * share, :]
        pairs = [(msg_scr.at[index], target.at[:, pl.ds(aligned(place * share, 8), share), :])]
        lines = pl.ds(aligned(parts * share + line, 8), count)
        pairs += [(ext_scr, target.at[i, lines, :]) for i in range(grid_rows)]
        for src, dst in pairs:
            copy = pltpu.make_async_copy(src, dst, sems.at[len(copies)])
            copy.start()
            copies.append(copy)
    for copy in copies:
        copy.wait()


def norm_back(
    spot, d_hid, xhat, rstd, attn_a, attn_b, rden, w_out, rest, attn_t, sums_two, up_sums
):
    tokens, model = d_hid.shape
    grid_rows = lax.axis_size("mx")
    row = pl.BlockSpec((TILE, model), lambda r, p: (r, 0))
    half = pl.BlockSpec((TILE, model // 2), lambda r, p: (r, 0))
    share = model // grid_rows
    message = (grid_rows, 3 * share + VECTOR_ROWS, model // 2)
    return pl.pallas_call(
        functools.partial(norm_kernel, grid_rows),
        grid_spec=pltpu.PrefetchScalarGridSpec(
            num_scalar_prefetch=1,
            grid=(tokens // TILE,),
            in_specs=[
                row,
                row,
                pl.BlockSpec((TILE, LANE), lambda r, p: (r, 0)),
                half,
                half,
                row,
                once((model, model)),
                once((8, model)),
                once((model, tokens)),
                once(sums_two.shape),
                once(up_sums.shape),
            ],
            out_specs=[pl.BlockSpec((TILE, 2 * model), lambda r, p: (r, 0)), row, ANY, ANY],
            scratch_shapes=[
                pltpu.VMEM((8, model), F32),
                pltpu.VMEM((tokens, model), BF),
                pltpu.VMEM((2, grid_rows, share, model // 2), BF),
                pltpu.VMEM((VECTOR_ROWS, model // 2), BF),
                pltpu.SemaphoreType.DMA((2 * (grid_rows + 1),)),
            ],
        ),
        out_shape=[
            hbm((tokens, 2 * model), BF),
            hbm((tokens, model), F32),
            hbm(message, BF),
            hbm(message, BF),
        ],
        compiler_params=params(VMEM_MIB, 1),
        cost_estimate=cost(),
        name="norm_back",
    )(spot, d_hid, xhat, rstd, attn_a, attn_b, rden, w_out, rest, attn_t, sums_two, up_sums)


def group_kernel(grid_rows, shared, spot_ref, *refs):
    place, parts, line = shared
    place = place + pl.program_id(0)
    line = line + 8 * pl.program_id(0)
    (
        qf_ref,
        kf_ref,
        vp_ref,
        dn_ref,
        cs_ref,
        segc_ref,
        segr_ref,
        qm_ref,
        km_ref,
        xt_ref,
    ) = refs[:10]
    dp_ref, keep_ref, send_ref, msg_scr, ext_scr, sems = refs[-6:]
    tokens = qf_ref.shape[0]
    model = xt_ref.shape[0]
    chunks = tokens // TILE
    low = low_half((TILE, LANE))
    ii = lax.broadcasted_iota(jnp.int32, (TILE, TILE), 0)
    jj = lax.broadcasted_iota(jnp.int32, (TILE, TILE), 1)
    kept = [[None] * 4 for _ in range(chunks)]
    for h in range(4):
        cols = slice(h * LANE, (h + 1) * LANE)
        state = None
        for c in range(chunks - 1):
            rows = slice(c * TILE, (c + 1) * TILE)
            grown = t_dot(kf_ref[rows, cols] * km_ref[rows, :].astype(BF), vp_ref[rows, cols])
            if c > 0:
                grown = grown + state * qm_ref[(c + 1) * TILE - 1 : (c + 1) * TILE, :]
            state = grown
            kept[c + 1][h] = state.astype(BF)
    back = [None] * 4
    sums = [jnp.zeros((1, LANE), F32) for _ in range(6)]
    for c in range(chunks - 1, -1, -1):
        rows = slice(c * TILE, (c + 1) * TILE)
        same = segc_ref[rows, :] == segr_ref[:, rows]
        lower = jnp.where(same & (jj <= ii), 1.0, 0.0)
        upper = jnp.where(same & (jj >= ii), 1.0, 0.0)
        qm = qm_ref[rows, :]
        km = km_ref[rows, :]
        cs = cs_ref[rows, :]
        for a in range(2):
            dqs, dks, dvs, q_on, k_on = [], [], [], [], []
            for h in (2 * a, 2 * a + 1):
                cols = slice(h * LANE, (h + 1) * LANE)
                q = qf_ref[rows, cols]
                k = kf_ref[rows, cols]
                v = vp_ref[rows, cols]
                g = dn_ref[rows, cols]
                d_scores = (dot_t(g, v) * lower).astype(BF)
                d_scores_t = (dot_t(v, g) * upper).astype(BF)
                scores_t = (dot_t(k, q) * upper).astype(BF)
                dq = dot(d_scores, k)
                dk = dot(d_scores_t, q)
                dv = dot(scores_t, g)
                if c > 0:
                    dq = dq + qm * dot_t(g, kept[c][h])
                if c < chunks - 1:
                    held = back[h].astype(BF)
                    dk = dk + km * dot_t(v, held)
                    dv = dv + km * dot(k, held)
                if c > 0:
                    grown = t_dot(q * qm.astype(BF), g)
                    if c < chunks - 1:
                        grown = grown + back[h] * km[0:1, :]
                    back[h] = grown
                dq = dq * cs
                dk = dk * cs
                dqs.append(dq + pltpu.roll(dq, HD, 1))
                dks.append(dk + pltpu.roll(dk, HD, 1))
                dvs.append(dv)
                q_abs = jnp.abs(q.astype(F32))
                k_abs = jnp.abs(k.astype(F32))
                q_on.append(q_abs + pltpu.roll(q_abs, HD, 1))
                k_on.append(k_abs + pltpu.roll(k_abs, HD, 1))
            dq = jnp.where(low, dqs[0], dqs[1]) * 0.125
            dk = jnp.where(low, dks[0], dks[1])
            dq = jnp.where(jnp.where(low, q_on[0], q_on[1]) > 0.0, dq, 0.0).astype(BF)
            dk = jnp.where(jnp.where(low, k_on[0], k_on[1]) > 0.0, dk, 0.0).astype(BF)
            dv = jnp.where(low, dvs[0], dvs[1]).astype(BF)
            for part, item in enumerate((dq, dk, dv)):
                unit = 2 * part + a
                dp_ref[rows, unit * LANE : (unit + 1) * LANE] = item
                sums[unit] = sums[unit] + jnp.sum(item.astype(F32), axis=0, keepdims=True)
    ext_scr[...] = jnp.zeros_like(ext_scr)
    for unit in range(6):
        lane = (unit % 3) * LANE
        ext_scr[unit // 3 : unit // 3 + 1, lane : lane + LANE] = sums[unit].astype(BF)
    message_out(
        spot_ref[0], spot_ref[1], grid_rows, xt_ref, dp_ref, msg_scr, ext_scr, keep_ref, send_ref,
        place, parts, line, sems,
    )


def group_back(spot, qf, kf, vp, dn, cs, segc, segr, qm, km, x_t, first, count, messages):
    model, tokens = x_t.shape
    grid_rows = lax.axis_size("mx")
    pick = pl.BlockSpec((tokens, 4 * LANE), lambda s, p: (0, first + s))
    lane = once((tokens, LANE))
    share = model // grid_rows
    if messages:
        shared = (1 + first, 3, 24 + 8 * first)
        shape = messages[0].shape
    else:
        shared = (0, 1, 0)
        shape = (grid_rows, share + 16, 3 * LANE)
    lines = 8 if messages else 16
    return pl.pallas_call(
        functools.partial(group_kernel, grid_rows, shared),
        grid_spec=pltpu.PrefetchScalarGridSpec(
            num_scalar_prefetch=1,
            grid=(count,),
            in_specs=[
                pick,
                pick,
                pick,
                pick,
                lane,
                once((tokens, 1)),
                once((1, tokens)),
                lane,
                lane,
                once((model, tokens)),
            ]
            + [ANY] * len(messages),
            out_specs=[
                pl.BlockSpec((None, tokens, 6 * LANE), lambda s, p: (s, 0, 0)),
                ANY,
                ANY,
            ],
            scratch_shapes=[
                pltpu.VMEM((2, grid_rows, share, 3 * LANE), BF),
                pltpu.VMEM((lines, 3 * LANE), BF),
                pltpu.SemaphoreType.DMA((2 * (grid_rows + 1),)),
            ],
        ),
        out_shape=[hbm((count, tokens, 6 * LANE), BF), hbm(shape, BF), hbm(shape, BF)],
        input_output_aliases={11: 1, 12: 2} if messages else {},
        compiler_params=params(VMEM_MIB, 1),
        cost_estimate=cost(),
        name="group%d" % first,
    )(spot, qf, kf, vp, dn, cs, segc, segr, qm, km, x_t, *messages)


def input_kernel(early_ref, late_ref, w_ref, dr_ref, out_ref):
    total = dr_ref[...]
    early = early_ref.shape[0]
    for g in range(GROUPS):
        grad = early_ref[g] if g < early else late_ref[g - early]
        total = total + dot_t(grad, w_ref[g])
    out_ref[...] = total.astype(BF)


def input_back(early, late, w_qkv, d_res):
    tokens, model = d_res.shape
    row = pl.BlockSpec((TILE, model), lambda r: (r, 0))
    return pl.pallas_call(
        input_kernel,
        grid=(tokens // TILE,),
        in_specs=[
            pl.BlockSpec((item.shape[0], TILE, 6 * LANE), lambda r: (0, r, 0))
            for item in (early, late)
        ]
        + [once(w_qkv.shape), row],
        out_specs=row,
        out_shape=hbm((tokens, model), BF),
        compiler_params=params(VMEM_MIB, 1),
        cost_estimate=cost(),
        name="input_back",
    )(early, late, w_qkv, d_res)


def settle(spot_ref, mine_ref, other_ref, target, split):
    side = spot_ref[2]
    rows = mine_ref.shape[0]
    for half, ref in ((side, mine_ref), (1 - side, other_ref)):
        if split == 1:
            target[pl.ds(aligned(half * rows, 8), rows), :] = ref[...].astype(F32)
        else:
            deep = lax.rem(spot_ref[3], 2)
            block = rows // 2
            for quarter, first in ((deep, 0), (1 - deep, block)):
                start = aligned(half * rows + quarter * block, 8)
                target[pl.ds(start, block), :] = ref[first : first + block, :].astype(F32)


def ffn_final_kernel(chunk_count, grid_rows, spot_ref, mine_ref, other_ref, up_ref, down_ref, scr):
    piece = mine_ref.shape[1]
    rows = mine_ref.shape[0] // chunk_count
    per = grid_rows // 2
    half = scr.shape[0] // 2
    share = half // per
    for c in range(chunk_count):
        part = pl.ds(c * rows, rows)
        settle(spot_ref, mine_ref.at[part, :], other_ref.at[part, :], scr, 1)
        down_ref[c * piece : (c + 1) * piece, :] = scr[0:half, :].T
        for n in range(per):
            lane = (n * chunk_count + c) * piece
            up_ref[:, lane : lane + piece] = scr[half + n * share : half + (n + 1) * share, :]


def ffn_final(spot, mine, other, chunk_count):
    grid_rows = lax.axis_size("mx")
    rows, piece = mine.shape
    rows = 2 * rows // chunk_count
    share = rows // 2 // (grid_rows // 2)
    up_shape = (share, piece * chunk_count * (grid_rows // 2))
    down_shape = (piece * chunk_count, rows // 2)
    return pl.pallas_call(
        functools.partial(ffn_final_kernel, chunk_count, grid_rows),
        grid_spec=pltpu.PrefetchScalarGridSpec(
            num_scalar_prefetch=1,
            grid=(1,),
            in_specs=[full(mine.shape), full(other.shape)],
            out_specs=[full(up_shape), full(down_shape)],
            scratch_shapes=[pltpu.VMEM((rows, piece), F32)],
        ),
        out_shape=[hbm(up_shape, F32), hbm(down_shape, F32)],
        compiler_params=params(VMEM_MIB, 1),
        cost_estimate=cost(),
        name="ffn_final",
    )(spot, mine, other)


def attn_final_kernel(grid_rows, chunk_count, spot_ref, *refs):
    halves = refs[:4]
    out_ref, qkv_ref = refs[4:6]
    one_scr, two_scr = refs[-2:]
    share = out_ref.shape[0]
    settle(spot_ref, halves[0], halves[1], one_scr, SPLITS[0])
    settle(spot_ref, halves[2], halves[3], two_scr, SPLITS[1])
    out_ref[...] = one_scr[0:share, :]
    groups = []
    for g in range(GROUPS):
        last = g == GROUPS - 1
        scr, start = (two_scr, 0) if last else (one_scr, (1 + g) * share)
        for t in range(3):
            lane = (3 * t + g) * LANE
            qkv_ref[:, lane : lane + LANE] = scr[start : start + share, t * LANE : (t + 1) * LANE]
        line = share if last else 3 * share + 24 + 8 * g
        groups.append(scr[line : line + 8, :])
    rows = one_scr[3 * share : 3 * share + 24, :]
    share_vectors(spot_ref, rows, groups, refs[6:-2], grid_rows, chunk_count)


def attn_final(spot, halves, sizes, model, chunk_count):
    grid_rows = lax.axis_size("mx")
    share, wide = model // grid_rows, model // 2
    return pl.pallas_call(
        functools.partial(attn_final_kernel, grid_rows, chunk_count),
        grid_spec=pltpu.PrefetchScalarGridSpec(
            num_scalar_prefetch=1,
            grid=(1,),
            in_specs=[full(item.shape) for item in halves],
            out_specs=[full((share, wide)), full((share, 3 * wide))]
            + [full((size,)) for size in sizes],
            scratch_shapes=[
                pltpu.VMEM((2 * halves[0].shape[0], wide), F32),
                pltpu.VMEM((2 * halves[2].shape[0], wide), F32),
            ],
        ),
        out_shape=[hbm((share, wide), F32), hbm((share, 3 * wide), F32)]
        + [jax.ShapeDtypeStruct((size,), F32) for size in sizes],
        compiler_params=params(VMEM_MIB, 1),
        cost_estimate=cost(),
        name="attn_final",
    )(spot, *halves)


def chunks_for(grid_rows, hidden_units):
    for count in (2, 3):
        if hidden_units % (grid_rows * count * LANE) == 0:
            return count
    return 1


def body(
    layer_input,
    w_qkv,
    b_qkv,
    w_out,
    b_out,
    ln1_gain,
    ln1_bias,
    w_up,
    b_up,
    w_down,
    b_down,
    ln2_gain,
    ln2_bias,
    segment_ids,
    doc_lengths,
    cotangent,
):
    tokens, model = layer_input.shape
    seqs, docs = doc_lengths.shape
    length = tokens // seqs
    grid_rows = lax.axis_size("mx")
    hidden_units = 2 * w_up.shape[1]
    chunk_count = chunks_for(grid_rows, hidden_units)
    row = lax.axis_index("mx")
    col = lax.axis_index("my")
    place = lax.axis_index("dp")
    spot = jnp.stack(
        [jnp.asarray(item, jnp.int32) for item in (row, col, place % 2, place // 2)]
    )
    places = piece_places()

    small = [b_qkv, b_out, ln1_gain, ln1_bias, b_up, b_down, ln2_gain, ln2_bias]
    sizes = [item.shape[0] for item in small]
    packed = pack_vectors(small)
    far_packed = fetch_far(packed)
    w_attn = jnp.concatenate([w_qkv, w_out], axis=1)
    far_attn = fetch_far(w_attn, packed)
    n_attn, n_up, n_down = (fetch_near(item) for item in (w_attn, w_up, w_down))
    p_packed = fetch_rest(fetch_near(packed), far_packed)
    bias_qkv, bias_up, rest = spread_vectors(places, p_packed, sizes, chunk_count)

    segs = segment_ids.reshape(seqs, length)
    member = segs[:, :, None] == jnp.arange(docs, dtype=jnp.int32)[None, None, :]
    span = jnp.sum(jnp.where(member, doc_lengths[:, None, :], 0), axis=2)
    spots = jnp.arange(length, dtype=jnp.int32)[None, :]
    angle = 0.5 * math.pi * spots.astype(F32) / span.astype(F32)
    angle = angle.reshape(tokens, 1)
    lane = jnp.arange(LANE, dtype=jnp.int32)[None, :]
    cs = jnp.where(lane < HD, jnp.cos(angle), jnp.sin(angle))
    seg = (segs + docs * jnp.arange(seqs, dtype=jnp.int32)[:, None]).reshape(tokens)
    segc = seg.reshape(tokens, 1)
    segr = seg.reshape(1, tokens)
    tiles = seg.reshape(tokens // TILE, TILE)
    before = jnp.concatenate([jnp.full((1,), -1, jnp.int32), tiles[:-1, -1]])
    q_on = (tiles == before[:, None]).reshape(tokens, 1)
    k_on = (tiles == tiles[:, -1:]).reshape(tokens, 1)
    qm = jnp.broadcast_to(q_on.astype(F32), (tokens, LANE))
    km = jnp.broadcast_to(k_on.astype(F32), (tokens, LANE))
    x_t = layer_input.T

    cs, segc, qm, km = lax.optimization_barrier((cs, segc, qm, km))
    p_attn = fetch_rest(n_attn, far_attn, bias_qkv, cs, segc, qm, km)
    far_up = fetch_far(w_up, p_attn[-1])
    far_down = fetch_far(w_down, p_attn[-1])
    qf, kf, vp, attn_a, attn_b, rden, wp_qkv = attend(
        places, layer_input, p_attn, bias_qkv, cs, segc, segr, qm, km
    )
    xhat, rstd, hidden, hidden_t, attn_t, wp_out = join(
        places, attn_a, attn_b, layer_input, p_attn, rest
    )
    p_up = fetch_rest(n_up, far_up, hidden)
    act, slope, wp_up = up_project(places, hidden, p_up, bias_up, chunk_count)
    p_down = fetch_rest(n_down, far_down, act)
    block_out, sums_two, d_hid, up_sums, *messages = ffn(
        places, spot, act, slope, xhat, cotangent, p_down, rest, hidden_t, wp_up, chunk_count
    )
    keeps, sends = messages[:chunk_count], messages[chunk_count:]
    chains = [
        Chain(send, keep, [("halve", 1), ("mx", None)] if i % 2 else [("mx", None), ("halve", 1)])
        for i, (send, keep) in enumerate(zip(sends, keeps))
    ]

    def turn(after, *rounds):
        for picks in rounds:
            live = [chains[i] for i in picks]
            arrived = lax.optimization_barrier((after,) + tuple(item.terms[-1][0] for item in live))
            after = arrived[0]
            for item, array in zip(live, arrived[1:]):
                item.terms[-1] = (array, item.terms[-1][1])
                if item.step(after):
                    after = item.fresh
        return after

    d_hid = gate(d_hid, sends)
    first = chunk_count
    dn, d_res1, keep, send = norm_back(
        spot, d_hid, xhat, rstd, attn_a, attn_b, rden, wp_out, rest, attn_t, sums_two, up_sums
    )
    dn = gate(dn, [turn(d_res1, tuple(range(first)))])
    early, keep, send = group_back(
        spot, qf, kf, vp, dn, cs, segc, segr, qm, km, x_t, 0, GROUPS - 1, (keep, send)
    )
    chains.append(Chain(send, keep, plan(SPLITS[0])))
    dn = gate(dn, [send, turn(early, tuple(range(first)))])
    late, keep, send = group_back(
        spot, qf, kf, vp, dn, cs, segc, segr, qm, km, x_t, GROUPS - 1, 1, ()
    )
    chains.append(Chain(send, keep, plan(SPLITS[1])))
    arrived = lax.optimization_barrier(
        (late,) + tuple(chain.terms[-1][0] for chain in chains[:first])
    )
    for chain, array in zip(chains, arrived[1:]):
        chain.terms[-1] = (array, chain.terms[-1][1])
    ffn_part = jnp.concatenate([chain.part(0, chain.rows, 0) for chain in chains[:first]], axis=0)
    ffn_sum = deep_sum(ffn_part)
    chains = chains[first:]
    after = turn(ffn_part, *TURNS[0])
    early = gate(early, [send, after])
    input_grad = input_back(early, late, wp_qkv, d_res1)
    after = turn(input_grad, *TURNS[1])
    ffn_sum = gate(ffn_sum, [after])
    ffn_other = flip(ffn_sum, 1)
    turn(ffn_sum, *TURNS[2])
    attn_halves = [item for chain in chains for item in chain.finish()]
    g_up, g_down = ffn_final(spot, ffn_sum, ffn_other, chunk_count)
    g_out, g_qkv, g_bqkv, g_bout, g_gain1, g_bias1, g_bup, g_bdown, g_gain2, g_bias2 = attn_final(
        spot, attn_halves, sizes, model, chunk_count
    )
    return (
        block_out,
        input_grad,
        g_qkv,
        g_bqkv,
        g_out,
        g_bout,
        g_gain1,
        g_bias1,
        g_up,
        g_bup,
        g_down,
        g_bdown,
        g_gain2,
        g_bias2,
    )


def solution(mesh):
    return jax.shard_map(
        body,
        mesh=mesh,
        in_specs=(
            P(("dp", "mx", "my"), None),
            P("mx", "my"),
            P(("mx", "my")),
            P("mx", "my"),
            P(("mx", "my")),
            P(("mx", "my")),
            P(("mx", "my")),
            P("mx", "my"),
            P(("mx", "my")),
            P("mx", "my"),
            P(("mx", "my")),
            P(("mx", "my")),
            P(("mx", "my")),
            P(("dp", "mx", "my")),
            P(("dp", "mx", "my"), None),
            P(("dp", "mx", "my"), None),
        ),
        out_specs=(
            P(("dp", "mx", "my"), None),
            P(("dp", "mx", "my"), None),
            P("mx", "my"),
            P(("mx", "my")),
            P("mx", "my"),
            P(("mx", "my")),
            P(("mx", "my")),
            P(("mx", "my")),
            P("mx", "my"),
            P(("mx", "my")),
            P("mx", "my"),
            P(("mx", "my")),
            P(("mx", "my")),
            P(("mx", "my")),
        ),
        check_vma=False,
    )
```

```python
import functools
import math

import jax
import jax.numpy as jnp
from jax import lax
from jax.experimental import pallas as pl
from jax.experimental.pallas import tpu as pltpu
from jax.sharding import PartitionSpec as P

HD = 64
LANE = 128
TILE = 256
GROUPS = 3
MIB = 1 << 20
VMEM_MIB = 58
BLOCK = 768
VECTOR_ROWS = 64
SPLITS = (2, 1)
TURNS = (
    ((0,), (1,)),
    ((0,), (1,), (0,), (1,), (0,), (1,)),
    ((0,), (1,), (0,)),
)

BF = jnp.bfloat16
F32 = jnp.float32
norm_eps = 1e-05


def dot(left, right):
    return lax.dot_general(left, right, (((1,), (0,)), ((), ())), preferred_element_type=F32)


def dot_t(left, right):
    return lax.dot_general(left, right, (((1,), (1,)), ((), ())), preferred_element_type=F32)


def t_dot(left, right):
    return lax.dot_general(left, right, (((0,), (0,)), ((), ())), preferred_element_type=F32)


def low_half(shape):
    return lax.broadcasted_iota(jnp.int32, shape, 1) < HD


def params(limit, grid_dims=0):
    return pltpu.CompilerParams(
        dimension_semantics=("arbitrary",) * grid_dims if grid_dims else None,
        vmem_limit_bytes=limit * MIB,
    )


def cost(*_):
    return pl.CostEstimate(flops=1000, bytes_accessed=1000, transcendentals=0)


def hbm(shape, dtype):
    return pltpu.HBM(shape, dtype)


def vmem(shape, dtype):
    return jax.ShapeDtypeStruct(shape, dtype)


def full(shape):
    return pl.BlockSpec(shape, lambda *_: (0,) * len(shape))


ANY = pl.BlockSpec(memory_space=pl.ANY)


def shift(value, axis, step):
    size = lax.axis_size(axis)
    return lax.ppermute(value, axis, [(i, (i + step) % size) for i in range(size)])


def pair_swap(value, axis):
    size = lax.axis_size(axis)
    return lax.ppermute(value, axis, [(i, i ^ 1) for i in range(size)])


def flip(value, bit):
    size = lax.axis_size("dp")
    return lax.ppermute(value, "dp", [(i, i ^ bit) for i in range(size)])


def gate(value, deps):
    return lax.optimization_barrier((value,) + tuple(deps))[0]


def fetch_near(block):
    return [block, pair_swap(block, "my")]


def fetch_far(block, *deps):
    grid_rows = lax.axis_size("mx")
    block = gate(block, deps) if deps else block
    return [shift(block, "mx", step) for step in range(1, grid_rows)]


def fetch_rest(near, far, *deps):
    if deps:
        far = list(lax.optimization_barrier(tuple(far) + deps)[: len(far)])
    return near + far + [pair_swap(item, "my") for item in far]


def fetch_thirds(block, *deps):
    rows = block.shape[0] // 3
    grid_rows = lax.axis_size("mx")
    side = lax.axis_index("dp") % 2
    own = lax.dynamic_slice_in_dim(block, side * rows, rows, axis=0)
    pieces, places = [], []
    for step in range(1, grid_rows):
        first = shift(gate(own, deps), "mx", step)
        row = (lax.axis_index("mx") - step + grid_rows) % grid_rows * 3
        pieces += [first, flip(first, 1), shift(block[2 * rows :], "mx", step)]
        places += [(row + side) * rows, (row + 1 - side) * rows, (row + 2) * rows]
    return pieces, places


def third_places(places, rows):
    row = lax.axis_index("mx") * rows
    col = lax.axis_index("my")
    flat = [row, col, row, 1 - col]
    for c in (col, 1 - col):
        for place in places:
            flat += [place, c]
    return jnp.stack([jnp.asarray(item, jnp.int32) for item in flat])


def piece_places():
    grid_rows = lax.axis_size("mx")
    row = lax.axis_index("mx")
    col = lax.axis_index("my")
    places = [(row, col), (row, 1 - col)]
    for c in (col, 1 - col):
        for step in range(1, grid_rows):
            places.append(((row - step + grid_rows) % grid_rows, c))
    return jnp.stack([jnp.asarray(item, jnp.int32) for place in places for item in place])


def pack_kernel(*refs):
    out_ref = refs[-1]
    for index, ref in enumerate(refs[:-1]):
        size = ref.shape[0]
        out_ref[index : index + 1, 0:size] = ref[...].astype(F32).reshape(1, size)


def pack_vectors(vectors):
    wide = max(item.shape[0] for item in vectors)
    return pl.pallas_call(
        pack_kernel,
        out_shape=jax.ShapeDtypeStruct((len(vectors), wide), F32),
        compiler_params=params(VMEM_MIB),
        name="pack",
    )(*vectors)


def spread_kernel(sizes, grid_rows, chunk_count, places_ref, *refs):
    owners = grid_rows * 2
    qkv_ref, up_ref, rest_ref = refs[owners : owners + 3]
    scr = refs[owners + 3]
    rest = 0
    for index, size in enumerate(sizes):
        total = size * owners
        whole = jnp.zeros((1, total), F32)
        for owner in range(owners):
            place = places_ref[2 * owner] * 2 + places_ref[2 * owner + 1]
            scr[...] = jnp.zeros_like(scr)
            scr[:, 0:size] = refs[owner][index : index + 1, 0:size]
            whole = whole + pltpu.roll(scr[:, 0:total], place * size, 1)
        if index == 0:
            for unit in range(6 * GROUPS):
                part, pair = unit // (2 * GROUPS), unit % (2 * GROUPS)
                lane = (pair % GROUPS) * 6 * LANE + (2 * part + pair // GROUPS) * LANE
                qkv_ref[:, lane : lane + LANE] = whole[:, unit * LANE : (unit + 1) * LANE]
        elif index == 4:
            piece = total // grid_rows // chunk_count
            for i in range(grid_rows):
                for c in range(chunk_count):
                    src, dst = (i * chunk_count + c) * piece, (c * grid_rows + i) * piece
                    up_ref[:, dst : dst + piece] = whole[:, src : src + piece]
        else:
            rest_ref[rest : rest + 1, :] = whole
            rest += 1
    rest_ref[rest:8, :] = jnp.zeros((8 - rest, rest_ref.shape[1]), F32)


def spread_vectors(places, packs, sizes, chunk_count):
    grid_rows = lax.axis_size("mx")
    owners = grid_rows * 2
    wide = max(sizes) * owners
    return pl.pallas_call(
        functools.partial(spread_kernel, sizes, grid_rows, chunk_count),
        grid_spec=pltpu.PrefetchScalarGridSpec(
            num_scalar_prefetch=1,
            grid=(1,),
            in_specs=[full(item.shape) for item in packs],
            out_specs=[
                full((1, sizes[0] * owners)),
                full((1, sizes[4] * owners)),
                full((8, sizes[1] * owners)),
            ],
            scratch_shapes=[pltpu.VMEM((1, wide), F32)],
        ),
        out_shape=[
            jax.ShapeDtypeStruct((1, sizes[0] * owners), F32),
            jax.ShapeDtypeStruct((1, sizes[4] * owners), F32),
            jax.ShapeDtypeStruct((8, sizes[1] * owners), F32),
        ],
        compiler_params=params(VMEM_MIB, 1),
        name="spread",
    )(places, *packs)


def share_vectors(spot_ref, rows, groups, outs, grid_rows, chunk_count):
    owners = grid_rows * 2
    owner = spot_ref[0] * 2 + spot_ref[1]

    def pair(index):
        return [rows[2 * index : 2 * index + 1, :], rows[2 * index + 1 : 2 * index + 2, :]]

    qkv = []
    for unit in range(6 * GROUPS):
        part, place = unit // (2 * GROUPS), unit % (2 * GROUPS)
        lane = 2 * part + place // GROUPS
        row = groups[place % GROUPS][lane // 3 : lane // 3 + 1, :]
        qkv.append(row[:, (lane % 3) * LANE : (lane % 3 + 1) * LANE])
    wide = rows.shape[1]
    piece = outs[4].shape[0] * owners // grid_rows // chunk_count
    ups = []
    for i in range(grid_rows):
        for c in range(chunk_count):
            for part in range(piece // LANE):
                place = (c * grid_rows + i) * piece + part * LANE
                row, lane = 12 + place // wide, place % wide
                ups.append(rows[row : row + 1, lane : lane + LANE])
    for items, out_ref in zip(
        (qkv, pair(0), pair(1), pair(2), ups, pair(3), pair(4), pair(5)), outs
    ):
        size = out_ref.shape[0]
        total = size * owners
        whole = jnp.concatenate(items, axis=1)
        turned = pltpu.roll(whole, lax.rem(total - owner * size, total), 1)
        out_ref[...] = turned[:, 0:size].reshape(size)


def gates(values, dep):
    return list(lax.optimization_barrier(tuple(values) + (dep,))[:-1])


class Chain:
    def __init__(self, send, keep, plan):
        self.plan = plan
        self.stage = 0
        self.fresh = send
        self.terms = [(keep, 0), (pair_swap(send, "my"), 0)]
        self.rows = send.shape[1]
        self.split = True

    def part(self, first, rows, owner=None):
        result = None
        for array, start in self.terms:
            if array.ndim == 3:
                count = array.shape[0] if owner is None else 1
                at = (0 if owner is None else owner, start + first, 0)
                item = lax.dynamic_slice(array, at, (count, rows, array.shape[2]))
                item = item if owner is None else item[0]
            else:
                item = lax.dynamic_slice(array, (start + first, 0), (rows, array.shape[1]))
            if len(self.terms) > 2:
                item = item.astype(F32)
            result = item if result is None else result + item
        return result.astype(BF)

    def step(self, after=None):
        if self.stage == len(self.plan):
            return False
        kind, bit = self.plan[self.stage]
        self.stage += 1
        array, start = self.terms[-1]
        if after is not None:
            self.terms[-1] = (gate(array, [after]), start)
        owner = None if self.split else 0
        if kind == "mx":
            parts = [self.part(0, self.rows, i) for i in range(1, lax.axis_size("mx"))]
            self.fresh = parts[0]
            self.terms += [(shift(part, "mx", i + 1), 0) for i, part in enumerate(parts)]
            self.split = False
        elif kind == "halve":
            side = lax.axis_index("dp") // bit % 2
            self.rows //= 2
            self.fresh = self.part((1 - side) * self.rows, self.rows, owner)
            self.terms = [(array, start + side * self.rows) for array, start in self.terms]
            self.terms.append((flip(self.fresh, bit), 0))
        else:
            if kind == "join" and self.plan[self.stage - 2][0] == "join":
                self.fresh = jnp.concatenate([array for array, _ in self.terms], axis=0)
            else:
                self.fresh = self.part(0, self.rows, owner)
            self.terms = [(self.fresh, 0), (flip(self.fresh, bit), 0)]
        return True

    def finish(self):
        while self.step():
            pass
        return [array for array, _ in self.terms]


def plan(split):
    bits = []
    while 1 << len(bits) < lax.axis_size("dp"):
        bits.append(1 << len(bits))
    return (
        [("mx", None)]
        + [("halve", bit) for bit in bits[:split]]
        + [("whole", bit) for bit in bits[split:]]
        + [("join", bit) for bit in bits[:split][::-1]]
    )


def deep_sum(value):
    size = lax.axis_size("dp")
    groups = [list(range(start, size, 2)) for start in range(2)]
    return lax.psum(value, "dp", axis_index_groups=groups)


def place_copies(places_ref, refs, sems, put):
    copies = []
    for index, ref in enumerate(refs):
        copies += put(places_ref[2 * index], places_ref[2 * index + 1], ref)
    return [
        pltpu.make_async_copy(src, dst, sems.at[index]) for index, (src, dst) in enumerate(copies)
    ]


def aligned(value, size):
    return pl.multiple_of(value, size)


def attend_kernel(pieces, width, places_ref, *refs):
    x_ref = refs[0]
    w_refs = refs[1 : 1 + pieces]
    bias_ref, cs_ref, segc_ref, segr_ref, qm_ref, km_ref = refs[1 + pieces : 7 + pieces]
    qf_ref, kf_ref, vp_ref, out_a, out_b, rden_ref, wp_ref = refs[7 + pieces : 14 + pieces]
    w_scr, mask_scr, sems, out_sem = refs[14 + pieces :]
    step = pl.program_id(0)
    tokens = x_ref.shape[0]
    model = x_ref.shape[1]
    chunks = tokens // TILE
    units = width // LANE

    def put(row, col, ref):
        rows = ref.shape[0]
        start = aligned(row, 16)
        result = []
        for unit in range(units):
            where = col * units + unit
            part = where // (2 * GROUPS)
            pair = where % (2 * GROUPS)
            group = pair % GROUPS
            lane = aligned(part * (2 * LANE) + (pair // GROUPS) * LANE, LANE)
            result.append(
                (
                    ref.at[:, unit * LANE : (unit + 1) * LANE],
                    w_scr.at[group, pl.ds(start, rows), pl.ds(lane, LANE)],
                )
            )
        return result

    out_copy = pltpu.make_async_copy(w_scr, wp_ref, out_sem)

    @pl.when(step == 0)
    def _():
        copies = place_copies(places_ref, w_refs, sems, put)
        for copy in copies:
            copy.start()
        ii = lax.broadcasted_iota(jnp.int32, (TILE, TILE), 0)
        jj = lax.broadcasted_iota(jnp.int32, (TILE, TILE), 1)
        for c in range(chunks):
            rows = slice(c * TILE, (c + 1) * TILE)
            keep = (segc_ref[rows, :] == segr_ref[:, rows]) & (jj <= ii)
            mask_scr[c] = jnp.where(keep, 1.0, 0.0)
        for copy in copies:
            copy.wait()
        out_copy.start()

    low = low_half((TILE, LANE))
    for r in range(chunks):
        rows = slice(r * TILE, (r + 1) * TILE)
        acc = dot(x_ref[rows, :], w_scr[step]) + bias_ref[...]
        cs = cs_ref[rows, :]
        for a in range(2):
            q = jnp.maximum(acc[:, a * LANE : (a + 1) * LANE], 0.0) * 0.125
            k = jnp.maximum(acc[:, (2 + a) * LANE : (3 + a) * LANE], 0.0)
            v = acc[:, (4 + a) * LANE : (5 + a) * LANE]
            q_r = pltpu.roll(q, HD, 1)
            k_r = pltpu.roll(k, HD, 1)
            first = slice(2 * a * LANE, (2 * a + 1) * LANE)
            second = slice((2 * a + 1) * LANE, (2 * a + 2) * LANE)
            qf_ref[rows, first] = (jnp.where(low, q, q_r) * cs).astype(BF)
            qf_ref[rows, second] = (jnp.where(low, q_r, q) * cs).astype(BF)
            kf_ref[rows, first] = (jnp.where(low, k, k_r) * cs).astype(BF)
            kf_ref[rows, second] = (jnp.where(low, k_r, k) * cs).astype(BF)
            vp_ref[rows, first] = jnp.where(low, v, 1.0).astype(BF)
            vp_ref[rows, second] = jnp.where(low, 1.0, v).astype(BF)

    states = [None] * 4
    totals = [None] * 4
    for c in range(chunks):
        rows = slice(c * TILE, (c + 1) * TILE)
        mask = mask_scr[c]
        qm = qm_ref[rows, :]
        km = km_ref[rows, :]
        for a in range(2):
            outs, denoms = [], []
            for h in (2 * a, 2 * a + 1):
                cols = slice(h * LANE, (h + 1) * LANE)
                q = qf_ref[rows, cols]
                k = kf_ref[rows, cols]
                v = vp_ref[rows, cols]
                scores = dot_t(q, k) * mask
                out = dot(scores.astype(BF), v)
                denom = scores[:, :LANE] + scores[:, LANE:]
                if c > 0:
                    out = out + qm * dot(q, states[h].astype(BF))
                    denom = denom + q.astype(F32) * (totals[h] * qm)
                outs.append(out)
                denoms.append(jnp.sum(denom, axis=1, keepdims=True))
                if c < chunks - 1:
                    held = k * km.astype(BF)
                    grown = t_dot(held, v)
                    total = jnp.sum(held.astype(F32), axis=0, keepdims=True)
                    if c > 0:
                        whole = qm[TILE - 1 : TILE, :]
                        grown = grown + states[h] * whole
                        total = total + totals[h] * whole
                    states[h] = grown
                    totals[h] = total
            numer = jnp.where(low, outs[0], outs[1])
            rden = 1.0 / jnp.maximum(jnp.where(low, denoms[0], denoms[1]), 1.0)
            rden_ref[rows, a * LANE : (a + 1) * LANE] = rden
            (out_a, out_b)[a][rows, :] = (numer * rden).astype(BF)

    @pl.when(step == GROUPS - 1)
    def _():
        out_copy.wait()


def attend(places, x, pieces, bias, cs, segc, segr, qm, km):
    tokens, model = x.shape
    count = len(pieces)
    width = 3 * model // 2
    group = 6 * LANE
    spec = pl.BlockSpec((tokens, 4 * LANE), lambda g, p: (0, g))
    half = pl.BlockSpec((tokens, LANE), lambda g, p: (0, g))
    return pl.pallas_call(
        functools.partial(attend_kernel, count, width),
        grid_spec=pltpu.PrefetchScalarGridSpec(
            num_scalar_prefetch=1,
            grid=(GROUPS,),
            in_specs=[full((tokens, model))]
            + [ANY] * count
            + [
                pl.BlockSpec((1, group), lambda g, p: (0, g)),
                full((tokens, LANE)),
                full((tokens, 1)),
                full((1, tokens)),
                full((tokens, LANE)),
                full((tokens, LANE)),
            ],
            out_specs=[
                spec,
                spec,
                spec,
                half,
                half,
                pl.BlockSpec((tokens, 2 * LANE), lambda g, p: (0, g)),
                ANY,
            ],
            scratch_shapes=[
                pltpu.VMEM((GROUPS, model, group), BF),
                pltpu.VMEM((tokens // TILE, TILE, TILE), F32),
                pltpu.SemaphoreType.DMA((count * (width // LANE),)),
                pltpu.SemaphoreType.DMA,
            ],
        ),
        out_shape=[hbm((tokens, GROUPS * 4 * LANE), BF)] * 3
        + [jax.ShapeDtypeStruct((tokens, GROUPS * LANE), BF)] * 2
        + [
            hbm((tokens, model), F32),
            hbm((GROUPS, model, group), BF),
        ],
        compiler_params=params(VMEM_MIB, 1),
        cost_estimate=cost(2 * tokens * model * 3 * model * 1.8, 20 * MIB),
        name="attend",
    )(places, x, *pieces, bias, cs, segc, segr, qm, km)


def rows_put(target, first):
    def put(row, col, ref):
        rows = ref.shape[0]
        width = ref.shape[1] - first
        start = row
        return [
            (
                ref.at[:, first : first + width],
                target.at[pl.ds(aligned(start, 16), rows), pl.ds(aligned(col * width, LANE), width)],
            )
        ]

    return put


def join_kernel(pieces, places_ref, *refs):
    a_ref, b_ref, x_ref = refs[:3]
    w_refs = refs[3 : 3 + pieces]
    rest_ref = refs[3 + pieces]
    xhat_ref, rstd_ref, hb_ref, ht_ref, at_ref, wo_ref = refs[4 + pieces : 10 + pieces]
    w_scr, sems, out_sem = refs[10 + pieces :]
    step = pl.program_id(0)
    out_copy = pltpu.make_async_copy(w_scr, wo_ref, out_sem)

    @pl.when(step == 0)
    def _():
        copies = place_copies(places_ref, w_refs, sems, rows_put(w_scr, 3 * w_scr.shape[1] // 2))
        for copy in copies:
            copy.start()
        for copy in copies:
            copy.wait()
        out_copy.start()

    attn = jnp.concatenate([a_ref[...], b_ref[...]], axis=1)
    resid = x_ref[...].astype(F32) + dot(attn, w_scr[...]) + rest_ref[0:1, :]
    center = resid - jnp.mean(resid, axis=1, keepdims=True)
    rstd = lax.rsqrt(jnp.mean(center * center, axis=1, keepdims=True) + norm_eps)
    xhat = center * rstd
    hidden = xhat * rest_ref[1:2, :] + rest_ref[2:3, :]
    xhat_ref[...] = xhat
    rstd_ref[...] = jnp.broadcast_to(rstd, rstd_ref.shape)
    hb_ref[...] = hidden.astype(BF)
    ht_ref[...] = hidden.T.astype(BF)
    at_ref[...] = attn.astype(F32).T.astype(BF)

    @pl.when(step == pl.num_programs(0) - 1)
    def _():
        out_copy.wait()


def join(places, attn_a, attn_b, x, pieces, rest):
    tokens, model = x.shape
    count = len(pieces)
    row = pl.BlockSpec((TILE, model), lambda r, p: (r, 0))
    half = pl.BlockSpec((TILE, model // 2), lambda r, p: (r, 0))
    flip = pl.BlockSpec((model, TILE), lambda r, p: (0, r))
    return pl.pallas_call(
        functools.partial(join_kernel, count),
        grid_spec=pltpu.PrefetchScalarGridSpec(
            num_scalar_prefetch=1,
            grid=(tokens // TILE,),
            in_specs=[half, half, row] + [ANY] * count + [full((8, model))],
            out_specs=[row, pl.BlockSpec((TILE, LANE), lambda r, p: (r, 0)), row, flip, flip, ANY],
            scratch_shapes=[
                pltpu.VMEM((model, model), BF),
                pltpu.SemaphoreType.DMA((count,)),
                pltpu.SemaphoreType.DMA,
            ],
        ),
        out_shape=[
            hbm((tokens, model), F32),
            hbm((tokens, LANE), F32),
            vmem((tokens, model), BF),
            hbm((model, tokens), BF),
            hbm((model, tokens), BF),
            hbm((model, model), BF),
        ],
        compiler_params=params(VMEM_MIB, 1),
        cost_estimate=cost(2 * tokens * model * model, 14 * MIB),
        name="join",
    )(places, attn_a, attn_b, x, *pieces, rest)


def up_kernel(pieces, chunk_count, places_ref, *refs):
    h_ref = refs[0]
    w_refs = refs[1 : 1 + pieces]
    bias_ref = refs[1 + pieces]
    act_ref, slope_ref, wp_ref = refs[2 + pieces : 5 + pieces]
    w_scr, sems, out_sem = refs[5 + pieces :]
    step = pl.program_id(0)
    wide = w_scr.shape[2]
    out_copy = pltpu.make_async_copy(w_scr, wp_ref, out_sem)

    @pl.when(step == 0)
    def _():
        width = w_refs[0].shape[1]
        piece = wide // lax.axis_size("mx")
        blocks = width // (piece * chunk_count)

        def put(row, col, ref):
            rows = ref.shape[0]
            start = row * rows
            result = []
            for i in range(blocks):
                for c in range(chunk_count):
                    lane = aligned((col * blocks + i) * piece, LANE)
                    src = (i * chunk_count + c) * piece
                    result.append(
                        (
                            ref.at[:, src : src + piece],
                            w_scr.at[c, pl.ds(aligned(start, 16), rows), pl.ds(lane, piece)],
                        )
                    )
            return result

        copies = place_copies(places_ref, w_refs, sems, put)
        for copy in copies:
            copy.start()
        for copy in copies:
            copy.wait()
        out_copy.start()

    tokens = h_ref.shape[0]
    for r in range(tokens // TILE):
        rows = slice(r * TILE, (r + 1) * TILE)
        up = dot(h_ref[rows, :], w_scr[step]) + bias_ref[...]
        phi = lax.erf(up * math.sqrt(0.5)) * 0.5 + 0.5
        bell = jnp.exp(up * up * -0.5) * (1.0 / math.sqrt(2.0 * math.pi))
        act_ref[rows, :] = (up * phi).astype(BF)
        slope_ref[rows, :] = (phi + up * bell).astype(BF)

    @pl.when(step == pl.num_programs(0) - 1)
    def _():
        out_copy.wait()


def up_project(places, hidden, pieces, bias, chunk_count):
    tokens, model = hidden.shape
    count = len(pieces)
    hidden_units = pieces[0].shape[1] * 2
    wide = hidden_units // chunk_count
    piece = wide // lax.axis_size("mx")
    per = pieces[0].shape[1] // piece
    col = pl.BlockSpec((tokens, wide), lambda c, p: (0, c))
    return pl.pallas_call(
        functools.partial(up_kernel, count, chunk_count),
        grid_spec=pltpu.PrefetchScalarGridSpec(
            num_scalar_prefetch=1,
            grid=(chunk_count,),
            in_specs=[full((tokens, model))]
            + [ANY] * count
            + [pl.BlockSpec((1, wide), lambda c, p: (0, c))],
            out_specs=[col, col, ANY],
            scratch_shapes=[
                pltpu.VMEM((chunk_count, model, wide), BF),
                pltpu.SemaphoreType.DMA((count * per,)),
                pltpu.SemaphoreType.DMA,
            ],
        ),
        out_shape=[hbm((tokens, hidden_units), BF)] * 2 + [hbm((chunk_count, model, wide), BF)],
        compiler_params=params(VMEM_MIB, 1),
        cost_estimate=cost(
            2 * tokens * model * hidden_units, 24 * MIB, 2 * tokens * hidden_units
        ),
        name="up",
    )(places, hidden, *pieces, bias)


def once(shape):
    return pl.BlockSpec(shape, lambda *_: (0,) * len(shape), pipeline_mode=pl.Buffered(1))


def ffn_kernel(pieces, chunk_count, grid_rows, piece, tiles, places_ref, spot_ref, *refs):
    rowa_ref, xhat_ref, cot_ref = refs[:3]
    w_refs = refs[3 : 3 + pieces]
    rest_ref, ht_hbm, act_ref, slope_ref, wu_ref = refs[3 + pieces : 8 + pieces]
    outs = refs[8 + pieces :]
    out_ref, sums_ref, dh_ref, bsum_ref = outs[:4]
    keeps = outs[4 : 4 + chunk_count]
    sends = outs[4 + chunk_count : 4 + 2 * chunk_count]
    w_scr, dup_scr, dd_ref, ddt_ref, ht_ref, sems, ht_sem = outs[4 + 2 * chunk_count :]
    row, col = spot_ref[0], spot_ref[1]
    step = pl.program_id(0)
    wide = w_scr.shape[0] // chunk_count
    tokens, block = act_ref.shape
    model = dh_ref.shape[1]
    half, share = model // 2, model // grid_rows
    per = grid_rows // 2
    ht_copy = pltpu.make_async_copy(ht_hbm, ht_ref, ht_sem)

    @pl.when(step == 0)
    def _():
        def put(row, col, ref):
            width = ref.shape[1]
            lane = pl.ds(aligned(col * width, LANE), width)
            return [
                (
                    ref.at[c * piece : (c + 1) * piece, :],
                    w_scr.at[pl.ds(aligned(c * wide + row * piece, 16), piece), lane],
                )
                for c in range(chunk_count)
            ]

        copies = place_copies(places_ref, w_refs, sems, put)
        for copy in copies:
            copy.start()
        ht_copy.start()
        sums_ref[...] = jnp.zeros_like(sums_ref)
        for copy in copies:
            copy.wait()

    @pl.when(step < tiles)
    def _():
        rows = pl.ds(aligned(step * TILE, TILE), TILE)
        hidden = xhat_ref[...] * rest_ref[1:2, :] + rest_ref[2:3, :]
        resid = hidden + dot(rowa_ref[...], w_scr[...]) + rest_ref[3:4, :]
        center = resid - jnp.mean(resid, axis=1, keepdims=True)
        rstd = lax.rsqrt(jnp.mean(center * center, axis=1, keepdims=True) + norm_eps)
        xhat = center * rstd
        out_ref[...] = (xhat * rest_ref[4:5, :] + rest_ref[5:6, :]).astype(BF)
        g = cot_ref[...].astype(F32)
        e = g * rest_ref[4:5, :]
        d_res = rstd * (
            e
            - jnp.mean(e, axis=1, keepdims=True)
            - xhat * jnp.mean(e * xhat, axis=1, keepdims=True)
        )
        dh_ref[rows, :] = d_res
        d_down = d_res.astype(BF)
        dd_ref[rows, :] = d_down
        ddt_ref[:, rows] = d_down.T
        sums_ref[0:1, :] += jnp.sum(g * xhat, axis=0, keepdims=True)
        sums_ref[1:2, :] += jnp.sum(g, axis=0, keepdims=True)
        sums_ref[2:3, :] += jnp.sum(d_down.astype(F32), axis=0, keepdims=True)

    @pl.when(step == tiles)
    def _():
        ht_copy.wait()

    @pl.when(step >= tiles)
    def _():
        turn = step - tiles
        blocks = piece // block
        owner = lax.rem(turn // blocks, grid_rows)
        chunk = turn // (blocks * grid_rows)
        lane = pl.ds(aligned(lax.rem(turn, blocks) * block, LANE), block)
        wd = w_scr.at[pl.ds(aligned(turn * block, 16), block), :]
        total = jnp.zeros((1, block), F32)
        for r in range(tokens // TILE):
            rows = slice(r * TILE, (r + 1) * TILE)
            grad = (dot_t(dd_ref[rows, :], wd[...]) * slope_ref[rows, :].astype(F32)).astype(BF)
            dup_scr[rows, :] = grad
            total = total + jnp.sum(grad.astype(F32), axis=0, keepdims=True)
        bsum_ref[...] = jnp.broadcast_to(total, bsum_ref.shape)
        for r in range(tokens // TILE):
            rows = slice(r * TILE, (r + 1) * TILE)
            dh_ref[rows, :] += dot_t(dup_scr[rows, :], wu_ref[...])
        slot = lax.rem(owner - row + grid_rows, grid_rows)
        place = aligned(half + lax.rem(owner, per) * share, 16)
        down = dot(ddt_ref[pl.ds(aligned(col * half, 16), half), :], act_ref[...]).astype(BF)
        down_far = dot(
            ddt_ref[pl.ds(aligned((1 - col) * half, 16), half), :], act_ref[...]
        ).astype(BF)
        up = dot(ht_ref[...], dup_scr[...]).astype(BF)
        for c in range(chunk_count):

            @pl.when(chunk == c)
            def _():
                keeps[c][slot, 0:half, lane] = down
                sends[c][slot, 0:half, lane] = down_far
                for mine, target in ((True, keeps[c]), (False, sends[c])):

                    @pl.when((owner // per == col) == mine)
                    def _():
                        for i in range(grid_rows):
                            where = lax.rem(i - row + grid_rows, grid_rows)
                            target[where, pl.ds(place, share), lane] = up[
                                i * share : (i + 1) * share, :
                            ]


def ffn(places, spot, act, slope, xhat, cot, pieces, rest, hidden_t, w_up, chunk_count):
    tokens, hidden_units = act.shape
    model = xhat.shape[1]
    count = len(pieces)
    grid_rows = lax.axis_size("mx")
    wide = hidden_units // chunk_count
    piece = wide // grid_rows
    block = min(piece, BLOCK)
    message = (grid_rows, model, piece)
    tiles = tokens // TILE
    inner = wide // block

    def row(width):
        return pl.BlockSpec((TILE, width), lambda s, *_: (jnp.minimum(s, tiles - 1), 0))

    def late(s):
        return jnp.maximum(s - tiles, 0)

    pick = pl.BlockSpec((tokens, block), lambda s, *_: (0, late(s)))
    return pl.pallas_call(
        functools.partial(ffn_kernel, count, chunk_count, grid_rows, piece, tiles),
        grid_spec=pltpu.PrefetchScalarGridSpec(
            num_scalar_prefetch=2,
            grid=(tiles + hidden_units // block,),
            in_specs=[row(hidden_units), row(model), row(model)]
            + [ANY] * count
            + [
                once((8, model)),
                ANY,
                pick,
                pick,
                pl.BlockSpec(
                    (None, model, block), lambda s, *_: (late(s) // inner, 0, late(s) % inner)
                ),
            ],
            out_specs=[
                row(model),
                once((8, model)),
                once((tokens, model)),
                pl.BlockSpec((8, block), lambda s, *_: (0, late(s))),
            ]
            + [once(message)] * (2 * chunk_count),
            scratch_shapes=[
                pltpu.VMEM((hidden_units, model), BF),
                pltpu.VMEM((tokens, block), BF),
                pltpu.VMEM((tokens, model), BF),
                pltpu.VMEM((model, tokens), BF),
                pltpu.VMEM((model, tokens), BF),
                pltpu.SemaphoreType.DMA((count * chunk_count,)),
                pltpu.SemaphoreType.DMA,
            ],
        ),
        out_shape=[
            hbm((tokens, model), BF),
            vmem((8, model), F32),
            hbm((tokens, model), F32),
            vmem((8, hidden_units), F32),
        ]
        + [hbm(message, BF)] * (2 * chunk_count),
        compiler_params=params(VMEM_MIB, 1),
        cost_estimate=cost(),
        name="ffn",
    )(places, spot, act, xhat, cot, *pieces, rest, hidden_t, act, slope, w_up)


def norm_kernel(grid_rows, spot_ref, *refs):
    (
        dres_ref,
        xhat_ref,
        rstd_ref,
        a_ref,
        b_ref,
        rden_ref,
        wo_ref,
        gain_ref,
        at_ref,
        two_ref,
        up_ref,
    ) = refs[:11]
    dn_ref, dr_ref, keep_ref, send_ref, sums_ref, db_scr, msg_scr, ext_scr, sems = refs[11:]
    step = pl.program_id(0)
    model = dres_ref.shape[1]

    @pl.when(step == 0)
    def _():
        sums_ref[...] = jnp.zeros_like(sums_ref)

    d_hidden = dres_ref[...]
    xhat = xhat_ref[...]
    e = d_hidden * gain_ref[1:2, :]
    d_res = rstd_ref[:, 0:1] * (
        e
        - jnp.mean(e, axis=1, keepdims=True)
        - xhat * jnp.mean(e * xhat, axis=1, keepdims=True)
    )
    dr_ref[...] = d_res
    d_branch = d_res.astype(BF)
    db_scr[pl.ds(aligned(step * TILE, TILE), TILE), :] = d_branch
    sums_ref[0:1, :] += jnp.sum(d_hidden * xhat, axis=0, keepdims=True)
    sums_ref[1:2, :] += jnp.sum(d_hidden, axis=0, keepdims=True)
    sums_ref[2:3, :] += jnp.sum(d_branch.astype(F32), axis=0, keepdims=True)
    d_attn = dot_t(d_branch, wo_ref[...])
    low = low_half((TILE, LANE))
    li = lax.broadcasted_iota(jnp.int32, (LANE, LANE), 0) < HD
    lj = lax.broadcasted_iota(jnp.int32, (LANE, LANE), 1) < HD
    swap = jnp.where(li == lj, 0.0, 1.0 / HD).astype(BF)
    front = lax.broadcasted_iota(jnp.int32, (TILE, LANE), 1) % HD < HD // 2
    for pair in range(2 * GROUPS):
        a, g = pair // GROUPS, pair % GROUPS
        d_pair = d_attn[:, pair * LANE : (pair + 1) * LANE]
        attn = (a_ref, b_ref)[a][:, g * LANE : (g + 1) * LANE].astype(F32)
        rden = rden_ref[:, (2 * g + a) * LANE : (2 * g + a + 1) * LANE]
        prod = d_pair * attn
        high = prod.astype(BF)
        rest = (prod - high.astype(F32)).astype(BF)
        other = dot(high, swap) + dot(rest, swap)
        turned = pltpu.roll(rden, HD, 1)
        d_denom = jnp.where(turned < 1.0, -other * turned, 0.0)
        coarse = d_denom.astype(BF).astype(F32)
        d_denom = 2.0 * jnp.where(front, coarse, d_denom - coarse)
        d_numer = d_pair * rden
        place = (4 * g + 2 * a) * LANE
        dn_ref[:, place : place + LANE] = jnp.where(low, d_numer, d_denom).astype(BF)
        dn_ref[:, place + LANE : place + 2 * LANE] = jnp.where(low, d_denom, d_numer).astype(BF)

    @pl.when(step == pl.num_programs(0) - 1)
    def _():
        row, col = spot_ref[0], spot_ref[1]
        half = model // 2
        share = model // grid_rows
        wide = ext_scr.shape[1]
        ext_scr[...] = jnp.zeros_like(ext_scr)
        for index, (ref, line) in enumerate(
            ((sums_ref, 2), (sums_ref, 0), (sums_ref, 1), (two_ref, 2), (two_ref, 0), (two_ref, 1))
        ):
            for part in range(2):
                ext_scr[2 * index + part : 2 * index + part + 1, :] = ref[
                    line : line + 1, part * wide : (part + 1) * wide
                ].astype(BF)
        for part in range(up_ref.shape[1] // wide):
            ext_scr[12 + part : 13 + part, :] = up_ref[
                0:1, part * wide : (part + 1) * wide
            ].astype(BF)
        message_out(
            row, col, grid_rows, at_ref, db_scr, msg_scr, ext_scr, keep_ref, send_ref, 0, 3, 0, sems
        )


def message_out(
    row, col, grid_rows, left_ref, right_ref, msg_scr, ext_scr, keep_ref, send_ref, place, parts,
    line, sems,
):
    share, half = msg_scr.shape[2:]
    count = ext_scr.shape[0]
    copies = []
    for index, (side, target) in enumerate(((1 - col, send_ref), (col, keep_ref))):
        right = right_ref[:, pl.ds(aligned(side * half, LANE), half)]
        grad = dot(left_ref[...], right).astype(BF)
        for i in range(grid_rows):
            slot = lax.rem(i - row + grid_rows, grid_rows)
            msg_scr[index, slot] = grad[i * share : (i + 1) * share, :]
        pairs = [(msg_scr.at[index], target.at[:, pl.ds(aligned(place * share, 8), share), :])]
        lines = pl.ds(aligned(parts * share + line, 8), count)
        pairs += [(ext_scr, target.at[i, lines, :]) for i in range(grid_rows)]
        for src, dst in pairs:
            copy = pltpu.make_async_copy(src, dst, sems.at[len(copies)])
            copy.start()
            copies.append(copy)
    for copy in copies:
        copy.wait()


def norm_back(
    spot, d_hid, xhat, rstd, attn_a, attn_b, rden, w_out, rest, attn_t, sums_two, up_sums
):
    tokens, model = d_hid.shape
    grid_rows = lax.axis_size("mx")
    row = pl.BlockSpec((TILE, model), lambda r, p: (r, 0))
    half = pl.BlockSpec((TILE, model // 2), lambda r, p: (r, 0))
    share = model // grid_rows
    message = (grid_rows, 3 * share + VECTOR_ROWS, model // 2)
    return pl.pallas_call(
        functools.partial(norm_kernel, grid_rows),
        grid_spec=pltpu.PrefetchScalarGridSpec(
            num_scalar_prefetch=1,
            grid=(tokens // TILE,),
            in_specs=[
                row,
                row,
                pl.BlockSpec((TILE, LANE), lambda r, p: (r, 0)),
                half,
                half,
                row,
                once((model, model)),
                once((8, model)),
                once((model, tokens)),
                once(sums_two.shape),
                once(up_sums.shape),
            ],
            out_specs=[pl.BlockSpec((TILE, 2 * model), lambda r, p: (r, 0)), row, ANY, ANY],
            scratch_shapes=[
                pltpu.VMEM((8, model), F32),
                pltpu.VMEM((tokens, model), BF),
                pltpu.VMEM((2, grid_rows, share, model // 2), BF),
                pltpu.VMEM((VECTOR_ROWS, model // 2), BF),
                pltpu.SemaphoreType.DMA((2 * (grid_rows + 1),)),
            ],
        ),
        out_shape=[
            hbm((tokens, 2 * model), BF),
            hbm((tokens, model), F32),
            hbm(message, BF),
            hbm(message, BF),
        ],
        compiler_params=params(VMEM_MIB, 1),
        cost_estimate=cost(),
        name="norm_back",
    )(spot, d_hid, xhat, rstd, attn_a, attn_b, rden, w_out, rest, attn_t, sums_two, up_sums)


def diagonal(pair):
    first, second = (item.astype(BF) for item in pair)
    zero = jnp.zeros_like(first)
    return jnp.concatenate(
        [jnp.concatenate([first, zero], axis=1), jnp.concatenate([zero, second], axis=1)], axis=0
    )


def group_kernel(grid_rows, shared, spot_ref, *refs):
    place, parts, line = shared
    place = place + pl.program_id(0)
    line = line + 8 * pl.program_id(0)
    (
        qf_ref,
        kf_ref,
        vp_ref,
        dn_ref,
        cs_ref,
        segc_ref,
        segr_ref,
        qm_ref,
        km_ref,
        xt_ref,
    ) = refs[:10]
    dp_ref, keep_ref, send_ref, msg_scr, ext_scr, sems = refs[-6:]
    tokens = qf_ref.shape[0]
    model = xt_ref.shape[0]
    chunks = tokens // TILE
    low = low_half((TILE, LANE))
    ii = lax.broadcasted_iota(jnp.int32, (TILE, TILE), 0)
    jj = lax.broadcasted_iota(jnp.int32, (TILE, TILE), 1)
    kept = [[None] * 2 for _ in range(chunks)]
    for a in range(2):
        state = [None, None]
        for c in range(chunks - 1):
            rows = slice(c * TILE, (c + 1) * TILE)
            km = km_ref[rows, :].astype(BF)
            for n in range(2):
                cols = slice((2 * a + n) * LANE, (2 * a + n + 1) * LANE)
                grown = t_dot(kf_ref[rows, cols] * km, vp_ref[rows, cols])
                if c > 0:
                    grown = grown + state[n] * qm_ref[(c + 1) * TILE - 1 : (c + 1) * TILE, :]
                state[n] = grown
            kept[c + 1][a] = diagonal(state)
    back = [[None, None], [None, None]]
    sums = [jnp.zeros((1, LANE), F32) for _ in range(6)]
    for c in range(chunks - 1, -1, -1):
        rows = slice(c * TILE, (c + 1) * TILE)
        same = segc_ref[rows, :] == segr_ref[:, rows]
        lower = jnp.where(same & (jj <= ii), 1.0, 0.0)
        upper = jnp.where(same & (jj >= ii), 1.0, 0.0)
        qm = qm_ref[rows, :]
        km = km_ref[rows, :]
        cs = cs_ref[rows, :]
        scores = []
        for h in range(4):
            cols = slice(h * LANE, (h + 1) * LANE)
            q = qf_ref[rows, cols]
            k = kf_ref[rows, cols]
            v = vp_ref[rows, cols]
            g = dn_ref[rows, cols]
            scores.append(
                (
                    (dot_t(g, v) * lower).astype(BF),
                    None,
                    (dot_t(k, q) * upper).astype(BF),
                )
            )
        for a in range(2):
            wide = slice(2 * a * LANE, (2 * a + 2) * LANE)
            far_q, far_k, far_v = None, None, None
            if c > 0:
                far_q = dot_t(dn_ref[rows, wide], kept[c][a])
            if c < chunks - 1:
                held = diagonal(back[a])
                far_k = dot_t(vp_ref[rows, wide], held)
                far_v = dot(kf_ref[rows, wide], held)
            dqs, dks, dvs, q_on, k_on = [], [], [], [], []
            for n in range(2):
                h = 2 * a + n
                cols = slice(h * LANE, (h + 1) * LANE)
                part = slice(n * LANE, (n + 1) * LANE)
                q = qf_ref[rows, cols]
                k = kf_ref[rows, cols]
                g = dn_ref[rows, cols]
                d_scores, d_scores_t, scores_t = scores[h]
                dq = dot(d_scores, k)
                dk = t_dot(d_scores, q)
                dv = dot(scores_t, g)
                if c > 0:
                    dq = dq + qm * far_q[:, part]
                if c < chunks - 1:
                    dk = dk + km * far_k[:, part]
                    dv = dv + km * far_v[:, part]
                if c > 0:
                    grown = t_dot(q * qm.astype(BF), g)
                    if c < chunks - 1:
                        grown = grown + back[a][n] * km[0:1, :]
                    back[a][n] = grown
                dq = dq * cs
                dk = dk * cs
                dqs.append(dq + pltpu.roll(dq, HD, 1))
                dks.append(dk + pltpu.roll(dk, HD, 1))
                dvs.append(dv)
                q_abs = jnp.abs(q.astype(F32))
                k_abs = jnp.abs(k.astype(F32))
                q_on.append(q_abs + pltpu.roll(q_abs, HD, 1))
                k_on.append(k_abs + pltpu.roll(k_abs, HD, 1))
            dq = jnp.where(low, dqs[0], dqs[1]) * 0.125
            dk = jnp.where(low, dks[0], dks[1])
            dq = jnp.where(jnp.where(low, q_on[0], q_on[1]) > 0.0, dq, 0.0).astype(BF)
            dk = jnp.where(jnp.where(low, k_on[0], k_on[1]) > 0.0, dk, 0.0).astype(BF)
            dv = jnp.where(low, dvs[0], dvs[1]).astype(BF)
            for part, item in enumerate((dq, dk, dv)):
                unit = 2 * part + a
                dp_ref[rows, unit * LANE : (unit + 1) * LANE] = item
                sums[unit] = sums[unit] + jnp.sum(item.astype(F32), axis=0, keepdims=True)
    ext_scr[...] = jnp.zeros_like(ext_scr)
    for unit in range(6):
        lane = (unit % 3) * LANE
        ext_scr[unit // 3 : unit // 3 + 1, lane : lane + LANE] = sums[unit].astype(BF)
    message_out(
        spot_ref[0], spot_ref[1], grid_rows, xt_ref, dp_ref, msg_scr, ext_scr, keep_ref, send_ref,
        place, parts, line, sems,
    )


def group_back(spot, qf, kf, vp, dn, cs, segc, segr, qm, km, x_t, first, count, messages):
    model, tokens = x_t.shape
    grid_rows = lax.axis_size("mx")
    pick = pl.BlockSpec((tokens, 4 * LANE), lambda s, p: (0, first + s))
    lane = once((tokens, LANE))
    share = model // grid_rows
    if messages:
        shared = (1 + first, 3, 24 + 8 * first)
        shape = messages[0].shape
    else:
        shared = (0, 1, 0)
        shape = (grid_rows, share + 16, 3 * LANE)
    lines = 8 if messages else 16
    return pl.pallas_call(
        functools.partial(group_kernel, grid_rows, shared),
        grid_spec=pltpu.PrefetchScalarGridSpec(
            num_scalar_prefetch=1,
            grid=(count,),
            in_specs=[
                pick,
                pick,
                pick,
                pick,
                lane,
                once((tokens, 1)),
                once((1, tokens)),
                lane,
                lane,
                once((model, tokens)),
            ]
            + [ANY] * len(messages),
            out_specs=[
                pl.BlockSpec((None, tokens, 6 * LANE), lambda s, p: (s, 0, 0)),
                ANY,
                ANY,
            ],
            scratch_shapes=[
                pltpu.VMEM((2, grid_rows, share, 3 * LANE), BF),
                pltpu.VMEM((lines, 3 * LANE), BF),
                pltpu.SemaphoreType.DMA((2 * (grid_rows + 1),)),
            ],
        ),
        out_shape=[hbm((count, tokens, 6 * LANE), BF), hbm(shape, BF), hbm(shape, BF)],
        input_output_aliases={11: 1, 12: 2} if messages else {},
        compiler_params=params(VMEM_MIB, 1),
        cost_estimate=cost(),
        name="group%d" % first,
    )(spot, qf, kf, vp, dn, cs, segc, segr, qm, km, x_t, *messages)


def input_kernel(early_ref, late_ref, w_ref, dr_ref, out_ref):
    total = dr_ref[...]
    early = early_ref.shape[0]
    for g in range(GROUPS):
        grad = early_ref[g] if g < early else late_ref[g - early]
        total = total + dot_t(grad, w_ref[g])
    out_ref[...] = total.astype(BF)


def input_back(early, late, w_qkv, d_res):
    tokens, model = d_res.shape
    row = pl.BlockSpec((TILE, model), lambda r: (r, 0))
    return pl.pallas_call(
        input_kernel,
        grid=(tokens // TILE,),
        in_specs=[
            pl.BlockSpec((item.shape[0], TILE, 6 * LANE), lambda r: (0, r, 0))
            for item in (early, late)
        ]
        + [once(w_qkv.shape), row],
        out_specs=row,
        out_shape=hbm((tokens, model), BF),
        compiler_params=params(VMEM_MIB, 1),
        cost_estimate=cost(),
        name="input_back",
    )(early, late, w_qkv, d_res)


def settle(spot_ref, mine_ref, other_ref, target, split):
    side = spot_ref[2]
    rows = mine_ref.shape[0]
    for half, ref in ((side, mine_ref), (1 - side, other_ref)):
        if split == 1:
            target[pl.ds(aligned(half * rows, 8), rows), :] = ref[...].astype(F32)
        else:
            deep = lax.rem(spot_ref[3], 2)
            block = rows // 2
            for quarter, first in ((deep, 0), (1 - deep, block)):
                start = aligned(half * rows + quarter * block, 8)
                target[pl.ds(start, block), :] = ref[first : first + block, :].astype(F32)


def ffn_final_kernel(chunk_count, grid_rows, spot_ref, mine_ref, other_ref, up_ref, down_ref, scr):
    piece = mine_ref.shape[1]
    rows = mine_ref.shape[0] // chunk_count
    per = grid_rows // 2
    half = scr.shape[0] // 2
    share = half // per
    for c in range(chunk_count):
        part = pl.ds(c * rows, rows)
        settle(spot_ref, mine_ref.at[part, :], other_ref.at[part, :], scr, 1)
        down_ref[c * piece : (c + 1) * piece, :] = scr[0:half, :].T
        for n in range(per):
            lane = (n * chunk_count + c) * piece
            up_ref[:, lane : lane + piece] = scr[half + n * share : half + (n + 1) * share, :]


def ffn_final(spot, mine, other, chunk_count):
    grid_rows = lax.axis_size("mx")
    rows, piece = mine.shape
    rows = 2 * rows // chunk_count
    share = rows // 2 // (grid_rows // 2)
    up_shape = (share, piece * chunk_count * (grid_rows // 2))
    down_shape = (piece * chunk_count, rows // 2)
    return pl.pallas_call(
        functools.partial(ffn_final_kernel, chunk_count, grid_rows),
        grid_spec=pltpu.PrefetchScalarGridSpec(
            num_scalar_prefetch=1,
            grid=(1,),
            in_specs=[full(mine.shape), full(other.shape)],
            out_specs=[full(up_shape), full(down_shape)],
            scratch_shapes=[pltpu.VMEM((rows, piece), F32)],
        ),
        out_shape=[hbm(up_shape, F32), hbm(down_shape, F32)],
        compiler_params=params(VMEM_MIB, 1),
        cost_estimate=cost(),
        name="ffn_final",
    )(spot, mine, other)


def attn_final_kernel(grid_rows, chunk_count, spot_ref, *refs):
    halves = refs[:4]
    out_ref, qkv_ref = refs[4:6]
    one_scr, two_scr = refs[-2:]
    share = out_ref.shape[0]
    settle(spot_ref, halves[0], halves[1], one_scr, SPLITS[0])
    settle(spot_ref, halves[2], halves[3], two_scr, SPLITS[1])
    out_ref[...] = one_scr[0:share, :]
    groups = []
    for g in range(GROUPS):
        last = g == GROUPS - 1
        scr, start = (two_scr, 0) if last else (one_scr, (1 + g) * share)
        for t in range(3):
            lane = (3 * t + g) * LANE
            qkv_ref[:, lane : lane + LANE] = scr[start : start + share, t * LANE : (t + 1) * LANE]
        line = share if last else 3 * share + 24 + 8 * g
        groups.append(scr[line : line + 8, :])
    rows = one_scr[3 * share : 3 * share + 24, :]
    share_vectors(spot_ref, rows, groups, refs[6:-2], grid_rows, chunk_count)


def attn_final(spot, halves, sizes, model, chunk_count):
    grid_rows = lax.axis_size("mx")
    share, wide = model // grid_rows, model // 2
    return pl.pallas_call(
        functools.partial(attn_final_kernel, grid_rows, chunk_count),
        grid_spec=pltpu.PrefetchScalarGridSpec(
            num_scalar_prefetch=1,
            grid=(1,),
            in_specs=[full(item.shape) for item in halves],
            out_specs=[full((share, wide)), full((share, 3 * wide))]
            + [full((size,)) for size in sizes],
            scratch_shapes=[
                pltpu.VMEM((2 * halves[0].shape[0], wide), F32),
                pltpu.VMEM((2 * halves[2].shape[0], wide), F32),
            ],
        ),
        out_shape=[hbm((share, wide), F32), hbm((share, 3 * wide), F32)]
        + [jax.ShapeDtypeStruct((size,), F32) for size in sizes],
        compiler_params=params(VMEM_MIB, 1),
        cost_estimate=cost(),
        name="attn_final",
    )(spot, *halves)


def chunks_for(grid_rows, hidden_units):
    for count in (2, 3):
        if hidden_units % (grid_rows * count * LANE) == 0:
            return count
    return 1


def body(
    layer_input,
    w_qkv,
    b_qkv,
    w_out,
    b_out,
    ln1_gain,
    ln1_bias,
    w_up,
    b_up,
    w_down,
    b_down,
    ln2_gain,
    ln2_bias,
    segment_ids,
    doc_lengths,
    cotangent,
):
    tokens, model = layer_input.shape
    seqs, docs = doc_lengths.shape
    length = tokens // seqs
    grid_rows = lax.axis_size("mx")
    hidden_units = 2 * w_up.shape[1]
    chunk_count = chunks_for(grid_rows, hidden_units)
    row = lax.axis_index("mx")
    col = lax.axis_index("my")
    place = lax.axis_index("dp")
    spot = jnp.stack(
        [jnp.asarray(item, jnp.int32) for item in (row, col, place % 2, place // 2)]
    )
    places = piece_places()

    small = [b_qkv, b_out, ln1_gain, ln1_bias, b_up, b_down, ln2_gain, ln2_bias]
    sizes = [item.shape[0] for item in small]
    packed = pack_vectors(small)
    far_packed = fetch_far(packed)
    w_attn = jnp.concatenate([w_qkv, w_out], axis=1)
    far_attn, far_places = fetch_thirds(w_attn, packed)
    attn_places = third_places(far_places, w_attn.shape[0])
    n_attn, n_up, n_down = (fetch_near(item) for item in (w_attn, w_up, w_down))
    p_packed = fetch_rest(fetch_near(packed), far_packed)
    bias_qkv, bias_up, rest = spread_vectors(places, p_packed, sizes, chunk_count)

    segs = segment_ids.reshape(seqs, length)
    member = segs[:, :, None] == jnp.arange(docs, dtype=jnp.int32)[None, None, :]
    span = jnp.sum(jnp.where(member, doc_lengths[:, None, :], 0), axis=2)
    spots = jnp.arange(length, dtype=jnp.int32)[None, :]
    angle = 0.5 * math.pi * spots.astype(F32) / span.astype(F32)
    angle = angle.reshape(tokens, 1)
    lane = jnp.arange(LANE, dtype=jnp.int32)[None, :]
    cs = jnp.where(lane < HD, jnp.cos(angle), jnp.sin(angle))
    seg = (segs + docs * jnp.arange(seqs, dtype=jnp.int32)[:, None]).reshape(tokens)
    segc = seg.reshape(tokens, 1)
    segr = seg.reshape(1, tokens)
    tiles = seg.reshape(tokens // TILE, TILE)
    before = jnp.concatenate([jnp.full((1,), -1, jnp.int32), tiles[:-1, -1]])
    q_on = (tiles == before[:, None]).reshape(tokens, 1)
    k_on = (tiles == tiles[:, -1:]).reshape(tokens, 1)
    qm = jnp.broadcast_to(q_on.astype(F32), (tokens, LANE))
    km = jnp.broadcast_to(k_on.astype(F32), (tokens, LANE))
    x_t = layer_input.T

    cs, segc, qm, km = lax.optimization_barrier((cs, segc, qm, km))
    p_attn = fetch_rest(n_attn, far_attn, bias_qkv, cs, segc, qm, km)
    far_up = fetch_far(w_up, p_attn[-1])
    far_down = fetch_far(w_down, p_attn[-1])
    qf, kf, vp, attn_a, attn_b, rden, wp_qkv = attend(
        attn_places, layer_input, p_attn, bias_qkv, cs, segc, segr, qm, km
    )
    xhat, rstd, hidden, hidden_t, attn_t, wp_out = join(
        attn_places, attn_a, attn_b, layer_input, p_attn, rest
    )
    p_up = fetch_rest(n_up, far_up, hidden)
    act, slope, wp_up = up_project(places, hidden, p_up, bias_up, chunk_count)
    p_down = fetch_rest(n_down, far_down, act)
    block_out, sums_two, d_hid, up_sums, *messages = ffn(
        places, spot, act, slope, xhat, cotangent, p_down, rest, hidden_t, wp_up, chunk_count
    )
    keeps, sends = messages[:chunk_count], messages[chunk_count:]
    chains = [
        Chain(send, keep, [("halve", 1), ("mx", None)] if i % 2 else [("mx", None), ("halve", 1)])
        for i, (send, keep) in enumerate(zip(sends, keeps))
    ]

    def turn(after, *rounds):
        for picks in rounds:
            live = [chains[i] for i in picks]
            arrived = lax.optimization_barrier((after,) + tuple(item.terms[-1][0] for item in live))
            after = arrived[0]
            for item, array in zip(live, arrived[1:]):
                item.terms[-1] = (array, item.terms[-1][1])
                if item.step(after):
                    after = item.fresh
        return after

    d_hid = gate(d_hid, sends)
    first = chunk_count
    dn, d_res1, keep, send = norm_back(
        spot, d_hid, xhat, rstd, attn_a, attn_b, rden, wp_out, rest, attn_t, sums_two, up_sums
    )
    dn = gate(dn, [turn(d_res1, tuple(range(first)))])
    early, keep, send = group_back(
        spot, qf, kf, vp, dn, cs, segc, segr, qm, km, x_t, 0, GROUPS - 1, (keep, send)
    )
    chains.append(Chain(send, keep, plan(SPLITS[0])))
    dn = gate(dn, [send, turn(early, tuple(range(first)))])
    late, keep, send = group_back(
        spot, qf, kf, vp, dn, cs, segc, segr, qm, km, x_t, GROUPS - 1, 1, ()
    )
    chains.append(Chain(send, keep, plan(SPLITS[1])))
    arrived = lax.optimization_barrier(
        (late,) + tuple(chain.terms[-1][0] for chain in chains[:first])
    )
    for chain, array in zip(chains, arrived[1:]):
        chain.terms[-1] = (array, chain.terms[-1][1])
    ffn_part = jnp.concatenate([chain.part(0, chain.rows, 0) for chain in chains[:first]], axis=0)
    ffn_sum = deep_sum(ffn_part)
    chains = chains[first:]
    after = turn(ffn_part, *TURNS[0])
    early = gate(early, [send, after])
    input_grad = input_back(early, late, wp_qkv, d_res1)
    after = turn(input_grad, *TURNS[1])
    ffn_sum = gate(ffn_sum, [after])
    ffn_other = flip(ffn_sum, 1)
    turn(ffn_sum, *TURNS[2])
    attn_halves = [item for chain in chains for item in chain.finish()]
    g_up, g_down = ffn_final(spot, ffn_sum, ffn_other, chunk_count)
    g_out, g_qkv, g_bqkv, g_bout, g_gain1, g_bias1, g_bup, g_bdown, g_gain2, g_bias2 = attn_final(
        spot, attn_halves, sizes, model, chunk_count
    )
    return (
        block_out,
        input_grad,
        g_qkv,
        g_bqkv,
        g_out,
        g_bout,
        g_gain1,
        g_bias1,
        g_up,
        g_bup,
        g_down,
        g_bdown,
        g_gain2,
        g_bias2,
    )


def solution(mesh):
    return jax.shard_map(
        body,
        mesh=mesh,
        in_specs=(
            P(("dp", "mx", "my"), None),
            P("mx", "my"),
            P(("mx", "my")),
            P("mx", "my"),
            P(("mx", "my")),
            P(("mx", "my")),
            P(("mx", "my")),
            P("mx", "my"),
            P(("mx", "my")),
            P("mx", "my"),
            P(("mx", "my")),
            P(("mx", "my")),
            P(("mx", "my")),
            P(("dp", "mx", "my")),
            P(("dp", "mx", "my"), None),
            P(("dp", "mx", "my"), None),
        ),
        out_specs=(
            P(("dp", "mx", "my"), None),
            P(("dp", "mx", "my"), None),
            P("mx", "my"),
            P(("mx", "my")),
            P("mx", "my"),
            P(("mx", "my")),
            P(("mx", "my")),
            P(("mx", "my")),
            P("mx", "my"),
            P(("mx", "my")),
            P("mx", "my"),
            P(("mx", "my")),
            P(("mx", "my")),
            P(("mx", "my")),
        ),
        check_vma=False,
    )
```

```python
import functools
import math

import jax
import jax.numpy as jnp
from jax import lax
from jax.experimental import pallas as pl
from jax.experimental.pallas import tpu as pltpu
from jax.sharding import PartitionSpec as P

HD = 64
LANE = 128
TILE = 256
GROUPS = 3
MIB = 1 << 20
VMEM_MIB = 58
BLOCK = 768
VECTOR_ROWS = 64
SPLITS = (2, 1)
ORDER = "ABIABABFABABA"

BF = jnp.bfloat16
F32 = jnp.float32
norm_eps = 1e-05


def dot(left, right):
    return lax.dot_general(left, right, (((1,), (0,)), ((), ())), preferred_element_type=F32)


def dot_t(left, right):
    return lax.dot_general(left, right, (((1,), (1,)), ((), ())), preferred_element_type=F32)


def t_dot(left, right):
    return lax.dot_general(left, right, (((0,), (0,)), ((), ())), preferred_element_type=F32)


def low_half(shape):
    return lax.broadcasted_iota(jnp.int32, shape, 1) < HD


def params(limit, grid_dims=0):
    return pltpu.CompilerParams(
        dimension_semantics=("arbitrary",) * grid_dims if grid_dims else None,
        vmem_limit_bytes=limit * MIB,
    )


def cost(*_):
    return pl.CostEstimate(flops=1000, bytes_accessed=1000, transcendentals=0)


def hbm(shape, dtype):
    return pltpu.HBM(shape, dtype)


def vmem(shape, dtype):
    return jax.ShapeDtypeStruct(shape, dtype)


def full(shape):
    return pl.BlockSpec(shape, lambda *_: (0,) * len(shape))


def once(shape):
    return pl.BlockSpec(shape, lambda *_: (0,) * len(shape), pipeline_mode=pl.Buffered(1))


ANY = pl.BlockSpec(memory_space=pl.ANY)


def shift(value, axis, step):
    size = lax.axis_size(axis)
    return lax.ppermute(value, axis, [(i, (i + step) % size) for i in range(size)])


def pair_swap(value, axis):
    size = lax.axis_size(axis)
    return lax.ppermute(value, axis, [(i, i ^ 1) for i in range(size)])


def flip(value, bit):
    size = lax.axis_size("dp")
    return lax.ppermute(value, "dp", [(i, i ^ bit) for i in range(size)])


def gate(value, deps):
    return lax.optimization_barrier((value,) + tuple(deps))[0]


def fetch_near(block):
    return [block, pair_swap(block, "my")]


def fetch_far(block, *deps):
    grid_rows = lax.axis_size("mx")
    block = gate(block, deps) if deps else block
    return [shift(block, "mx", step) for step in range(1, grid_rows)]


def fetch_rest(near, far, *deps):
    if deps:
        far = list(lax.optimization_barrier(tuple(far) + deps)[: len(far)])
    return near + far + [pair_swap(item, "my") for item in far]


def fetch_thirds(block, *deps):
    rows = block.shape[0] // 3
    grid_rows = lax.axis_size("mx")
    side = lax.axis_index("dp") % 2
    own = lax.dynamic_slice_in_dim(block, side * rows, rows, axis=0)
    pieces, places = [], []
    for step in range(1, grid_rows):
        first = shift(gate(own, deps), "mx", step)
        row = (lax.axis_index("mx") - step + grid_rows) % grid_rows * 3
        pieces += [first, flip(first, 1), shift(block[2 * rows :], "mx", step)]
        places += [(row + side) * rows, (row + 1 - side) * rows, (row + 2) * rows]
    return pieces, places


def third_places(places, rows):
    row = lax.axis_index("mx") * rows
    col = lax.axis_index("my")
    flat = [row, col, row, 1 - col]
    for c in (col, 1 - col):
        for place in places:
            flat += [place, c]
    return jnp.stack([jnp.asarray(item, jnp.int32) for item in flat])


def piece_places():
    grid_rows = lax.axis_size("mx")
    row = lax.axis_index("mx")
    col = lax.axis_index("my")
    places = [(row, col), (row, 1 - col)]
    for c in (col, 1 - col):
        for step in range(1, grid_rows):
            places.append(((row - step + grid_rows) % grid_rows, c))
    return jnp.stack([jnp.asarray(item, jnp.int32) for place in places for item in place])


def pack_kernel(*refs):
    out_ref = refs[-1]
    for index, ref in enumerate(refs[:-1]):
        size = ref.shape[0]
        out_ref[index : index + 1, 0:size] = ref[...].astype(F32).reshape(1, size)


def pack_vectors(vectors):
    wide = max(item.shape[0] for item in vectors)
    return pl.pallas_call(
        pack_kernel,
        out_shape=jax.ShapeDtypeStruct((len(vectors), wide), F32),
        compiler_params=params(VMEM_MIB),
        name="pack",
    )(*vectors)


def spread_kernel(sizes, grid_rows, chunk_count, places_ref, *refs):
    owners = grid_rows * 2
    qkv_ref, up_ref, rest_ref = refs[owners : owners + 3]
    scr = refs[owners + 3]
    rest = 0
    for index, size in enumerate(sizes):
        total = size * owners
        whole = jnp.zeros((1, total), F32)
        for owner in range(owners):
            place = places_ref[2 * owner] * 2 + places_ref[2 * owner + 1]
            scr[...] = jnp.zeros_like(scr)
            scr[:, 0:size] = refs[owner][index : index + 1, 0:size]
            whole = whole + pltpu.roll(scr[:, 0:total], place * size, 1)
        if index == 0:
            for unit in range(6 * GROUPS):
                part, pair = unit // (2 * GROUPS), unit % (2 * GROUPS)
                lane = (pair % GROUPS) * 6 * LANE + (2 * part + pair // GROUPS) * LANE
                qkv_ref[:, lane : lane + LANE] = whole[:, unit * LANE : (unit + 1) * LANE]
        elif index == 4:
            piece = total // grid_rows // chunk_count
            for i in range(grid_rows):
                for c in range(chunk_count):
                    src, dst = (i * chunk_count + c) * piece, (c * grid_rows + i) * piece
                    up_ref[:, dst : dst + piece] = whole[:, src : src + piece]
        else:
            rest_ref[rest : rest + 1, :] = whole
            rest += 1
    rest_ref[rest:8, :] = jnp.zeros((8 - rest, rest_ref.shape[1]), F32)


def spread_vectors(places, packs, sizes, chunk_count):
    grid_rows = lax.axis_size("mx")
    owners = grid_rows * 2
    wide = max(sizes) * owners
    return pl.pallas_call(
        functools.partial(spread_kernel, sizes, grid_rows, chunk_count),
        grid_spec=pltpu.PrefetchScalarGridSpec(
            num_scalar_prefetch=1,
            grid=(1,),
            in_specs=[full(item.shape) for item in packs],
            out_specs=[
                full((1, sizes[0] * owners)),
                full((1, sizes[4] * owners)),
                full((8, sizes[1] * owners)),
            ],
            scratch_shapes=[pltpu.VMEM((1, wide), F32)],
        ),
        out_shape=[
            jax.ShapeDtypeStruct((1, sizes[0] * owners), F32),
            jax.ShapeDtypeStruct((1, sizes[4] * owners), F32),
            jax.ShapeDtypeStruct((8, sizes[1] * owners), F32),
        ],
        compiler_params=params(VMEM_MIB, 1),
        name="spread",
    )(places, *packs)


def share_vectors(spot_ref, rows, groups, outs, grid_rows, chunk_count):
    owners = grid_rows * 2
    owner = spot_ref[0] * 2 + spot_ref[1]

    def pair(index):
        return [rows[2 * index : 2 * index + 1, :], rows[2 * index + 1 : 2 * index + 2, :]]

    qkv = []
    for unit in range(6 * GROUPS):
        part, place = unit // (2 * GROUPS), unit % (2 * GROUPS)
        lane = 2 * part + place // GROUPS
        row = groups[place % GROUPS][lane // 3 : lane // 3 + 1, :]
        qkv.append(row[:, (lane % 3) * LANE : (lane % 3 + 1) * LANE])
    wide = rows.shape[1]
    piece = outs[4].shape[0] * owners // grid_rows // chunk_count
    ups = []
    for i in range(grid_rows):
        for c in range(chunk_count):
            for part in range(piece // LANE):
                place = (c * grid_rows + i) * piece + part * LANE
                row, lane = 12 + place // wide, place % wide
                ups.append(rows[row : row + 1, lane : lane + LANE])
    for items, out_ref in zip(
        (qkv, pair(0), pair(1), pair(2), ups, pair(3), pair(4), pair(5)), outs
    ):
        size = out_ref.shape[0]
        total = size * owners
        whole = jnp.concatenate(items, axis=1)
        turned = pltpu.roll(whole, lax.rem(total - owner * size, total), 1)
        out_ref[...] = turned[:, 0:size].reshape(size)


def gates(values, dep):
    return list(lax.optimization_barrier(tuple(values) + (dep,))[:-1])


class Chain:
    def __init__(self, send, keep, plan):
        self.plan = plan
        self.stage = 0
        self.fresh = send
        self.terms = [(keep, 0), (pair_swap(send, "my"), 0)]
        self.rows = send.shape[1]
        self.split = True

    def part(self, first, rows, owner=None):
        result = None
        for array, start in self.terms:
            if array.ndim == 3:
                count = array.shape[0] if owner is None else 1
                at = (0 if owner is None else owner, start + first, 0)
                item = lax.dynamic_slice(array, at, (count, rows, array.shape[2]))
                item = item if owner is None else item[0]
            else:
                item = lax.dynamic_slice(array, (start + first, 0), (rows, array.shape[1]))
            if len(self.terms) > 2:
                item = item.astype(F32)
            result = item if result is None else result + item
        return result.astype(BF)

    def step(self, after=None):
        if self.stage == len(self.plan):
            return False
        kind, bit = self.plan[self.stage]
        self.stage += 1
        array, start = self.terms[-1]
        if after is not None:
            self.terms[-1] = (gate(array, [after]), start)
        owner = None if self.split else 0
        if kind == "mx":
            parts = [self.part(0, self.rows, i) for i in range(1, lax.axis_size("mx"))]
            self.fresh = parts[0]
            self.terms += [(shift(part, "mx", i + 1), 0) for i, part in enumerate(parts)]
            self.split = False
        elif kind == "halve":
            side = lax.axis_index("dp") // bit % 2
            self.rows //= 2
            self.fresh = self.part((1 - side) * self.rows, self.rows, owner)
            self.terms = [(array, start + side * self.rows) for array, start in self.terms]
            self.terms.append((flip(self.fresh, bit), 0))
        else:
            if kind == "join" and self.plan[self.stage - 2][0] == "join":
                self.fresh = jnp.concatenate([array for array, _ in self.terms], axis=0)
            else:
                self.fresh = self.part(0, self.rows, owner)
            self.terms = [(self.fresh, 0), (flip(self.fresh, bit), 0)]
        return True

    def finish(self):
        while self.step():
            pass
        return [array for array, _ in self.terms]


def plan(split):
    bits = []
    while 1 << len(bits) < lax.axis_size("dp"):
        bits.append(1 << len(bits))
    return (
        [("mx", None)]
        + [("halve", bit) for bit in bits[:split]]
        + [("whole", bit) for bit in bits[split:]]
        + [("join", bit) for bit in bits[:split][::-1]]
    )


def deep_sum(value):
    size = lax.axis_size("dp")
    groups = [list(range(start, size, 2)) for start in range(2)]
    return lax.psum(value, "dp", axis_index_groups=groups)


def place_copies(places_ref, refs, sems, put):
    copies = []
    for index, ref in enumerate(refs):
        copies += put(places_ref[2 * index], places_ref[2 * index + 1], ref)
    return [
        pltpu.make_async_copy(src, dst, sems.at[index]) for index, (src, dst) in enumerate(copies)
    ]


def aligned(value, size):
    return pl.multiple_of(value, size)


def spread_lane(aux_ref, rows, lane):
    return jnp.broadcast_to(aux_ref[rows, lane : lane + 1], (TILE, LANE))


def turn_of(aux_ref, rows):
    return jnp.where(
        low_half((TILE, LANE)), spread_lane(aux_ref, rows, 3), spread_lane(aux_ref, rows, 4)
    )


def attend_kernel(pieces, width, places_ref, *refs):
    x_ref = refs[0]
    w_refs = refs[1 : 1 + pieces]
    bias_ref, aux_ref, segr_ref = refs[1 + pieces : 4 + pieces]
    qf_ref, kf_ref, vp_ref, out_a, out_b, rden_ref, wp_ref = refs[4 + pieces : 11 + pieces]
    w_scr, mask_scr, sems, out_sem = refs[11 + pieces :]
    step = pl.program_id(0)
    tokens = x_ref.shape[0]
    model = x_ref.shape[1]
    chunks = tokens // TILE
    units = width // LANE

    def put(row, col, ref):
        rows = ref.shape[0]
        start = aligned(row, 16)
        result = []
        for unit in range(units):
            where = col * units + unit
            part = where // (2 * GROUPS)
            pair = where % (2 * GROUPS)
            group = pair % GROUPS
            lane = aligned(part * (2 * LANE) + (pair // GROUPS) * LANE, LANE)
            result.append(
                (
                    ref.at[:, unit * LANE : (unit + 1) * LANE],
                    w_scr.at[group, pl.ds(start, rows), pl.ds(lane, LANE)],
                )
            )
        return result

    out_copy = pltpu.make_async_copy(w_scr, wp_ref, out_sem)

    @pl.when(step == 0)
    def _():
        copies = place_copies(places_ref, w_refs, sems, put)
        for copy in copies:
            copy.start()
        ii = lax.broadcasted_iota(jnp.int32, (TILE, TILE), 0)
        jj = lax.broadcasted_iota(jnp.int32, (TILE, TILE), 1)
        for c in range(chunks):
            rows = slice(c * TILE, (c + 1) * TILE)
            keep = (aux_ref[rows, 0:1] == segr_ref[:, rows]) & (jj <= ii)
            mask_scr[c] = jnp.where(keep, 1.0, 0.0)
        for copy in copies:
            copy.wait()
        out_copy.start()

    low = low_half((TILE, LANE))
    for r in range(chunks):
        rows = slice(r * TILE, (r + 1) * TILE)
        acc = dot(x_ref[rows, :], w_scr[step]) + bias_ref[...]
        cs = turn_of(aux_ref, rows)
        for a in range(2):
            q = jnp.maximum(acc[:, a * LANE : (a + 1) * LANE], 0.0) * 0.125
            k = jnp.maximum(acc[:, (2 + a) * LANE : (3 + a) * LANE], 0.0)
            v = acc[:, (4 + a) * LANE : (5 + a) * LANE]
            q_r = pltpu.roll(q, HD, 1)
            k_r = pltpu.roll(k, HD, 1)
            first = slice(2 * a * LANE, (2 * a + 1) * LANE)
            second = slice((2 * a + 1) * LANE, (2 * a + 2) * LANE)
            qf_ref[rows, first] = (jnp.where(low, q, q_r) * cs).astype(BF)
            qf_ref[rows, second] = (jnp.where(low, q_r, q) * cs).astype(BF)
            kf_ref[rows, first] = (jnp.where(low, k, k_r) * cs).astype(BF)
            kf_ref[rows, second] = (jnp.where(low, k_r, k) * cs).astype(BF)
            vp_ref[rows, first] = jnp.where(low, v, 1.0).astype(BF)
            vp_ref[rows, second] = jnp.where(low, 1.0, v).astype(BF)

    states = [None] * 4
    totals = [None] * 4
    for c in range(chunks):
        rows = slice(c * TILE, (c + 1) * TILE)
        mask = mask_scr[c]
        qm = spread_lane(aux_ref, rows, 1)
        km = spread_lane(aux_ref, rows, 2)
        for a in range(2):
            outs, denoms = [], []
            for h in (2 * a, 2 * a + 1):
                cols = slice(h * LANE, (h + 1) * LANE)
                q = qf_ref[rows, cols]
                k = kf_ref[rows, cols]
                v = vp_ref[rows, cols]
                scores = dot_t(q, k) * mask
                out = dot(scores.astype(BF), v)
                denom = scores[:, :LANE] + scores[:, LANE:]
                if c > 0:
                    out = out + qm * dot(q, states[h].astype(BF))
                    denom = denom + q.astype(F32) * (totals[h] * qm)
                outs.append(out)
                denoms.append(jnp.sum(denom, axis=1, keepdims=True))
                if c < chunks - 1:
                    held = k * km.astype(BF)
                    grown = t_dot(held, v)
                    total = jnp.sum(held.astype(F32), axis=0, keepdims=True)
                    if c > 0:
                        whole = qm[TILE - 1 : TILE, :]
                        grown = grown + states[h] * whole
                        total = total + totals[h] * whole
                    states[h] = grown
                    totals[h] = total
            numer = jnp.where(low, outs[0], outs[1])
            rden = 1.0 / jnp.maximum(jnp.where(low, denoms[0], denoms[1]), 1.0)
            rden_ref[rows, a * LANE : (a + 1) * LANE] = rden
            (out_a, out_b)[a][rows, :] = (numer * rden).astype(BF)

    @pl.when(step == GROUPS - 1)
    def _():
        out_copy.wait()


def attend(places, x, pieces, bias, aux, segr):
    tokens, model = x.shape
    count = len(pieces)
    width = 3 * model // 2
    group = 6 * LANE
    spec = pl.BlockSpec((tokens, 4 * LANE), lambda g, p: (0, g))
    half = pl.BlockSpec((tokens, LANE), lambda g, p: (0, g))
    return pl.pallas_call(
        functools.partial(attend_kernel, count, width),
        grid_spec=pltpu.PrefetchScalarGridSpec(
            num_scalar_prefetch=1,
            grid=(GROUPS,),
            in_specs=[once((tokens, model))]
            + [ANY] * count
            + [
                pl.BlockSpec((1, group), lambda g, p: (0, g)),
                once((tokens, LANE)),
                once((1, tokens)),
            ],
            out_specs=[
                spec,
                spec,
                spec,
                half,
                half,
                pl.BlockSpec((tokens, 2 * LANE), lambda g, p: (0, g)),
                ANY,
            ],
            scratch_shapes=[
                pltpu.VMEM((GROUPS, model, group), BF),
                pltpu.VMEM((tokens // TILE, TILE, TILE), F32),
                pltpu.SemaphoreType.DMA((count * (width // LANE),)),
                pltpu.SemaphoreType.DMA,
            ],
        ),
        out_shape=[hbm((tokens, GROUPS * 4 * LANE), BF)] * 3
        + [jax.ShapeDtypeStruct((tokens, GROUPS * LANE), BF)] * 2
        + [
            hbm((tokens, model), F32),
            hbm((GROUPS, model, group), BF),
        ],
        compiler_params=params(VMEM_MIB, 1),
        cost_estimate=cost(2 * tokens * model * 3 * model * 1.8, 20 * MIB),
        name="attend",
    )(places, x, *pieces, bias, aux, segr)


def rows_put(target, first):
    def put(row, col, ref):
        rows = ref.shape[0]
        width = ref.shape[1] - first
        start = row
        return [
            (
                ref.at[:, first : first + width],
                target.at[pl.ds(aligned(start, 16), rows), pl.ds(aligned(col * width, LANE), width)],
            )
        ]

    return put


def join_kernel(pieces, places_ref, *refs):
    a_ref, b_ref, x_ref = refs[:3]
    w_refs = refs[3 : 3 + pieces]
    rest_ref = refs[3 + pieces]
    xhat_ref, rstd_ref, hb_ref, ht_ref, at_ref, wo_ref = refs[4 + pieces : 10 + pieces]
    w_scr, sems, out_sem = refs[10 + pieces :]
    step = pl.program_id(0)
    out_copy = pltpu.make_async_copy(w_scr, wo_ref, out_sem)

    @pl.when(step == 0)
    def _():
        copies = place_copies(places_ref, w_refs, sems, rows_put(w_scr, 3 * w_scr.shape[1] // 2))
        for copy in copies:
            copy.start()
        for copy in copies:
            copy.wait()
        out_copy.start()

    attn = jnp.concatenate([a_ref[...], b_ref[...]], axis=1)
    resid = x_ref[...].astype(F32) + dot(attn, w_scr[...]) + rest_ref[0:1, :]
    center = resid - jnp.mean(resid, axis=1, keepdims=True)
    rstd = lax.rsqrt(jnp.mean(center * center, axis=1, keepdims=True) + norm_eps)
    xhat = center * rstd
    hidden = xhat * rest_ref[1:2, :] + rest_ref[2:3, :]
    xhat_ref[...] = xhat
    rstd_ref[...] = jnp.broadcast_to(rstd, rstd_ref.shape)
    hb_ref[...] = hidden.astype(BF)
    ht_ref[...] = hidden.T.astype(BF)
    at_ref[...] = attn.astype(F32).T.astype(BF)

    @pl.when(step == pl.num_programs(0) - 1)
    def _():
        out_copy.wait()


def join(places, attn_a, attn_b, x, pieces, rest):
    tokens, model = x.shape
    count = len(pieces)
    row = pl.BlockSpec((TILE, model), lambda r, p: (r, 0))
    half = pl.BlockSpec((TILE, model // 2), lambda r, p: (r, 0))
    flip = pl.BlockSpec((model, TILE), lambda r, p: (0, r))
    return pl.pallas_call(
        functools.partial(join_kernel, count),
        grid_spec=pltpu.PrefetchScalarGridSpec(
            num_scalar_prefetch=1,
            grid=(tokens // TILE,),
            in_specs=[half, half, row] + [ANY] * count + [full((8, model))],
            out_specs=[row, pl.BlockSpec((TILE, LANE), lambda r, p: (r, 0)), row, flip, flip, ANY],
            scratch_shapes=[
                pltpu.VMEM((model, model), BF),
                pltpu.SemaphoreType.DMA((count,)),
                pltpu.SemaphoreType.DMA,
            ],
        ),
        out_shape=[
            hbm((tokens, model), F32),
            hbm((tokens, LANE), F32),
            vmem((tokens, model), BF),
            hbm((model, tokens), BF),
            hbm((model, tokens), BF),
            hbm((model, model), BF),
        ],
        compiler_params=params(VMEM_MIB, 1),
        cost_estimate=cost(2 * tokens * model * model, 14 * MIB),
        name="join",
    )(places, attn_a, attn_b, x, *pieces, rest)


def up_kernel(pieces, chunk_count, places_ref, *refs):
    h_ref = refs[0]
    w_refs = refs[1 : 1 + pieces]
    bias_ref = refs[1 + pieces]
    act_ref, slope_ref, wp_ref = refs[2 + pieces : 5 + pieces]
    w_scr, sems, out_sem = refs[5 + pieces :]
    step = pl.program_id(0)
    wide = w_scr.shape[2]
    out_copy = pltpu.make_async_copy(w_scr, wp_ref, out_sem)

    @pl.when(step == 0)
    def _():
        width = w_refs[0].shape[1]
        piece = wide // lax.axis_size("mx")
        blocks = width // (piece * chunk_count)

        def put(row, col, ref):
            rows = ref.shape[0]
            start = row * rows
            result = []
            for i in range(blocks):
                for c in range(chunk_count):
                    lane = aligned((col * blocks + i) * piece, LANE)
                    src = (i * chunk_count + c) * piece
                    result.append(
                        (
                            ref.at[:, src : src + piece],
                            w_scr.at[c, pl.ds(aligned(start, 16), rows), pl.ds(lane, piece)],
                        )
                    )
            return result

        copies = place_copies(places_ref, w_refs, sems, put)
        for copy in copies:
            copy.start()
        for copy in copies:
            copy.wait()
        out_copy.start()

    tokens = h_ref.shape[0]
    for r in range(tokens // TILE):
        rows = slice(r * TILE, (r + 1) * TILE)
        up = dot(h_ref[rows, :], w_scr[step]) + bias_ref[...]
        phi = lax.erf(up * math.sqrt(0.5)) * 0.5 + 0.5
        bell = jnp.exp(up * up * -0.5) * (1.0 / math.sqrt(2.0 * math.pi))
        act_ref[rows, :] = (up * phi).astype(BF)
        slope_ref[rows, :] = (phi + up * bell).astype(BF)

    @pl.when(step == pl.num_programs(0) - 1)
    def _():
        out_copy.wait()


def up_project(places, hidden, pieces, bias, chunk_count):
    tokens, model = hidden.shape
    count = len(pieces)
    hidden_units = pieces[0].shape[1] * 2
    wide = hidden_units // chunk_count
    piece = wide // lax.axis_size("mx")
    per = pieces[0].shape[1] // piece
    col = pl.BlockSpec((tokens, wide), lambda c, p: (0, c))
    return pl.pallas_call(
        functools.partial(up_kernel, count, chunk_count),
        grid_spec=pltpu.PrefetchScalarGridSpec(
            num_scalar_prefetch=1,
            grid=(chunk_count,),
            in_specs=[full((tokens, model))]
            + [ANY] * count
            + [pl.BlockSpec((1, wide), lambda c, p: (0, c))],
            out_specs=[col, col, ANY],
            scratch_shapes=[
                pltpu.VMEM((chunk_count, model, wide), BF),
                pltpu.SemaphoreType.DMA((count * per,)),
                pltpu.SemaphoreType.DMA,
            ],
        ),
        out_shape=[hbm((tokens, hidden_units), BF)] * 2 + [hbm((chunk_count, model, wide), BF)],
        compiler_params=params(VMEM_MIB, 1),
        cost_estimate=cost(
            2 * tokens * model * hidden_units, 24 * MIB, 2 * tokens * hidden_units
        ),
        name="up",
    )(places, hidden, *pieces, bias)


def ffn_kernel(pieces, chunk_count, grid_rows, piece, tiles, places_ref, spot_ref, *refs):
    rowa_ref, xhat_ref, cot_ref = refs[:3]
    w_refs = refs[3 : 3 + pieces]
    rest_ref, ht_hbm, act_ref, slope_ref, wu_ref = refs[3 + pieces : 8 + pieces]
    outs = refs[8 + pieces :]
    out_ref, sums_ref, dh_ref, bsum_ref = outs[:4]
    keeps = outs[4 : 4 + chunk_count]
    sends = outs[4 + chunk_count : 4 + 2 * chunk_count]
    w_scr, dup_scr, dd_ref, ddt_ref, ht_ref, sems, ht_sem = outs[4 + 2 * chunk_count :]
    row, col = spot_ref[0], spot_ref[1]
    step = pl.program_id(0)
    wide = w_scr.shape[0] // chunk_count
    tokens, block = act_ref.shape
    model = dh_ref.shape[1]
    half, share = model // 2, model // grid_rows
    per = grid_rows // 2
    ht_copy = pltpu.make_async_copy(ht_hbm, ht_ref, ht_sem)

    @pl.when(step == 0)
    def _():
        def put(row, col, ref):
            width = ref.shape[1]
            lane = pl.ds(aligned(col * width, LANE), width)
            return [
                (
                    ref.at[c * piece : (c + 1) * piece, :],
                    w_scr.at[pl.ds(aligned(c * wide + row * piece, 16), piece), lane],
                )
                for c in range(chunk_count)
            ]

        copies = place_copies(places_ref, w_refs, sems, put)
        for copy in copies:
            copy.start()
        ht_copy.start()
        sums_ref[...] = jnp.zeros_like(sums_ref)
        for copy in copies:
            copy.wait()

    @pl.when(step < tiles)
    def _():
        rows = pl.ds(aligned(step * TILE, TILE), TILE)
        hidden = xhat_ref[...] * rest_ref[1:2, :] + rest_ref[2:3, :]
        resid = hidden + dot(rowa_ref[...], w_scr[...]) + rest_ref[3:4, :]
        center = resid - jnp.mean(resid, axis=1, keepdims=True)
        rstd = lax.rsqrt(jnp.mean(center * center, axis=1, keepdims=True) + norm_eps)
        xhat = center * rstd
        out_ref[...] = (xhat * rest_ref[4:5, :] + rest_ref[5:6, :]).astype(BF)
        g = cot_ref[...].astype(F32)
        e = g * rest_ref[4:5, :]
        d_res = rstd * (
            e
            - jnp.mean(e, axis=1, keepdims=True)
            - xhat * jnp.mean(e * xhat, axis=1, keepdims=True)
        )
        dh_ref[rows, :] = d_res
        d_down = d_res.astype(BF)
        dd_ref[rows, :] = d_down
        ddt_ref[:, rows] = d_down.T
        sums_ref[0:1, :] += jnp.sum(g * xhat, axis=0, keepdims=True)
        sums_ref[1:2, :] += jnp.sum(g, axis=0, keepdims=True)
        sums_ref[2:3, :] += jnp.sum(d_down.astype(F32), axis=0, keepdims=True)

    @pl.when(step == tiles)
    def _():
        ht_copy.wait()

    @pl.when(step >= tiles)
    def _():
        turn = step - tiles
        blocks = piece // block
        owner = lax.rem(turn // blocks, grid_rows)
        chunk = turn // (blocks * grid_rows)
        lane = pl.ds(aligned(lax.rem(turn, blocks) * block, LANE), block)
        wd = w_scr.at[pl.ds(aligned(turn * block, 16), block), :]
        total = jnp.zeros((1, block), F32)
        for r in range(tokens // TILE):
            rows = slice(r * TILE, (r + 1) * TILE)
            grad = (dot_t(dd_ref[rows, :], wd[...]) * slope_ref[rows, :].astype(F32)).astype(BF)
            dup_scr[rows, :] = grad
            total = total + jnp.sum(grad.astype(F32), axis=0, keepdims=True)
        bsum_ref[...] = jnp.broadcast_to(total, bsum_ref.shape)
        for r in range(tokens // TILE):
            rows = slice(r * TILE, (r + 1) * TILE)
            dh_ref[rows, :] += dot_t(dup_scr[rows, :], wu_ref[...])
        slot = lax.rem(owner - row + grid_rows, grid_rows)
        place = aligned(half + lax.rem(owner, per) * share, 16)
        down = dot(ddt_ref[pl.ds(aligned(col * half, 16), half), :], act_ref[...]).astype(BF)
        down_far = dot(
            ddt_ref[pl.ds(aligned((1 - col) * half, 16), half), :], act_ref[...]
        ).astype(BF)
        up = dot(ht_ref[...], dup_scr[...]).astype(BF)
        for c in range(chunk_count):

            @pl.when(chunk == c)
            def _():
                keeps[c][slot, 0:half, lane] = down
                sends[c][slot, 0:half, lane] = down_far
                for mine, target in ((True, keeps[c]), (False, sends[c])):

                    @pl.when((owner // per == col) == mine)
                    def _():
                        for i in range(grid_rows):
                            where = lax.rem(i - row + grid_rows, grid_rows)
                            target[where, pl.ds(place, share), lane] = up[
                                i * share : (i + 1) * share, :
                            ]


def ffn(places, spot, act, slope, xhat, cot, pieces, rest, hidden_t, w_up, chunk_count):
    tokens, hidden_units = act.shape
    model = xhat.shape[1]
    count = len(pieces)
    grid_rows = lax.axis_size("mx")
    wide = hidden_units // chunk_count
    piece = wide // grid_rows
    block = min(piece, BLOCK)
    message = (grid_rows, model, piece)
    tiles = tokens // TILE
    inner = wide // block

    def row(width):
        return pl.BlockSpec((TILE, width), lambda s, *_: (jnp.minimum(s, tiles - 1), 0))

    def late(s):
        return jnp.maximum(s - tiles, 0)

    pick = pl.BlockSpec((tokens, block), lambda s, *_: (0, late(s)))
    return pl.pallas_call(
        functools.partial(ffn_kernel, count, chunk_count, grid_rows, piece, tiles),
        grid_spec=pltpu.PrefetchScalarGridSpec(
            num_scalar_prefetch=2,
            grid=(tiles + hidden_units // block,),
            in_specs=[row(hidden_units), row(model), row(model)]
            + [ANY] * count
            + [
                once((8, model)),
                ANY,
                pick,
                pick,
                pl.BlockSpec(
                    (None, model, block), lambda s, *_: (late(s) // inner, 0, late(s) % inner)
                ),
            ],
            out_specs=[
                row(model),
                once((8, model)),
                once((tokens, model)),
                pl.BlockSpec((8, block), lambda s, *_: (0, late(s))),
            ]
            + [once(message)] * (2 * chunk_count),
            scratch_shapes=[
                pltpu.VMEM((hidden_units, model), BF),
                pltpu.VMEM((tokens, block), BF),
                pltpu.VMEM((tokens, model), BF),
                pltpu.VMEM((model, tokens), BF),
                pltpu.VMEM((model, tokens), BF),
                pltpu.SemaphoreType.DMA((count * chunk_count,)),
                pltpu.SemaphoreType.DMA,
            ],
        ),
        out_shape=[
            hbm((tokens, model), BF),
            vmem((8, model), F32),
            hbm((tokens, model), F32),
            vmem((8, hidden_units), F32),
        ]
        + [hbm(message, BF)] * (2 * chunk_count),
        compiler_params=params(VMEM_MIB, 1),
        cost_estimate=cost(),
        name="ffn",
    )(places, spot, act, xhat, cot, *pieces, rest, hidden_t, act, slope, w_up)


def norm_kernel(grid_rows, spot_ref, *refs):
    (
        dres_ref,
        xhat_ref,
        rstd_ref,
        a_ref,
        b_ref,
        rden_ref,
        wo_ref,
        gain_ref,
        at_ref,
        two_ref,
        up_ref,
    ) = refs[:11]
    dn_ref, dr_ref, keep_ref, send_ref, sums_ref, db_scr, msg_scr, ext_scr, sems = refs[11:20]
    at_hbm, (at_ref, at_sem) = at_ref, refs[20:]
    at_copy = pltpu.make_async_copy(at_hbm, at_ref, at_sem)
    step = pl.program_id(0)
    model = dres_ref.shape[1]

    @pl.when(step == 0)
    def _():
        sums_ref[...] = jnp.zeros_like(sums_ref)
        at_copy.start()

    d_hidden = dres_ref[...]
    xhat = xhat_ref[...]
    e = d_hidden * gain_ref[1:2, :]
    d_res = rstd_ref[:, 0:1] * (
        e
        - jnp.mean(e, axis=1, keepdims=True)
        - xhat * jnp.mean(e * xhat, axis=1, keepdims=True)
    )
    dr_ref[...] = d_res
    d_branch = d_res.astype(BF)
    db_scr[pl.ds(aligned(step * TILE, TILE), TILE), :] = d_branch
    sums_ref[0:1, :] += jnp.sum(d_hidden * xhat, axis=0, keepdims=True)
    sums_ref[1:2, :] += jnp.sum(d_hidden, axis=0, keepdims=True)
    sums_ref[2:3, :] += jnp.sum(d_branch.astype(F32), axis=0, keepdims=True)
    d_attn = dot_t(d_branch, wo_ref[...])
    low = low_half((TILE, LANE))
    li = lax.broadcasted_iota(jnp.int32, (LANE, LANE), 0) < HD
    lj = lax.broadcasted_iota(jnp.int32, (LANE, LANE), 1) < HD
    swap = jnp.where(li == lj, 0.0, 1.0 / HD).astype(BF)
    front = lax.broadcasted_iota(jnp.int32, (TILE, LANE), 1) % HD < HD // 2
    for pair in range(2 * GROUPS):
        a, g = pair // GROUPS, pair % GROUPS
        d_pair = d_attn[:, pair * LANE : (pair + 1) * LANE]
        attn = (a_ref, b_ref)[a][:, g * LANE : (g + 1) * LANE].astype(F32)
        rden = rden_ref[:, (2 * g + a) * LANE : (2 * g + a + 1) * LANE]
        prod = d_pair * attn
        high = prod.astype(BF)
        rest = (prod - high.astype(F32)).astype(BF)
        other = dot(high, swap) + dot(rest, swap)
        turned = pltpu.roll(rden, HD, 1)
        d_denom = jnp.where(turned < 1.0, -other * turned, 0.0)
        coarse = d_denom.astype(BF).astype(F32)
        d_denom = 2.0 * jnp.where(front, coarse, d_denom - coarse)
        d_numer = d_pair * rden
        place = (4 * g + 2 * a) * LANE
        dn_ref[:, place : place + LANE] = jnp.where(low, d_numer, d_denom).astype(BF)
        dn_ref[:, place + LANE : place + 2 * LANE] = jnp.where(low, d_denom, d_numer).astype(BF)

    @pl.when(step == pl.num_programs(0) - 1)
    def _():
        row, col = spot_ref[0], spot_ref[1]
        half = model // 2
        share = model // grid_rows
        at_copy.wait()
        wide = ext_scr.shape[1]
        ext_scr[...] = jnp.zeros_like(ext_scr)
        for index, (ref, line) in enumerate(
            ((sums_ref, 2), (sums_ref, 0), (sums_ref, 1), (two_ref, 2), (two_ref, 0), (two_ref, 1))
        ):
            for part in range(2):
                ext_scr[2 * index + part : 2 * index + part + 1, :] = ref[
                    line : line + 1, part * wide : (part + 1) * wide
                ].astype(BF)
        for part in range(up_ref.shape[1] // wide):
            ext_scr[12 + part : 13 + part, :] = up_ref[
                0:1, part * wide : (part + 1) * wide
            ].astype(BF)
        message_out(
            row, col, grid_rows, at_ref, db_scr, msg_scr, ext_scr, keep_ref, send_ref, 0, 3, 0, sems
        )


def message_out(
    row, col, grid_rows, left_ref, right_ref, msg_scr, ext_scr, keep_ref, send_ref, place, parts,
    line, sems,
):
    share, half = msg_scr.shape[2:]
    count = ext_scr.shape[0]
    copies = []
    for index, (side, target) in enumerate(((1 - col, send_ref), (col, keep_ref))):
        right = right_ref[:, pl.ds(aligned(side * half, LANE), half)]
        grad = dot(left_ref[...], right).astype(BF)
        for i in range(grid_rows):
            slot = lax.rem(i - row + grid_rows, grid_rows)
            msg_scr[index, slot] = grad[i * share : (i + 1) * share, :]
        pairs = [(msg_scr.at[index], target.at[:, pl.ds(aligned(place * share, 8), share), :])]
        lines = pl.ds(aligned(parts * share + line, 8), count)
        pairs += [(ext_scr, target.at[i, lines, :]) for i in range(grid_rows)]
        for src, dst in pairs:
            copy = pltpu.make_async_copy(src, dst, sems.at[len(copies)])
            copy.start()
            copies.append(copy)
    for copy in copies:
        copy.wait()


def norm_back(
    spot, d_hid, xhat, rstd, attn_a, attn_b, rden, w_out, rest, attn_t, sums_two, up_sums
):
    tokens, model = d_hid.shape
    grid_rows = lax.axis_size("mx")
    row = pl.BlockSpec((TILE, model), lambda r, p: (r, 0))
    half = pl.BlockSpec((TILE, model // 2), lambda r, p: (r, 0))
    share = model // grid_rows
    message = (grid_rows, 3 * share + VECTOR_ROWS, model // 2)
    return pl.pallas_call(
        functools.partial(norm_kernel, grid_rows),
        grid_spec=pltpu.PrefetchScalarGridSpec(
            num_scalar_prefetch=1,
            grid=(tokens // TILE,),
            in_specs=[
                row,
                row,
                pl.BlockSpec((TILE, LANE), lambda r, p: (r, 0)),
                half,
                half,
                row,
                once((model, model)),
                once((8, model)),
                ANY,
                once(sums_two.shape),
                once(up_sums.shape),
            ],
            out_specs=[pl.BlockSpec((TILE, 2 * model), lambda r, p: (r, 0)), row, ANY, ANY],
            scratch_shapes=[
                pltpu.VMEM((8, model), F32),
                pltpu.VMEM((tokens, model), BF),
                pltpu.VMEM((2, grid_rows, share, model // 2), BF),
                pltpu.VMEM((VECTOR_ROWS, model // 2), BF),
                pltpu.SemaphoreType.DMA((2 * (grid_rows + 1),)),
                pltpu.VMEM((model, tokens), BF),
                pltpu.SemaphoreType.DMA,
            ],
        ),
        out_shape=[
            hbm((tokens, 2 * model), BF),
            hbm((tokens, model), F32),
            hbm(message, BF),
            hbm(message, BF),
        ],
        compiler_params=params(VMEM_MIB, 1),
        cost_estimate=cost(),
        name="norm_back",
    )(spot, d_hid, xhat, rstd, attn_a, attn_b, rden, w_out, rest, attn_t, sums_two, up_sums)


def diagonal(pair):
    first, second = (item.astype(BF) for item in pair)
    zero = jnp.zeros_like(first)
    return jnp.concatenate(
        [jnp.concatenate([first, zero], axis=1), jnp.concatenate([zero, second], axis=1)], axis=0
    )


def group_kernel(grid_rows, shared, spot_ref, *refs):
    place, parts, line = shared
    qf_ref, kf_ref, vp_ref, dn_ref, aux_ref, segr_ref, xt_hbm = refs[:7]
    dp_ref, keep_ref, send_ref, msg_scr, ext_scr, xt_ref, sems, xt_sem = refs[-8:]
    step = pl.program_id(0)
    tokens = qf_ref.shape[0]
    chunks = tokens // TILE
    xt_copy = pltpu.make_async_copy(xt_hbm, xt_ref, xt_sem)

    @pl.when(step == 0)
    def _():
        xt_copy.start()

    low = low_half((TILE, LANE))
    ii = lax.broadcasted_iota(jnp.int32, (TILE, TILE), 0)
    jj = lax.broadcasted_iota(jnp.int32, (TILE, TILE), 1)
    kept = [[None] * 2 for _ in range(chunks)]
    for a in range(2):
        state = [None, None]
        for c in range(chunks - 1):
            rows = slice(c * TILE, (c + 1) * TILE)
            km = spread_lane(aux_ref, rows, 2).astype(BF)
            for n in range(2):
                cols = slice((2 * a + n) * LANE, (2 * a + n + 1) * LANE)
                grown = t_dot(kf_ref[rows, cols] * km, vp_ref[rows, cols])
                if c > 0:
                    grown = grown + state[n] * aux_ref[(c + 1) * TILE - 1 : (c + 1) * TILE, 1:2]
                state[n] = grown
            kept[c + 1][a] = diagonal(state)
    back = [[None, None], [None, None]]
    sums = [jnp.zeros((1, LANE), F32) for _ in range(6)]
    for c in range(chunks - 1, -1, -1):
        rows = slice(c * TILE, (c + 1) * TILE)
        same = aux_ref[rows, 0:1] == segr_ref[:, rows]
        lower = jnp.where(same & (jj <= ii), 1.0, 0.0)
        upper = jnp.where(same & (jj >= ii), 1.0, 0.0)
        qm = spread_lane(aux_ref, rows, 1)
        km = spread_lane(aux_ref, rows, 2)
        cs = turn_of(aux_ref, rows)
        scores = []
        for h in range(4):
            cols = slice(h * LANE, (h + 1) * LANE)
            q = qf_ref[rows, cols]
            k = kf_ref[rows, cols]
            v = vp_ref[rows, cols]
            g = dn_ref[rows, cols]
            scores.append(
                (
                    (dot_t(g, v) * lower).astype(BF),
                    None,
                    (dot_t(k, q) * upper).astype(BF),
                )
            )
        for a in range(2):
            wide = slice(2 * a * LANE, (2 * a + 2) * LANE)
            far_q, far_k, far_v = None, None, None
            if c > 0:
                far_q = dot_t(dn_ref[rows, wide], kept[c][a])
            if c < chunks - 1:
                held = diagonal(back[a])
                far_k = dot_t(vp_ref[rows, wide], held)
                far_v = dot(kf_ref[rows, wide], held)
            dqs, dks, dvs, q_on, k_on = [], [], [], [], []
            for n in range(2):
                h = 2 * a + n
                cols = slice(h * LANE, (h + 1) * LANE)
                part = slice(n * LANE, (n + 1) * LANE)
                q = qf_ref[rows, cols]
                k = kf_ref[rows, cols]
                g = dn_ref[rows, cols]
                d_scores, d_scores_t, scores_t = scores[h]
                dq = dot(d_scores, k)
                dk = t_dot(d_scores, q)
                dv = dot(scores_t, g)
                if c > 0:
                    dq = dq + qm * far_q[:, part]
                if c < chunks - 1:
                    dk = dk + km * far_k[:, part]
                    dv = dv + km * far_v[:, part]
                if c > 0:
                    grown = t_dot(q * qm.astype(BF), g)
                    if c < chunks - 1:
                        grown = grown + back[a][n] * km[0:1, :]
                    back[a][n] = grown
                dq = dq * cs
                dk = dk * cs
                dqs.append(dq + pltpu.roll(dq, HD, 1))
                dks.append(dk + pltpu.roll(dk, HD, 1))
                dvs.append(dv)
                q_abs = jnp.abs(q.astype(F32))
                k_abs = jnp.abs(k.astype(F32))
                q_on.append(q_abs + pltpu.roll(q_abs, HD, 1))
                k_on.append(k_abs + pltpu.roll(k_abs, HD, 1))
            dq = jnp.where(low, dqs[0], dqs[1]) * 0.125
            dk = jnp.where(low, dks[0], dks[1])
            dq = jnp.where(jnp.where(low, q_on[0], q_on[1]) > 0.0, dq, 0.0).astype(BF)
            dk = jnp.where(jnp.where(low, k_on[0], k_on[1]) > 0.0, dk, 0.0).astype(BF)
            dv = jnp.where(low, dvs[0], dvs[1]).astype(BF)
            for part, item in enumerate((dq, dk, dv)):
                unit = 2 * part + a
                dp_ref[rows, unit * LANE : (unit + 1) * LANE] = item
                sums[unit] = sums[unit] + jnp.sum(item.astype(F32), axis=0, keepdims=True)
    @pl.when(step == 0)
    def _():
        xt_copy.wait()

    ext_scr[...] = jnp.zeros_like(ext_scr)
    for unit in range(6):
        lane = (unit % 3) * LANE
        ext_scr[unit // 3 : unit // 3 + 1, lane : lane + LANE] = sums[unit].astype(BF)
    message_out(
        spot_ref[0], spot_ref[1], grid_rows, xt_ref, dp_ref, msg_scr, ext_scr, keep_ref, send_ref,
        place + step, parts, line + 8 * step, sems,
    )


def group_back(spot, qf, kf, vp, dn, aux, segr, x_t, first, count, messages):
    model, tokens = x_t.shape
    grid_rows = lax.axis_size("mx")
    pick = pl.BlockSpec((tokens, 4 * LANE), lambda s, p: (0, first + s))
    share = model // grid_rows
    if messages:
        shared = (1 + first, 3, 24 + 8 * first)
        shape = messages[0].shape
    else:
        shared = (0, 1, 0)
        shape = (grid_rows, share + 16, 3 * LANE)
    lines = 8 if messages else 16
    return pl.pallas_call(
        functools.partial(group_kernel, grid_rows, shared),
        grid_spec=pltpu.PrefetchScalarGridSpec(
            num_scalar_prefetch=1,
            grid=(count,),
            in_specs=[
                pick,
                pick,
                pick,
                pick,
                once((tokens, LANE)),
                once((1, tokens)),
                ANY,
            ]
            + [ANY] * len(messages),
            out_specs=[
                pl.BlockSpec((None, tokens, 6 * LANE), lambda s, p: (s, 0, 0)),
                ANY,
                ANY,
            ],
            scratch_shapes=[
                pltpu.VMEM((2, grid_rows, share, 3 * LANE), BF),
                pltpu.VMEM((lines, 3 * LANE), BF),
                pltpu.VMEM((model, tokens), BF),
                pltpu.SemaphoreType.DMA((2 * (grid_rows + 1),)),
                pltpu.SemaphoreType.DMA,
            ],
        ),
        out_shape=[hbm((count, tokens, 6 * LANE), BF), hbm(shape, BF), hbm(shape, BF)],
        input_output_aliases={8: 1, 9: 2} if messages else {},
        compiler_params=params(VMEM_MIB, 1),
        cost_estimate=cost(),
        name="group%d" % first,
    )(spot, qf, kf, vp, dn, aux, segr, x_t, *messages)


def input_kernel(early_ref, late_ref, w_ref, dr_hbm, out_ref, acc_ref, dr_ref, sem):
    step = pl.program_id(0)
    tokens = acc_ref.shape[0]
    dr_copy = pltpu.make_async_copy(dr_hbm, dr_ref, sem)

    @pl.when(step == 0)
    def _():
        dr_copy.start()
        for r in range(tokens // TILE):
            rows = slice(r * TILE, (r + 1) * TILE)
            acc_ref[rows, :] = dot_t(early_ref[rows, :], w_ref[...])

    @pl.when((step > 0) & (step < GROUPS - 1))
    def _():
        for r in range(tokens // TILE):
            rows = slice(r * TILE, (r + 1) * TILE)
            acc_ref[rows, :] += dot_t(early_ref[rows, :], w_ref[...])

    @pl.when(step == GROUPS - 1)
    def _():
        dr_copy.wait()
        for r in range(tokens // TILE):
            rows = slice(r * TILE, (r + 1) * TILE)
            total = acc_ref[rows, :] + dot_t(late_ref[rows, :], w_ref[...]) + dr_ref[rows, :]
            out_ref[rows, :] = total.astype(BF)


def input_back(early, late, w_qkv, d_res):
    tokens, model = d_res.shape
    last = GROUPS - 2
    return pl.pallas_call(
        input_kernel,
        grid=(GROUPS,),
        in_specs=[
            pl.BlockSpec((None, tokens, 6 * LANE), lambda s: (jnp.minimum(s, last), 0, 0)),
            pl.BlockSpec((None, tokens, 6 * LANE), lambda s: (0, 0, 0)),
            pl.BlockSpec((None, model, 6 * LANE), lambda s: (s, 0, 0)),
            ANY,
        ],
        out_specs=once((tokens, model)),
        out_shape=hbm((tokens, model), BF),
        scratch_shapes=[
            pltpu.VMEM((tokens, model), F32),
            pltpu.VMEM((tokens, model), F32),
            pltpu.SemaphoreType.DMA,
        ],
        compiler_params=params(VMEM_MIB, 1),
        cost_estimate=cost(),
        name="input_back",
    )(early, late, w_qkv, d_res)


def settle(spot_ref, mine_ref, other_ref, target, split):
    side = spot_ref[2]
    rows = mine_ref.shape[0]
    for half, ref in ((side, mine_ref), (1 - side, other_ref)):
        if split == 1:
            target[pl.ds(aligned(half * rows, 8), rows), :] = ref[...].astype(F32)
        else:
            deep = lax.rem(spot_ref[3], 2)
            block = rows // 2
            for quarter, first in ((deep, 0), (1 - deep, block)):
                start = aligned(half * rows + quarter * block, 8)
                target[pl.ds(start, block), :] = ref[first : first + block, :].astype(F32)


def ffn_final_kernel(chunk_count, grid_rows, spot_ref, mine_ref, other_ref, up_ref, down_ref, scr):
    piece = mine_ref.shape[1]
    rows = mine_ref.shape[0] // chunk_count
    per = grid_rows // 2
    half = scr.shape[0] // 2
    share = half // per
    for c in range(chunk_count):
        part = pl.ds(c * rows, rows)
        settle(spot_ref, mine_ref.at[part, :], other_ref.at[part, :], scr, 1)
        down_ref[c * piece : (c + 1) * piece, :] = scr[0:half, :].T
        for n in range(per):
            lane = (n * chunk_count + c) * piece
            up_ref[:, lane : lane + piece] = scr[half + n * share : half + (n + 1) * share, :]


def ffn_final(spot, mine, other, chunk_count):
    grid_rows = lax.axis_size("mx")
    rows, piece = mine.shape
    rows = 2 * rows // chunk_count
    share = rows // 2 // (grid_rows // 2)
    up_shape = (share, piece * chunk_count * (grid_rows // 2))
    down_shape = (piece * chunk_count, rows // 2)
    return pl.pallas_call(
        functools.partial(ffn_final_kernel, chunk_count, grid_rows),
        grid_spec=pltpu.PrefetchScalarGridSpec(
            num_scalar_prefetch=1,
            grid=(1,),
            in_specs=[full(mine.shape), full(other.shape)],
            out_specs=[full(up_shape), full(down_shape)],
            scratch_shapes=[pltpu.VMEM((rows, piece), F32)],
        ),
        out_shape=[hbm(up_shape, F32), hbm(down_shape, F32)],
        compiler_params=params(VMEM_MIB, 1),
        cost_estimate=cost(),
        name="ffn_final",
    )(spot, mine, other)


def attn_final_kernel(grid_rows, chunk_count, spot_ref, *refs):
    halves = refs[:4]
    out_ref, qkv_ref = refs[4:6]
    one_scr, two_scr = refs[-2:]
    share = out_ref.shape[0]
    settle(spot_ref, halves[0], halves[1], one_scr, SPLITS[0])
    settle(spot_ref, halves[2], halves[3], two_scr, SPLITS[1])
    out_ref[...] = one_scr[0:share, :]
    groups = []
    for g in range(GROUPS):
        last = g == GROUPS - 1
        scr, start = (two_scr, 0) if last else (one_scr, (1 + g) * share)
        for t in range(3):
            lane = (3 * t + g) * LANE
            qkv_ref[:, lane : lane + LANE] = scr[start : start + share, t * LANE : (t + 1) * LANE]
        line = share if last else 3 * share + 24 + 8 * g
        groups.append(scr[line : line + 8, :])
    rows = one_scr[3 * share : 3 * share + 24, :]
    share_vectors(spot_ref, rows, groups, refs[6:-2], grid_rows, chunk_count)


def attn_final(spot, halves, sizes, model, chunk_count):
    grid_rows = lax.axis_size("mx")
    share, wide = model // grid_rows, model // 2
    return pl.pallas_call(
        functools.partial(attn_final_kernel, grid_rows, chunk_count),
        grid_spec=pltpu.PrefetchScalarGridSpec(
            num_scalar_prefetch=1,
            grid=(1,),
            in_specs=[full(item.shape) for item in halves],
            out_specs=[full((share, wide)), full((share, 3 * wide))]
            + [full((size,)) for size in sizes],
            scratch_shapes=[
                pltpu.VMEM((2 * halves[0].shape[0], wide), F32),
                pltpu.VMEM((2 * halves[2].shape[0], wide), F32),
            ],
        ),
        out_shape=[hbm((share, wide), F32), hbm((share, 3 * wide), F32)]
        + [jax.ShapeDtypeStruct((size,), F32) for size in sizes],
        compiler_params=params(VMEM_MIB, 1),
        cost_estimate=cost(),
        name="attn_final",
    )(spot, *halves)


def chunks_for(grid_rows, hidden_units):
    for count in (2, 3):
        if hidden_units % (grid_rows * count * LANE) == 0:
            return count
    return 1


def body(
    layer_input,
    w_qkv,
    b_qkv,
    w_out,
    b_out,
    ln1_gain,
    ln1_bias,
    w_up,
    b_up,
    w_down,
    b_down,
    ln2_gain,
    ln2_bias,
    segment_ids,
    doc_lengths,
    cotangent,
):
    tokens, model = layer_input.shape
    seqs, docs = doc_lengths.shape
    length = tokens // seqs
    grid_rows = lax.axis_size("mx")
    hidden_units = 2 * w_up.shape[1]
    chunk_count = chunks_for(grid_rows, hidden_units)
    row = lax.axis_index("mx")
    col = lax.axis_index("my")
    place = lax.axis_index("dp")
    spot = jnp.stack(
        [jnp.asarray(item, jnp.int32) for item in (row, col, place % 2, place // 2)]
    )
    places = piece_places()

    small = [b_qkv, b_out, ln1_gain, ln1_bias, b_up, b_down, ln2_gain, ln2_bias]
    sizes = [item.shape[0] for item in small]
    packed = pack_vectors(small)
    far_packed = fetch_far(packed)
    w_attn = jnp.concatenate([w_qkv, w_out], axis=1)
    far_attn, far_places = fetch_thirds(w_attn, packed)
    attn_places = third_places(far_places, w_attn.shape[0])
    n_attn, n_up, n_down = (fetch_near(item) for item in (w_attn, w_up, w_down))
    p_packed = fetch_rest(fetch_near(packed), far_packed)
    bias_qkv, bias_up, rest = spread_vectors(places, p_packed, sizes, chunk_count)

    segs = segment_ids.reshape(seqs, length)
    member = segs[:, :, None] == jnp.arange(docs, dtype=jnp.int32)[None, None, :]
    span = jnp.sum(jnp.where(member, doc_lengths[:, None, :], 0), axis=2)
    spots = jnp.arange(length, dtype=jnp.int32)[None, :]
    angle = 0.5 * math.pi * spots.astype(F32) / span.astype(F32)
    angle = angle.reshape(tokens, 1)
    seg = (segs + docs * jnp.arange(seqs, dtype=jnp.int32)[:, None]).reshape(tokens).astype(F32)
    segr = seg.reshape(1, tokens)
    tiles = seg.reshape(tokens // TILE, TILE)
    before = jnp.concatenate([jnp.full((1,), -1.0, F32), tiles[:-1, -1]])
    q_on = (tiles == before[:, None]).reshape(tokens, 1)
    k_on = (tiles == tiles[:, -1:]).reshape(tokens, 1)
    lane = jnp.arange(LANE, dtype=jnp.int32)[None, :]
    aux = jnp.zeros((tokens, LANE), F32)
    for index, item in enumerate(
        (seg.reshape(tokens, 1), q_on, k_on, jnp.cos(angle), jnp.sin(angle))
    ):
        aux = jnp.where(lane == index, item.astype(F32), aux)
    x_t = layer_input.T

    aux = lax.optimization_barrier(aux)
    p_attn = fetch_rest(n_attn, far_attn, bias_qkv, aux)
    far_up = fetch_far(w_up, p_attn[-1])
    far_down = fetch_far(w_down, p_attn[-1])
    qf, kf, vp, attn_a, attn_b, rden, wp_qkv = attend(
        attn_places, layer_input, p_attn, bias_qkv, aux, segr
    )
    xhat, rstd, hidden, hidden_t, attn_t, wp_out = join(
        attn_places, attn_a, attn_b, layer_input, p_attn, rest
    )
    p_up = fetch_rest(n_up, far_up, hidden)
    act, slope, wp_up = up_project(places, hidden, p_up, bias_up, chunk_count)
    p_down = fetch_rest(n_down, far_down, act)
    block_out, sums_two, d_hid, up_sums, *messages = ffn(
        places, spot, act, slope, xhat, cotangent, p_down, rest, hidden_t, wp_up, chunk_count
    )
    keeps, sends = messages[:chunk_count], messages[chunk_count:]
    chains = [
        Chain(send, keep, [("halve", 1), ("mx", None)] if i % 2 else [("mx", None), ("halve", 1)])
        for i, (send, keep) in enumerate(zip(sends, keeps))
    ]

    def turn(after, *rounds):
        for picks in rounds:
            live = [chains[i] for i in picks]
            arrived = lax.optimization_barrier((after,) + tuple(item.terms[-1][0] for item in live))
            after = arrived[0]
            for item, array in zip(live, arrived[1:]):
                item.terms[-1] = (array, item.terms[-1][1])
                if item.step(after):
                    after = item.fresh
        return after

    d_hid = gate(d_hid, sends)
    first = chunk_count
    dn, d_res1, keep, send = norm_back(
        spot, d_hid, xhat, rstd, attn_a, attn_b, rden, wp_out, rest, attn_t, sums_two, up_sums
    )
    dn = gate(dn, [turn(d_res1, tuple(range(first)))])
    early, keep, send = group_back(
        spot, qf, kf, vp, dn, aux, segr, x_t, 0, GROUPS - 1, (keep, send)
    )
    chains.append(Chain(send, keep, plan(SPLITS[0])))
    dn = gate(dn, [send, turn(early, tuple(range(first)))])
    late, keep, send = group_back(
        spot, qf, kf, vp, dn, aux, segr, x_t, GROUPS - 1, 1, ()
    )
    chains.append(Chain(send, keep, plan(SPLITS[1])))
    arrived = lax.optimization_barrier(
        (late,) + tuple(chain.terms[-1][0] for chain in chains[:first])
    )
    for chain, array in zip(chains, arrived[1:]):
        chain.terms[-1] = (array, chain.terms[-1][1])
    ffn_part = jnp.concatenate([chain.part(0, chain.rows, 0) for chain in chains[:first]], axis=0)
    ffn_sum = deep_sum(ffn_part)
    chains = chains[first:]
    after = ffn_part
    for kind in ORDER:
        if kind == "I":
            early = gate(early, [send, after])
            after = input_grad = input_back(early, late, wp_qkv, d_res1)
        elif kind == "F":
            after = ffn_sum = gate(ffn_sum, [after])
            ffn_other = flip(ffn_sum, 1)
        else:
            after = turn(after, ("AB".index(kind),))
    attn_halves = [item for chain in chains for item in chain.finish()]
    g_up, g_down = ffn_final(spot, ffn_sum, ffn_other, chunk_count)
    g_out, g_qkv, g_bqkv, g_bout, g_gain1, g_bias1, g_bup, g_bdown, g_gain2, g_bias2 = attn_final(
        spot, attn_halves, sizes, model, chunk_count
    )
    return (
        block_out,
        input_grad,
        g_qkv,
        g_bqkv,
        g_out,
        g_bout,
        g_gain1,
        g_bias1,
        g_up,
        g_bup,
        g_down,
        g_bdown,
        g_gain2,
        g_bias2,
    )


def solution(mesh):
    return jax.shard_map(
        body,
        mesh=mesh,
        in_specs=(
            P(("dp", "mx", "my"), None),
            P("mx", "my"),
            P(("mx", "my")),
            P("mx", "my"),
            P(("mx", "my")),
            P(("mx", "my")),
            P(("mx", "my")),
            P("mx", "my"),
            P(("mx", "my")),
            P("mx", "my"),
            P(("mx", "my")),
            P(("mx", "my")),
            P(("mx", "my")),
            P(("dp", "mx", "my")),
            P(("dp", "mx", "my"), None),
            P(("dp", "mx", "my"), None),
        ),
        out_specs=(
            P(("dp", "mx", "my"), None),
            P(("dp", "mx", "my"), None),
            P("mx", "my"),
            P(("mx", "my")),
            P("mx", "my"),
            P(("mx", "my")),
            P(("mx", "my")),
            P(("mx", "my")),
            P("mx", "my"),
            P(("mx", "my")),
            P("mx", "my"),
            P(("mx", "my")),
            P(("mx", "my")),
            P(("mx", "my")),
        ),
        check_vma=False,
    )
```

```python
import functools
import math

import jax
import jax.numpy as jnp
from jax import lax
from jax.experimental import pallas as pl
from jax.experimental.pallas import tpu as pltpu
from jax.sharding import PartitionSpec as P

HD = 64
LANE = 128
TILE = 256
GROUPS = 3
MIB = 1 << 20
VMEM_MIB = 58
BLOCK = 256
VECTOR_ROWS = 64
SPLITS = (2, 1)
ORDER = "ABIABABFABABA"

BF = jnp.bfloat16
F32 = jnp.float32
norm_eps = 1e-05


def dot(left, right):
    return lax.dot_general(left, right, (((1,), (0,)), ((), ())), preferred_element_type=F32)


def dot_t(left, right):
    return lax.dot_general(left, right, (((1,), (1,)), ((), ())), preferred_element_type=F32)


def t_dot(left, right):
    return lax.dot_general(left, right, (((0,), (0,)), ((), ())), preferred_element_type=F32)


def low_half(shape):
    return lax.broadcasted_iota(jnp.int32, shape, 1) < HD


def params(limit, grid_dims=0):
    return pltpu.CompilerParams(
        dimension_semantics=("arbitrary",) * grid_dims if grid_dims else None,
        vmem_limit_bytes=limit * MIB,
    )


def cost(*_):
    return pl.CostEstimate(flops=1000, bytes_accessed=1000, transcendentals=0)


def hbm(shape, dtype):
    return pltpu.HBM(shape, dtype)


def vmem(shape, dtype):
    return jax.ShapeDtypeStruct(shape, dtype)


def full(shape):
    return pl.BlockSpec(shape, lambda *_: (0,) * len(shape))


def once(shape):
    return pl.BlockSpec(shape, lambda *_: (0,) * len(shape), pipeline_mode=pl.Buffered(1))


ANY = pl.BlockSpec(memory_space=pl.ANY)


def shift(value, axis, step):
    size = lax.axis_size(axis)
    return lax.ppermute(value, axis, [(i, (i + step) % size) for i in range(size)])


def pair_swap(value, axis):
    size = lax.axis_size(axis)
    return lax.ppermute(value, axis, [(i, i ^ 1) for i in range(size)])


def flip(value, bit):
    size = lax.axis_size("dp")
    return lax.ppermute(value, "dp", [(i, i ^ bit) for i in range(size)])


def gate(value, deps):
    return lax.optimization_barrier((value,) + tuple(deps))[0]


def fetch_near(block):
    return [block, pair_swap(block, "my")]


def fetch_far(block, *deps):
    grid_rows = lax.axis_size("mx")
    block = gate(block, deps) if deps else block
    return [shift(block, "mx", step) for step in range(1, grid_rows)]


def fetch_rest(near, far, *deps):
    if deps:
        far = list(lax.optimization_barrier(tuple(far) + deps)[: len(far)])
    return near + far + [pair_swap(item, "my") for item in far]


def fetch_thirds(block, *deps):
    rows = block.shape[0] // 3
    grid_rows = lax.axis_size("mx")
    side = lax.axis_index("dp") % 2
    own = lax.dynamic_slice_in_dim(block, side * rows, rows, axis=0)
    pieces, places = [], []
    for step in range(1, grid_rows):
        first = shift(gate(own, deps), "mx", step)
        row = (lax.axis_index("mx") - step + grid_rows) % grid_rows * 3
        pieces += [first, flip(first, 1), shift(block[2 * rows :], "mx", step)]
        places += [(row + side) * rows, (row + 1 - side) * rows, (row + 2) * rows]
    return pieces, places


def third_places(places, rows):
    row = lax.axis_index("mx") * rows
    col = lax.axis_index("my")
    flat = [row, col, row, 1 - col]
    for c in (col, 1 - col):
        for place in places:
            flat += [place, c]
    return jnp.stack([jnp.asarray(item, jnp.int32) for item in flat])


def piece_places():
    grid_rows = lax.axis_size("mx")
    row = lax.axis_index("mx")
    col = lax.axis_index("my")
    places = [(row, col), (row, 1 - col)]
    for c in (col, 1 - col):
        for step in range(1, grid_rows):
            places.append(((row - step + grid_rows) % grid_rows, c))
    return jnp.stack([jnp.asarray(item, jnp.int32) for place in places for item in place])


def pack_kernel(*refs):
    out_ref = refs[-1]
    for index, ref in enumerate(refs[:-1]):
        size = ref.shape[0]
        out_ref[index : index + 1, 0:size] = ref[...].astype(F32).reshape(1, size)


def pack_vectors(vectors):
    wide = max(item.shape[0] for item in vectors)
    return pl.pallas_call(
        pack_kernel,
        out_shape=jax.ShapeDtypeStruct((len(vectors), wide), F32),
        compiler_params=params(VMEM_MIB),
        name="pack",
    )(*vectors)


def spread_kernel(sizes, grid_rows, chunk_count, places_ref, *refs):
    owners = grid_rows * 2
    qkv_ref, up_ref, rest_ref = refs[owners : owners + 3]
    scr = refs[owners + 3]
    rest = 0
    for index, size in enumerate(sizes):
        total = size * owners
        whole = jnp.zeros((1, total), F32)
        for owner in range(owners):
            place = places_ref[2 * owner] * 2 + places_ref[2 * owner + 1]
            scr[...] = jnp.zeros_like(scr)
            scr[:, 0:size] = refs[owner][index : index + 1, 0:size]
            whole = whole + pltpu.roll(scr[:, 0:total], place * size, 1)
        if index == 0:
            for unit in range(6 * GROUPS):
                part, pair = unit // (2 * GROUPS), unit % (2 * GROUPS)
                lane = (pair % GROUPS) * 6 * LANE + (2 * part + pair // GROUPS) * LANE
                qkv_ref[:, lane : lane + LANE] = whole[:, unit * LANE : (unit + 1) * LANE]
        elif index == 4:
            piece = total // grid_rows // chunk_count
            for i in range(grid_rows):
                for c in range(chunk_count):
                    src, dst = (i * chunk_count + c) * piece, (c * grid_rows + i) * piece
                    up_ref[:, dst : dst + piece] = whole[:, src : src + piece]
        else:
            rest_ref[rest : rest + 1, :] = whole
            rest += 1
    rest_ref[rest:8, :] = jnp.zeros((8 - rest, rest_ref.shape[1]), F32)


def spread_vectors(places, packs, sizes, chunk_count):
    grid_rows = lax.axis_size("mx")
    owners = grid_rows * 2
    wide = max(sizes) * owners
    return pl.pallas_call(
        functools.partial(spread_kernel, sizes, grid_rows, chunk_count),
        grid_spec=pltpu.PrefetchScalarGridSpec(
            num_scalar_prefetch=1,
            grid=(1,),
            in_specs=[full(item.shape) for item in packs],
            out_specs=[
                full((1, sizes[0] * owners)),
                full((1, sizes[4] * owners)),
                full((8, sizes[1] * owners)),
            ],
            scratch_shapes=[pltpu.VMEM((1, wide), F32)],
        ),
        out_shape=[
            jax.ShapeDtypeStruct((1, sizes[0] * owners), F32),
            jax.ShapeDtypeStruct((1, sizes[4] * owners), F32),
            jax.ShapeDtypeStruct((8, sizes[1] * owners), F32),
        ],
        compiler_params=params(VMEM_MIB, 1),
        name="spread",
    )(places, *packs)


def share_vectors(spot_ref, rows, groups, outs, grid_rows, chunk_count):
    owners = grid_rows * 2
    owner = spot_ref[0] * 2 + spot_ref[1]

    def pair(index):
        return [rows[2 * index : 2 * index + 1, :], rows[2 * index + 1 : 2 * index + 2, :]]

    qkv = []
    for unit in range(6 * GROUPS):
        part, place = unit // (2 * GROUPS), unit % (2 * GROUPS)
        lane = 2 * part + place // GROUPS
        row = groups[place % GROUPS][lane // 3 : lane // 3 + 1, :]
        qkv.append(row[:, (lane % 3) * LANE : (lane % 3 + 1) * LANE])
    wide = rows.shape[1]
    piece = outs[4].shape[0] * owners // grid_rows // chunk_count
    ups = []
    for i in range(grid_rows):
        for c in range(chunk_count):
            for part in range(piece // LANE):
                place = (c * grid_rows + i) * piece + part * LANE
                row, lane = 12 + place // wide, place % wide
                ups.append(rows[row : row + 1, lane : lane + LANE])
    for items, out_ref in zip(
        (qkv, pair(0), pair(1), pair(2), ups, pair(3), pair(4), pair(5)), outs
    ):
        size = out_ref.shape[0]
        total = size * owners
        whole = jnp.concatenate(items, axis=1)
        turned = pltpu.roll(whole, lax.rem(total - owner * size, total), 1)
        out_ref[...] = turned[:, 0:size].reshape(size)


def gates(values, dep):
    return list(lax.optimization_barrier(tuple(values) + (dep,))[:-1])


class Chain:
    def __init__(self, send, keep, plan):
        self.plan = plan
        self.stage = 0
        self.fresh = send
        self.terms = [(keep, 0), (pair_swap(send, "my"), 0)]
        self.rows = send.shape[1]
        self.split = True

    def part(self, first, rows, owner=None):
        result = None
        for array, start in self.terms:
            if array.ndim == 3:
                count = array.shape[0] if owner is None else 1
                at = (0 if owner is None else owner, start + first, 0)
                item = lax.dynamic_slice(array, at, (count, rows, array.shape[2]))
                item = item if owner is None else item[0]
            else:
                item = lax.dynamic_slice(array, (start + first, 0), (rows, array.shape[1]))
            if len(self.terms) > 2:
                item = item.astype(F32)
            result = item if result is None else result + item
        return result.astype(BF)

    def step(self, after=None):
        if self.stage == len(self.plan):
            return False
        kind, bit = self.plan[self.stage]
        self.stage += 1
        array, start = self.terms[-1]
        if after is not None:
            self.terms[-1] = (gate(array, [after]), start)
        owner = None if self.split else 0
        if kind == "mx":
            parts = [self.part(0, self.rows, i) for i in range(1, lax.axis_size("mx"))]
            self.fresh = parts[0]
            self.terms += [(shift(part, "mx", i + 1), 0) for i, part in enumerate(parts)]
            self.split = False
        elif kind == "halve":
            side = lax.axis_index("dp") // bit % 2
            self.rows //= 2
            self.fresh = self.part((1 - side) * self.rows, self.rows, owner)
            self.terms = [(array, start + side * self.rows) for array, start in self.terms]
            self.terms.append((flip(self.fresh, bit), 0))
        else:
            if kind == "join" and self.plan[self.stage - 2][0] == "join":
                self.fresh = jnp.concatenate([array for array, _ in self.terms], axis=0)
            else:
                self.fresh = self.part(0, self.rows, owner)
            self.terms = [(self.fresh, 0), (flip(self.fresh, bit), 0)]
        return True

    def finish(self):
        while self.step():
            pass
        return [array for array, _ in self.terms]


def plan(split):
    bits = []
    while 1 << len(bits) < lax.axis_size("dp"):
        bits.append(1 << len(bits))
    return (
        [("mx", None)]
        + [("halve", bit) for bit in bits[:split]]
        + [("whole", bit) for bit in bits[split:]]
        + [("join", bit) for bit in bits[:split][::-1]]
    )


def deep_sum(value):
    size = lax.axis_size("dp")
    groups = [list(range(start, size, 2)) for start in range(2)]
    return lax.psum(value, "dp", axis_index_groups=groups)


def place_copies(places_ref, refs, sems, put):
    copies = []
    for index, ref in enumerate(refs):
        copies += put(places_ref[2 * index], places_ref[2 * index + 1], ref)
    return [
        pltpu.make_async_copy(src, dst, sems.at[index]) for index, (src, dst) in enumerate(copies)
    ]


def aligned(value, size):
    return pl.multiple_of(value, size)


def spread_lane(aux_ref, rows, lane):
    return jnp.broadcast_to(aux_ref[rows, lane : lane + 1], (TILE, LANE))


def turn_of(aux_ref, rows):
    return jnp.where(
        low_half((TILE, LANE)), spread_lane(aux_ref, rows, 3), spread_lane(aux_ref, rows, 4)
    )


def attend_kernel(pieces, width, places_ref, *refs):
    x_ref = refs[0]
    w_refs = refs[1 : 1 + pieces]
    bias_ref, aux_ref, segr_ref = refs[1 + pieces : 4 + pieces]
    qf_ref, kf_ref, vp_ref, out_a, out_b, rden_ref, wp_ref = refs[4 + pieces : 11 + pieces]
    w_scr, mask_scr, sems, out_sem = refs[11 + pieces :]
    step = pl.program_id(0)
    tokens = x_ref.shape[0]
    model = x_ref.shape[1]
    chunks = tokens // TILE
    units = width // LANE

    def put(row, col, ref):
        rows = ref.shape[0]
        start = aligned(row, 16)
        result = []
        for unit in range(units):
            where = col * units + unit
            part = where // (2 * GROUPS)
            pair = where % (2 * GROUPS)
            group = pair % GROUPS
            lane = aligned(part * (2 * LANE) + (pair // GROUPS) * LANE, LANE)
            result.append(
                (
                    ref.at[:, unit * LANE : (unit + 1) * LANE],
                    w_scr.at[group, pl.ds(start, rows), pl.ds(lane, LANE)],
                )
            )
        return result

    out_copy = pltpu.make_async_copy(w_scr, wp_ref, out_sem)

    @pl.when(step == 0)
    def _():
        copies = place_copies(places_ref, w_refs, sems, put)
        for copy in copies:
            copy.start()
        ii = lax.broadcasted_iota(jnp.int32, (TILE, TILE), 0)
        jj = lax.broadcasted_iota(jnp.int32, (TILE, TILE), 1)
        for c in range(chunks):
            rows = slice(c * TILE, (c + 1) * TILE)
            keep = (aux_ref[rows, 0:1] == segr_ref[:, rows]) & (jj <= ii)
            mask_scr[c] = jnp.where(keep, 1.0, 0.0)
        for copy in copies:
            copy.wait()
        out_copy.start()

    low = low_half((TILE, LANE))
    for r in range(chunks):
        rows = slice(r * TILE, (r + 1) * TILE)
        acc = dot(x_ref[rows, :], w_scr[step]) + bias_ref[...]
        cs = turn_of(aux_ref, rows)
        for a in range(2):
            q = jnp.maximum(acc[:, a * LANE : (a + 1) * LANE], 0.0) * 0.125
            k = jnp.maximum(acc[:, (2 + a) * LANE : (3 + a) * LANE], 0.0)
            v = acc[:, (4 + a) * LANE : (5 + a) * LANE]
            q_r = pltpu.roll(q, HD, 1)
            k_r = pltpu.roll(k, HD, 1)
            first = slice(2 * a * LANE, (2 * a + 1) * LANE)
            second = slice((2 * a + 1) * LANE, (2 * a + 2) * LANE)
            qf_ref[rows, first] = (jnp.where(low, q, q_r) * cs).astype(BF)
            qf_ref[rows, second] = (jnp.where(low, q_r, q) * cs).astype(BF)
            kf_ref[rows, first] = (jnp.where(low, k, k_r) * cs).astype(BF)
            kf_ref[rows, second] = (jnp.where(low, k_r, k) * cs).astype(BF)
            vp_ref[rows, first] = jnp.where(low, v, 1.0).astype(BF)
            vp_ref[rows, second] = jnp.where(low, 1.0, v).astype(BF)

    states = [None] * 4
    totals = [None] * 4
    for c in range(chunks):
        rows = slice(c * TILE, (c + 1) * TILE)
        mask = mask_scr[c]
        qm = spread_lane(aux_ref, rows, 1)
        km = spread_lane(aux_ref, rows, 2)
        for a in range(2):
            outs, denoms = [], []
            for h in (2 * a, 2 * a + 1):
                cols = slice(h * LANE, (h + 1) * LANE)
                q = qf_ref[rows, cols]
                k = kf_ref[rows, cols]
                v = vp_ref[rows, cols]
                scores = dot_t(q, k) * mask
                out = dot(scores.astype(BF), v)
                denom = scores[:, :LANE] + scores[:, LANE:]
                if c > 0:
                    out = out + qm * dot(q, states[h].astype(BF))
                    denom = denom + q.astype(F32) * (totals[h] * qm)
                outs.append(out)
                denoms.append(jnp.sum(denom, axis=1, keepdims=True))
                if c < chunks - 1:
                    held = k * km.astype(BF)
                    grown = t_dot(held, v)
                    total = jnp.sum(held.astype(F32), axis=0, keepdims=True)
                    if c > 0:
                        whole = qm[TILE - 1 : TILE, :]
                        grown = grown + states[h] * whole
                        total = total + totals[h] * whole
                    states[h] = grown
                    totals[h] = total
            numer = jnp.where(low, outs[0], outs[1])
            rden = 1.0 / jnp.maximum(jnp.where(low, denoms[0], denoms[1]), 1.0)
            rden_ref[rows, a * LANE : (a + 1) * LANE] = rden
            (out_a, out_b)[a][rows, :] = (numer * rden).astype(BF)

    @pl.when(step == GROUPS - 1)
    def _():
        out_copy.wait()


def attend(places, x, pieces, bias, aux, segr):
    tokens, model = x.shape
    count = len(pieces)
    width = 3 * model // 2
    group = 6 * LANE
    spec = pl.BlockSpec((tokens, 4 * LANE), lambda g, p: (0, g))
    half = pl.BlockSpec((tokens, LANE), lambda g, p: (0, g))
    return pl.pallas_call(
        functools.partial(attend_kernel, count, width),
        grid_spec=pltpu.PrefetchScalarGridSpec(
            num_scalar_prefetch=1,
            grid=(GROUPS,),
            in_specs=[once((tokens, model))]
            + [ANY] * count
            + [
                pl.BlockSpec((1, group), lambda g, p: (0, g)),
                once((tokens, LANE)),
                once((1, tokens)),
            ],
            out_specs=[
                spec,
                spec,
                spec,
                half,
                half,
                pl.BlockSpec((tokens, 2 * LANE), lambda g, p: (0, g)),
                ANY,
            ],
            scratch_shapes=[
                pltpu.VMEM((GROUPS, model, group), BF),
                pltpu.VMEM((tokens // TILE, TILE, TILE), F32),
                pltpu.SemaphoreType.DMA((count * (width // LANE),)),
                pltpu.SemaphoreType.DMA,
            ],
        ),
        out_shape=[hbm((tokens, GROUPS * 4 * LANE), BF)] * 3
        + [jax.ShapeDtypeStruct((tokens, GROUPS * LANE), BF)] * 2
        + [
            hbm((tokens, model), F32),
            hbm((GROUPS, model, group), BF),
        ],
        compiler_params=params(VMEM_MIB, 1),
        cost_estimate=cost(2 * tokens * model * 3 * model * 1.8, 20 * MIB),
        name="attend",
    )(places, x, *pieces, bias, aux, segr)


def rows_put(target, first):
    def put(row, col, ref):
        rows = ref.shape[0]
        width = ref.shape[1] - first
        start = row
        return [
            (
                ref.at[:, first : first + width],
                target.at[pl.ds(aligned(start, 16), rows), pl.ds(aligned(col * width, LANE), width)],
            )
        ]

    return put


def join_kernel(pieces, places_ref, *refs):
    a_ref, b_ref, x_ref = refs[:3]
    w_refs = refs[3 : 3 + pieces]
    rest_ref = refs[3 + pieces]
    xhat_ref, rstd_ref, hb_ref, ht_ref, at_ref, wo_ref = refs[4 + pieces : 10 + pieces]
    w_scr, sems, out_sem = refs[10 + pieces :]
    step = pl.program_id(0)
    out_copy = pltpu.make_async_copy(w_scr, wo_ref, out_sem)

    @pl.when(step == 0)
    def _():
        copies = place_copies(places_ref, w_refs, sems, rows_put(w_scr, 3 * w_scr.shape[1] // 2))
        for copy in copies:
            copy.start()
        for copy in copies:
            copy.wait()
        out_copy.start()

    attn = jnp.concatenate([a_ref[...], b_ref[...]], axis=1)
    resid = x_ref[...].astype(F32) + dot(attn, w_scr[...]) + rest_ref[0:1, :]
    center = resid - jnp.mean(resid, axis=1, keepdims=True)
    rstd = lax.rsqrt(jnp.mean(center * center, axis=1, keepdims=True) + norm_eps)
    xhat = center * rstd
    hidden = xhat * rest_ref[1:2, :] + rest_ref[2:3, :]
    xhat_ref[...] = xhat
    rstd_ref[...] = jnp.broadcast_to(rstd, rstd_ref.shape)
    hb_ref[...] = hidden.astype(BF)
    ht_ref[...] = hidden.T.astype(BF)
    at_ref[...] = attn.astype(F32).T.astype(BF)

    @pl.when(step == pl.num_programs(0) - 1)
    def _():
        out_copy.wait()


def join(places, attn_a, attn_b, x, pieces, rest):
    tokens, model = x.shape
    count = len(pieces)
    row = pl.BlockSpec((TILE, model), lambda r, p: (r, 0))
    half = pl.BlockSpec((TILE, model // 2), lambda r, p: (r, 0))
    flip = pl.BlockSpec((model, TILE), lambda r, p: (0, r))
    return pl.pallas_call(
        functools.partial(join_kernel, count),
        grid_spec=pltpu.PrefetchScalarGridSpec(
            num_scalar_prefetch=1,
            grid=(tokens // TILE,),
            in_specs=[half, half, row] + [ANY] * count + [full((8, model))],
            out_specs=[row, pl.BlockSpec((TILE, LANE), lambda r, p: (r, 0)), row, flip, flip, ANY],
            scratch_shapes=[
                pltpu.VMEM((model, model), BF),
                pltpu.SemaphoreType.DMA((count,)),
                pltpu.SemaphoreType.DMA,
            ],
        ),
        out_shape=[
            hbm((tokens, model), F32),
            hbm((tokens, LANE), F32),
            vmem((tokens, model), BF),
            hbm((model, tokens), BF),
            hbm((model, tokens), BF),
            hbm((model, model), BF),
        ],
        compiler_params=params(VMEM_MIB, 1),
        cost_estimate=cost(2 * tokens * model * model, 14 * MIB),
        name="join",
    )(places, attn_a, attn_b, x, *pieces, rest)


def up_kernel(pieces, chunk_count, places_ref, *refs):
    h_ref = refs[0]
    w_refs = refs[1 : 1 + pieces]
    bias_ref = refs[1 + pieces]
    act_ref, slope_ref, wp_ref = refs[2 + pieces : 5 + pieces]
    w_scr, sems, out_sem = refs[5 + pieces :]
    step = pl.program_id(0)
    wide = w_scr.shape[2]
    out_copy = pltpu.make_async_copy(w_scr, wp_ref, out_sem)

    @pl.when(step == 0)
    def _():
        width = w_refs[0].shape[1]
        piece = wide // lax.axis_size("mx")
        blocks = width // (piece * chunk_count)

        def put(row, col, ref):
            rows = ref.shape[0]
            start = row * rows
            result = []
            for i in range(blocks):
                for c in range(chunk_count):
                    lane = aligned((col * blocks + i) * piece, LANE)
                    src = (i * chunk_count + c) * piece
                    result.append(
                        (
                            ref.at[:, src : src + piece],
                            w_scr.at[c, pl.ds(aligned(start, 16), rows), pl.ds(lane, piece)],
                        )
                    )
            return result

        copies = place_copies(places_ref, w_refs, sems, put)
        for copy in copies:
            copy.start()
        for copy in copies:
            copy.wait()
        out_copy.start()

    tokens = h_ref.shape[0]
    for r in range(tokens // TILE):
        rows = slice(r * TILE, (r + 1) * TILE)
        up = dot(h_ref[rows, :], w_scr[step]) + bias_ref[...]
        phi = lax.erf(up * math.sqrt(0.5)) * 0.5 + 0.5
        bell = jnp.exp(up * up * -0.5) * (1.0 / math.sqrt(2.0 * math.pi))
        act_ref[rows, :] = (up * phi).astype(BF)
        slope_ref[rows, :] = (phi + up * bell).astype(BF)

    @pl.when(step == pl.num_programs(0) - 1)
    def _():
        out_copy.wait()


def up_project(places, hidden, pieces, bias, chunk_count):
    tokens, model = hidden.shape
    count = len(pieces)
    hidden_units = pieces[0].shape[1] * 2
    wide = hidden_units // chunk_count
    piece = wide // lax.axis_size("mx")
    per = pieces[0].shape[1] // piece
    col = pl.BlockSpec((tokens, wide), lambda c, p: (0, c))
    return pl.pallas_call(
        functools.partial(up_kernel, count, chunk_count),
        grid_spec=pltpu.PrefetchScalarGridSpec(
            num_scalar_prefetch=1,
            grid=(chunk_count,),
            in_specs=[full((tokens, model))]
            + [ANY] * count
            + [pl.BlockSpec((1, wide), lambda c, p: (0, c))],
            out_specs=[col, col, ANY],
            scratch_shapes=[
                pltpu.VMEM((chunk_count, model, wide), BF),
                pltpu.SemaphoreType.DMA((count * per,)),
                pltpu.SemaphoreType.DMA,
            ],
        ),
        out_shape=[hbm((tokens, hidden_units), BF)] * 2 + [hbm((chunk_count, model, wide), BF)],
        compiler_params=params(VMEM_MIB, 1),
        cost_estimate=cost(
            2 * tokens * model * hidden_units, 24 * MIB, 2 * tokens * hidden_units
        ),
        name="up",
    )(places, hidden, *pieces, bias)


def ffn_kernel(pieces, chunk_count, grid_rows, piece, tiles, places_ref, spot_ref, *refs):
    rowa_ref, xhat_ref, cot_ref = refs[:3]
    w_refs = refs[3 : 3 + pieces]
    rest_ref, ht_hbm, act_ref, slope_ref, wu_ref = refs[3 + pieces : 8 + pieces]
    outs = refs[8 + pieces :]
    out_ref, sums_ref, dh_ref, bsum_ref = outs[:4]
    keeps = outs[4 : 4 + chunk_count]
    sends = outs[4 + chunk_count : 4 + 2 * chunk_count]
    w_scr, dup_scr, dd_ref, ddt_ref, ht_ref, sems, ht_sem = outs[4 + 2 * chunk_count :]
    row, col = spot_ref[0], spot_ref[1]
    step = pl.program_id(0)
    wide = w_scr.shape[0] // chunk_count
    tokens, block = act_ref.shape
    model = dh_ref.shape[1]
    half, share = model // 2, model // grid_rows
    per = grid_rows // 2
    ht_copy = pltpu.make_async_copy(ht_hbm, ht_ref, ht_sem)

    @pl.when(step == 0)
    def _():
        def put(row, col, ref):
            width = ref.shape[1]
            lane = pl.ds(aligned(col * width, LANE), width)
            return [
                (
                    ref.at[c * piece : (c + 1) * piece, :],
                    w_scr.at[pl.ds(aligned(c * wide + row * piece, 16), piece), lane],
                )
                for c in range(chunk_count)
            ]

        copies = place_copies(places_ref, w_refs, sems, put)
        for copy in copies:
            copy.start()
        ht_copy.start()
        sums_ref[...] = jnp.zeros_like(sums_ref)
        for copy in copies:
            copy.wait()

    @pl.when(step < tiles)
    def _():
        rows = pl.ds(aligned(step * TILE, TILE), TILE)
        hidden = xhat_ref[...] * rest_ref[1:2, :] + rest_ref[2:3, :]
        resid = hidden + dot(rowa_ref[...], w_scr[...]) + rest_ref[3:4, :]
        center = resid - jnp.mean(resid, axis=1, keepdims=True)
        rstd = lax.rsqrt(jnp.mean(center * center, axis=1, keepdims=True) + norm_eps)
        xhat = center * rstd
        out_ref[...] = (xhat * rest_ref[4:5, :] + rest_ref[5:6, :]).astype(BF)
        g = cot_ref[...].astype(F32)
        e = g * rest_ref[4:5, :]
        d_res = rstd * (
            e
            - jnp.mean(e, axis=1, keepdims=True)
            - xhat * jnp.mean(e * xhat, axis=1, keepdims=True)
        )
        dh_ref[rows, :] = d_res
        d_down = d_res.astype(BF)
        dd_ref[rows, :] = d_down
        ddt_ref[:, rows] = d_down.T
        sums_ref[0:1, :] += jnp.sum(g * xhat, axis=0, keepdims=True)
        sums_ref[1:2, :] += jnp.sum(g, axis=0, keepdims=True)
        sums_ref[2:3, :] += jnp.sum(d_down.astype(F32), axis=0, keepdims=True)

    @pl.when(step == tiles)
    def _():
        ht_copy.wait()

    @pl.when(step >= tiles)
    def _():
        turn = step - tiles
        blocks = piece // block
        owner = lax.rem(turn // blocks, grid_rows)
        chunk = turn // (blocks * grid_rows)
        lane = pl.ds(aligned(lax.rem(turn, blocks) * block, LANE), block)
        wd = w_scr.at[pl.ds(aligned(turn * block, 16), block), :]
        total = jnp.zeros((1, block), F32)
        for r in range(tokens // TILE):
            rows = slice(r * TILE, (r + 1) * TILE)
            grad = (dot_t(dd_ref[rows, :], wd[...]) * slope_ref[rows, :].astype(F32)).astype(BF)
            dup_scr[rows, :] = grad
            total = total + jnp.sum(grad.astype(F32), axis=0, keepdims=True)
        bsum_ref[...] = jnp.broadcast_to(total, bsum_ref.shape)
        for r in range(tokens // TILE):
            rows = slice(r * TILE, (r + 1) * TILE)
            dh_ref[rows, :] += dot_t(dup_scr[rows, :], wu_ref[...])
        slot = lax.rem(owner - row + grid_rows, grid_rows)
        place = aligned(half + lax.rem(owner, per) * share, 16)
        down = dot(ddt_ref[pl.ds(aligned(col * half, 16), half), :], act_ref[...]).astype(BF)
        down_far = dot(
            ddt_ref[pl.ds(aligned((1 - col) * half, 16), half), :], act_ref[...]
        ).astype(BF)
        up = dot(ht_ref[...], dup_scr[...]).astype(BF)
        for c in range(chunk_count):

            @pl.when(chunk == c)
            def _():
                keeps[c][slot, 0:half, lane] = down
                sends[c][slot, 0:half, lane] = down_far
                for mine, target in ((True, keeps[c]), (False, sends[c])):

                    @pl.when((owner // per == col) == mine)
                    def _():
                        for i in range(grid_rows):
                            where = lax.rem(i - row + grid_rows, grid_rows)
                            target[where, pl.ds(place, share), lane] = up[
                                i * share : (i + 1) * share, :
                            ]


def ffn(places, spot, act, slope, xhat, cot, pieces, rest, hidden_t, w_up, chunk_count):
    tokens, hidden_units = act.shape
    model = xhat.shape[1]
    count = len(pieces)
    grid_rows = lax.axis_size("mx")
    wide = hidden_units // chunk_count
    piece = wide // grid_rows
    block = min(piece, BLOCK)
    message = (grid_rows, model, piece)
    tiles = tokens // TILE
    inner = wide // block

    def row(width):
        return pl.BlockSpec((TILE, width), lambda s, *_: (jnp.minimum(s, tiles - 1), 0))

    def late(s):
        return jnp.maximum(s - tiles, 0)

    pick = pl.BlockSpec((tokens, block), lambda s, *_: (0, late(s)))
    return pl.pallas_call(
        functools.partial(ffn_kernel, count, chunk_count, grid_rows, piece, tiles),
        grid_spec=pltpu.PrefetchScalarGridSpec(
            num_scalar_prefetch=2,
            grid=(tiles + hidden_units // block,),
            in_specs=[row(hidden_units), row(model), row(model)]
            + [ANY] * count
            + [
                once((8, model)),
                ANY,
                pick,
                pick,
                pl.BlockSpec(
                    (None, model, block), lambda s, *_: (late(s) // inner, 0, late(s) % inner)
                ),
            ],
            out_specs=[
                row(model),
                once((8, model)),
                once((tokens, model)),
                pl.BlockSpec((8, block), lambda s, *_: (0, late(s))),
            ]
            + [once(message)] * (2 * chunk_count),
            scratch_shapes=[
                pltpu.VMEM((hidden_units, model), BF),
                pltpu.VMEM((tokens, block), BF),
                pltpu.VMEM((tokens, model), BF),
                pltpu.VMEM((model, tokens), BF),
                pltpu.VMEM((model, tokens), BF),
                pltpu.SemaphoreType.DMA((count * chunk_count,)),
                pltpu.SemaphoreType.DMA,
            ],
        ),
        out_shape=[
            hbm((tokens, model), BF),
            vmem((8, model), F32),
            hbm((tokens, model), F32),
            vmem((8, hidden_units), F32),
        ]
        + [hbm(message, BF)] * (2 * chunk_count),
        compiler_params=params(VMEM_MIB, 1),
        cost_estimate=cost(),
        name="ffn",
    )(places, spot, act, xhat, cot, *pieces, rest, hidden_t, act, slope, w_up)


def norm_kernel(grid_rows, spot_ref, *refs):
    (
        dres_ref,
        xhat_ref,
        rstd_ref,
        a_ref,
        b_ref,
        rden_ref,
        wo_ref,
        gain_ref,
        at_ref,
        two_ref,
        up_ref,
    ) = refs[:11]
    dn_ref, dr_ref, keep_ref, send_ref, sums_ref, db_scr, msg_scr, ext_scr, sems = refs[11:20]
    at_hbm, (at_ref, at_sem) = at_ref, refs[20:]
    at_copy = pltpu.make_async_copy(at_hbm, at_ref, at_sem)
    step = pl.program_id(0)
    model = dres_ref.shape[1]

    @pl.when(step == 0)
    def _():
        sums_ref[...] = jnp.zeros_like(sums_ref)
        at_copy.start()

    d_hidden = dres_ref[...]
    xhat = xhat_ref[...]
    e = d_hidden * gain_ref[1:2, :]
    d_res = rstd_ref[:, 0:1] * (
        e
        - jnp.mean(e, axis=1, keepdims=True)
        - xhat * jnp.mean(e * xhat, axis=1, keepdims=True)
    )
    dr_ref[...] = d_res
    d_branch = d_res.astype(BF)
    db_scr[pl.ds(aligned(step * TILE, TILE), TILE), :] = d_branch
    sums_ref[0:1, :] += jnp.sum(d_hidden * xhat, axis=0, keepdims=True)
    sums_ref[1:2, :] += jnp.sum(d_hidden, axis=0, keepdims=True)
    sums_ref[2:3, :] += jnp.sum(d_branch.astype(F32), axis=0, keepdims=True)
    d_attn = dot_t(d_branch, wo_ref[...])
    low = low_half((TILE, LANE))
    li = lax.broadcasted_iota(jnp.int32, (LANE, LANE), 0) < HD
    lj = lax.broadcasted_iota(jnp.int32, (LANE, LANE), 1) < HD
    swap = jnp.where(li == lj, 0.0, 1.0 / HD).astype(BF)
    front = lax.broadcasted_iota(jnp.int32, (TILE, LANE), 1) % HD < HD // 2
    for pair in range(2 * GROUPS):
        a, g = pair // GROUPS, pair % GROUPS
        d_pair = d_attn[:, pair * LANE : (pair + 1) * LANE]
        attn = (a_ref, b_ref)[a][:, g * LANE : (g + 1) * LANE].astype(F32)
        rden = rden_ref[:, (2 * g + a) * LANE : (2 * g + a + 1) * LANE]
        prod = d_pair * attn
        high = prod.astype(BF)
        rest = (prod - high.astype(F32)).astype(BF)
        other = dot(high, swap) + dot(rest, swap)
        turned = pltpu.roll(rden, HD, 1)
        d_denom = jnp.where(turned < 1.0, -other * turned, 0.0)
        coarse = d_denom.astype(BF).astype(F32)
        d_denom = 2.0 * jnp.where(front, coarse, d_denom - coarse)
        d_numer = d_pair * rden
        place = (4 * g + 2 * a) * LANE
        dn_ref[:, place : place + LANE] = jnp.where(low, d_numer, d_denom).astype(BF)
        dn_ref[:, place + LANE : place + 2 * LANE] = jnp.where(low, d_denom, d_numer).astype(BF)

    @pl.when(step == pl.num_programs(0) - 1)
    def _():
        row, col = spot_ref[0], spot_ref[1]
        half = model // 2
        share = model // grid_rows
        at_copy.wait()
        wide = ext_scr.shape[1]
        ext_scr[...] = jnp.zeros_like(ext_scr)
        for index, (ref, line) in enumerate(
            ((sums_ref, 2), (sums_ref, 0), (sums_ref, 1), (two_ref, 2), (two_ref, 0), (two_ref, 1))
        ):
            for part in range(2):
                ext_scr[2 * index + part : 2 * index + part + 1, :] = ref[
                    line : line + 1, part * wide : (part + 1) * wide
                ].astype(BF)
        for part in range(up_ref.shape[1] // wide):
            ext_scr[12 + part : 13 + part, :] = up_ref[
                0:1, part * wide : (part + 1) * wide
            ].astype(BF)
        message_out(
            row, col, grid_rows, at_ref, db_scr, msg_scr, ext_scr, keep_ref, send_ref, 0, 3, 0, sems
        )


def message_out(
    row, col, grid_rows, left_ref, right_ref, msg_scr, ext_scr, keep_ref, send_ref, place, parts,
    line, sems,
):
    share, half = msg_scr.shape[2:]
    count = ext_scr.shape[0]
    copies = []
    for index, (side, target) in enumerate(((1 - col, send_ref), (col, keep_ref))):
        right = right_ref[:, pl.ds(aligned(side * half, LANE), half)]
        grad = dot(left_ref[...], right).astype(BF)
        for i in range(grid_rows):
            slot = lax.rem(i - row + grid_rows, grid_rows)
            msg_scr[index, slot] = grad[i * share : (i + 1) * share, :]
        pairs = [(msg_scr.at[index], target.at[:, pl.ds(aligned(place * share, 8), share), :])]
        lines = pl.ds(aligned(parts * share + line, 8), count)
        pairs += [(ext_scr, target.at[i, lines, :]) for i in range(grid_rows)]
        for src, dst in pairs:
            copy = pltpu.make_async_copy(src, dst, sems.at[len(copies)])
            copy.start()
            copies.append(copy)
    for copy in copies:
        copy.wait()


def norm_back(
    spot, d_hid, xhat, rstd, attn_a, attn_b, rden, w_out, rest, attn_t, sums_two, up_sums
):
    tokens, model = d_hid.shape
    grid_rows = lax.axis_size("mx")
    row = pl.BlockSpec((TILE, model), lambda r, p: (r, 0))
    half = pl.BlockSpec((TILE, model // 2), lambda r, p: (r, 0))
    share = model // grid_rows
    message = (grid_rows, 3 * share + VECTOR_ROWS, model // 2)
    return pl.pallas_call(
        functools.partial(norm_kernel, grid_rows),
        grid_spec=pltpu.PrefetchScalarGridSpec(
            num_scalar_prefetch=1,
            grid=(tokens // TILE,),
            in_specs=[
                row,
                row,
                pl.BlockSpec((TILE, LANE), lambda r, p: (r, 0)),
                half,
                half,
                row,
                once((model, model)),
                once((8, model)),
                ANY,
                once(sums_two.shape),
                once(up_sums.shape),
            ],
            out_specs=[pl.BlockSpec((TILE, 2 * model), lambda r, p: (r, 0)), row, ANY, ANY],
            scratch_shapes=[
                pltpu.VMEM((8, model), F32),
                pltpu.VMEM((tokens, model), BF),
                pltpu.VMEM((2, grid_rows, share, model // 2), BF),
                pltpu.VMEM((VECTOR_ROWS, model // 2), BF),
                pltpu.SemaphoreType.DMA((2 * (grid_rows + 1),)),
                pltpu.VMEM((model, tokens), BF),
                pltpu.SemaphoreType.DMA,
            ],
        ),
        out_shape=[
            hbm((tokens, 2 * model), BF),
            hbm((tokens, model), F32),
            hbm(message, BF),
            hbm(message, BF),
        ],
        compiler_params=params(VMEM_MIB, 1),
        cost_estimate=cost(),
        name="norm_back",
    )(spot, d_hid, xhat, rstd, attn_a, attn_b, rden, w_out, rest, attn_t, sums_two, up_sums)


def diagonal(pair):
    first, second = (item.astype(BF) for item in pair)
    zero = jnp.zeros_like(first)
    return jnp.concatenate(
        [jnp.concatenate([first, zero], axis=1), jnp.concatenate([zero, second], axis=1)], axis=0
    )


def group_kernel(grid_rows, shared, spot_ref, *refs):
    place, parts, line = shared
    qf_ref, kf_ref, vp_ref, dn_ref, aux_ref, segr_ref, xt_hbm = refs[:7]
    dp_ref, keep_ref, send_ref, msg_scr, ext_scr, xt_ref, sems, xt_sem = refs[-8:]
    step = pl.program_id(0)
    tokens = qf_ref.shape[0]
    chunks = tokens // TILE
    xt_copy = pltpu.make_async_copy(xt_hbm, xt_ref, xt_sem)

    @pl.when(step == 0)
    def _():
        xt_copy.start()

    low = low_half((TILE, LANE))
    ii = lax.broadcasted_iota(jnp.int32, (TILE, TILE), 0)
    jj = lax.broadcasted_iota(jnp.int32, (TILE, TILE), 1)
    kept = [[None] * 2 for _ in range(chunks)]
    for a in range(2):
        state = [None, None]
        for c in range(chunks - 1):
            rows = slice(c * TILE, (c + 1) * TILE)
            km = spread_lane(aux_ref, rows, 2).astype(BF)
            for n in range(2):
                cols = slice((2 * a + n) * LANE, (2 * a + n + 1) * LANE)
                grown = t_dot(kf_ref[rows, cols] * km, vp_ref[rows, cols])
                if c > 0:
                    grown = grown + state[n] * aux_ref[(c + 1) * TILE - 1 : (c + 1) * TILE, 1:2]
                state[n] = grown
            kept[c + 1][a] = diagonal(state)
    back = [[None, None], [None, None]]
    sums = [jnp.zeros((1, LANE), F32) for _ in range(6)]
    for c in range(chunks - 1, -1, -1):
        rows = slice(c * TILE, (c + 1) * TILE)
        same = aux_ref[rows, 0:1] == segr_ref[:, rows]
        lower = jnp.where(same & (jj <= ii), 1.0, 0.0)
        upper = jnp.where(same & (jj >= ii), 1.0, 0.0)
        qm = spread_lane(aux_ref, rows, 1)
        km = spread_lane(aux_ref, rows, 2)
        cs = turn_of(aux_ref, rows)
        scores = []
        for h in range(4):
            cols = slice(h * LANE, (h + 1) * LANE)
            q = qf_ref[rows, cols]
            k = kf_ref[rows, cols]
            v = vp_ref[rows, cols]
            g = dn_ref[rows, cols]
            scores.append(
                (
                    (dot_t(g, v) * lower).astype(BF),
                    None,
                    (dot_t(k, q) * upper).astype(BF),
                )
            )
        for a in range(2):
            wide = slice(2 * a * LANE, (2 * a + 2) * LANE)
            far_q, far_k, far_v = None, None, None
            if c > 0:
                far_q = dot_t(dn_ref[rows, wide], kept[c][a])
            if c < chunks - 1:
                held = diagonal(back[a])
                far_k = dot_t(vp_ref[rows, wide], held)
                far_v = dot(kf_ref[rows, wide], held)
            dqs, dks, dvs, q_on, k_on = [], [], [], [], []
            for n in range(2):
                h = 2 * a + n
                cols = slice(h * LANE, (h + 1) * LANE)
                part = slice(n * LANE, (n + 1) * LANE)
                q = qf_ref[rows, cols]
                k = kf_ref[rows, cols]
                g = dn_ref[rows, cols]
                d_scores, d_scores_t, scores_t = scores[h]
                dq = dot(d_scores, k)
                dk = t_dot(d_scores, q)
                dv = dot(scores_t, g)
                if c > 0:
                    dq = dq + qm * far_q[:, part]
                if c < chunks - 1:
                    dk = dk + km * far_k[:, part]
                    dv = dv + km * far_v[:, part]
                if c > 0:
                    grown = t_dot(q * qm.astype(BF), g)
                    if c < chunks - 1:
                        grown = grown + back[a][n] * km[0:1, :]
                    back[a][n] = grown
                dq = dq * cs
                dk = dk * cs
                dqs.append(dq + pltpu.roll(dq, HD, 1))
                dks.append(dk + pltpu.roll(dk, HD, 1))
                dvs.append(dv)
                q_abs = jnp.abs(q.astype(F32))
                k_abs = jnp.abs(k.astype(F32))
                q_on.append(q_abs + pltpu.roll(q_abs, HD, 1))
                k_on.append(k_abs + pltpu.roll(k_abs, HD, 1))
            dq = jnp.where(low, dqs[0], dqs[1]) * 0.125
            dk = jnp.where(low, dks[0], dks[1])
            dq = jnp.where(jnp.where(low, q_on[0], q_on[1]) > 0.0, dq, 0.0).astype(BF)
            dk = jnp.where(jnp.where(low, k_on[0], k_on[1]) > 0.0, dk, 0.0).astype(BF)
            dv = jnp.where(low, dvs[0], dvs[1]).astype(BF)
            for part, item in enumerate((dq, dk, dv)):
                unit = 2 * part + a
                dp_ref[rows, unit * LANE : (unit + 1) * LANE] = item
                sums[unit] = sums[unit] + jnp.sum(item.astype(F32), axis=0, keepdims=True)
    @pl.when(step == 0)
    def _():
        xt_copy.wait()

    ext_scr[...] = jnp.zeros_like(ext_scr)
    for unit in range(6):
        lane = (unit % 3) * LANE
        ext_scr[unit // 3 : unit // 3 + 1, lane : lane + LANE] = sums[unit].astype(BF)
    message_out(
        spot_ref[0], spot_ref[1], grid_rows, xt_ref, dp_ref, msg_scr, ext_scr, keep_ref, send_ref,
        place + step, parts, line + 8 * step, sems,
    )


def group_back(spot, qf, kf, vp, dn, aux, segr, x_t, first, count, messages):
    model, tokens = x_t.shape
    grid_rows = lax.axis_size("mx")
    pick = pl.BlockSpec((tokens, 4 * LANE), lambda s, p: (0, first + s))
    share = model // grid_rows
    if messages:
        shared = (1 + first, 3, 24 + 8 * first)
        shape = messages[0].shape
    else:
        shared = (0, 1, 0)
        shape = (grid_rows, share + 16, 3 * LANE)
    lines = 8 if messages else 16
    return pl.pallas_call(
        functools.partial(group_kernel, grid_rows, shared),
        grid_spec=pltpu.PrefetchScalarGridSpec(
            num_scalar_prefetch=1,
            grid=(count,),
            in_specs=[
                pick,
                pick,
                pick,
                pick,
                once((tokens, LANE)),
                once((1, tokens)),
                ANY,
            ]
            + [ANY] * len(messages),
            out_specs=[
                pl.BlockSpec((None, tokens, 6 * LANE), lambda s, p: (s, 0, 0)),
                ANY,
                ANY,
            ],
            scratch_shapes=[
                pltpu.VMEM((2, grid_rows, share, 3 * LANE), BF),
                pltpu.VMEM((lines, 3 * LANE), BF),
                pltpu.VMEM((model, tokens), BF),
                pltpu.SemaphoreType.DMA((2 * (grid_rows + 1),)),
                pltpu.SemaphoreType.DMA,
            ],
        ),
        out_shape=[hbm((count, tokens, 6 * LANE), BF), hbm(shape, BF), hbm(shape, BF)],
        input_output_aliases={8: 1, 9: 2} if messages else {},
        compiler_params=params(VMEM_MIB, 1),
        cost_estimate=cost(),
        name="group%d" % first,
    )(spot, qf, kf, vp, dn, aux, segr, x_t, *messages)


def input_kernel(early_ref, late_ref, w_ref, dr_hbm, out_ref, acc_ref, dr_ref, sem):
    step = pl.program_id(0)
    tokens = acc_ref.shape[0]
    dr_copy = pltpu.make_async_copy(dr_hbm, dr_ref, sem)

    @pl.when(step == 0)
    def _():
        dr_copy.start()
        for r in range(tokens // TILE):
            rows = slice(r * TILE, (r + 1) * TILE)
            acc_ref[rows, :] = dot_t(early_ref[rows, :], w_ref[...])

    @pl.when((step > 0) & (step < GROUPS - 1))
    def _():
        for r in range(tokens // TILE):
            rows = slice(r * TILE, (r + 1) * TILE)
            acc_ref[rows, :] += dot_t(early_ref[rows, :], w_ref[...])

    @pl.when(step == GROUPS - 1)
    def _():
        dr_copy.wait()
        for r in range(tokens // TILE):
            rows = slice(r * TILE, (r + 1) * TILE)
            total = acc_ref[rows, :] + dot_t(late_ref[rows, :], w_ref[...]) + dr_ref[rows, :]
            out_ref[rows, :] = total.astype(BF)


def input_back(early, late, w_qkv, d_res):
    tokens, model = d_res.shape
    last = GROUPS - 2
    return pl.pallas_call(
        input_kernel,
        grid=(GROUPS,),
        in_specs=[
            pl.BlockSpec((None, tokens, 6 * LANE), lambda s: (jnp.minimum(s, last), 0, 0)),
            pl.BlockSpec((None, tokens, 6 * LANE), lambda s: (0, 0, 0)),
            pl.BlockSpec((None, model, 6 * LANE), lambda s: (s, 0, 0)),
            ANY,
        ],
        out_specs=once((tokens, model)),
        out_shape=hbm((tokens, model), BF),
        scratch_shapes=[
            pltpu.VMEM((tokens, model), F32),
            pltpu.VMEM((tokens, model), F32),
            pltpu.SemaphoreType.DMA,
        ],
        compiler_params=params(VMEM_MIB, 1),
        cost_estimate=cost(),
        name="input_back",
    )(early, late, w_qkv, d_res)


def settle(spot_ref, mine_ref, other_ref, target, split):
    side = spot_ref[2]
    rows = mine_ref.shape[0]
    for half, ref in ((side, mine_ref), (1 - side, other_ref)):
        if split == 1:
            target[pl.ds(aligned(half * rows, 8), rows), :] = ref[...].astype(F32)
        else:
            deep = lax.rem(spot_ref[3], 2)
            block = rows // 2
            for quarter, first in ((deep, 0), (1 - deep, block)):
                start = aligned(half * rows + quarter * block, 8)
                target[pl.ds(start, block), :] = ref[first : first + block, :].astype(F32)


def ffn_final_kernel(chunk_count, grid_rows, spot_ref, mine_ref, other_ref, up_ref, down_ref, scr):
    piece = mine_ref.shape[1]
    rows = mine_ref.shape[0] // chunk_count
    per = grid_rows // 2
    half = scr.shape[0] // 2
    share = half // per
    for c in range(chunk_count):
        part = pl.ds(c * rows, rows)
        settle(spot_ref, mine_ref.at[part, :], other_ref.at[part, :], scr, 1)
        down_ref[c * piece : (c + 1) * piece, :] = scr[0:half, :].T
        for n in range(per):
            lane = (n * chunk_count + c) * piece
            up_ref[:, lane : lane + piece] = scr[half + n * share : half + (n + 1) * share, :]


def ffn_final(spot, mine, other, chunk_count):
    grid_rows = lax.axis_size("mx")
    rows, piece = mine.shape
    rows = 2 * rows // chunk_count
    share = rows // 2 // (grid_rows // 2)
    up_shape = (share, piece * chunk_count * (grid_rows // 2))
    down_shape = (piece * chunk_count, rows // 2)
    return pl.pallas_call(
        functools.partial(ffn_final_kernel, chunk_count, grid_rows),
        grid_spec=pltpu.PrefetchScalarGridSpec(
            num_scalar_prefetch=1,
            grid=(1,),
            in_specs=[full(mine.shape), full(other.shape)],
            out_specs=[full(up_shape), full(down_shape)],
            scratch_shapes=[pltpu.VMEM((rows, piece), F32)],
        ),
        out_shape=[hbm(up_shape, F32), hbm(down_shape, F32)],
        compiler_params=params(VMEM_MIB, 1),
        cost_estimate=cost(),
        name="ffn_final",
    )(spot, mine, other)


def attn_final_kernel(grid_rows, chunk_count, spot_ref, *refs):
    halves = refs[:4]
    out_ref, qkv_ref = refs[4:6]
    one_scr, two_scr = refs[-2:]
    share = out_ref.shape[0]
    settle(spot_ref, halves[0], halves[1], one_scr, SPLITS[0])
    settle(spot_ref, halves[2], halves[3], two_scr, SPLITS[1])
    out_ref[...] = one_scr[0:share, :]
    groups = []
    for g in range(GROUPS):
        last = g == GROUPS - 1
        scr, start = (two_scr, 0) if last else (one_scr, (1 + g) * share)
        for t in range(3):
            lane = (3 * t + g) * LANE
            qkv_ref[:, lane : lane + LANE] = scr[start : start + share, t * LANE : (t + 1) * LANE]
        line = share if last else 3 * share + 24 + 8 * g
        groups.append(scr[line : line + 8, :])
    rows = one_scr[3 * share : 3 * share + 24, :]
    share_vectors(spot_ref, rows, groups, refs[6:-2], grid_rows, chunk_count)


def attn_final(spot, halves, sizes, model, chunk_count):
    grid_rows = lax.axis_size("mx")
    share, wide = model // grid_rows, model // 2
    return pl.pallas_call(
        functools.partial(attn_final_kernel, grid_rows, chunk_count),
        grid_spec=pltpu.PrefetchScalarGridSpec(
            num_scalar_prefetch=1,
            grid=(1,),
            in_specs=[full(item.shape) for item in halves],
            out_specs=[full((share, wide)), full((share, 3 * wide))]
            + [full((size,)) for size in sizes],
            scratch_shapes=[
                pltpu.VMEM((2 * halves[0].shape[0], wide), F32),
                pltpu.VMEM((2 * halves[2].shape[0], wide), F32),
            ],
        ),
        out_shape=[hbm((share, wide), F32), hbm((share, 3 * wide), F32)]
        + [jax.ShapeDtypeStruct((size,), F32) for size in sizes],
        compiler_params=params(VMEM_MIB, 1),
        cost_estimate=cost(),
        name="attn_final",
    )(spot, *halves)


def chunks_for(grid_rows, hidden_units):
    for count in (2, 3):
        if hidden_units % (grid_rows * count * LANE) == 0:
            return count
    return 1


def body(
    layer_input,
    w_qkv,
    b_qkv,
    w_out,
    b_out,
    ln1_gain,
    ln1_bias,
    w_up,
    b_up,
    w_down,
    b_down,
    ln2_gain,
    ln2_bias,
    segment_ids,
    doc_lengths,
    cotangent,
):
    tokens, model = layer_input.shape
    seqs, docs = doc_lengths.shape
    length = tokens // seqs
    grid_rows = lax.axis_size("mx")
    hidden_units = 2 * w_up.shape[1]
    chunk_count = chunks_for(grid_rows, hidden_units)
    row = lax.axis_index("mx")
    col = lax.axis_index("my")
    place = lax.axis_index("dp")
    spot = jnp.stack(
        [jnp.asarray(item, jnp.int32) for item in (row, col, place % 2, place // 2)]
    )
    places = piece_places()

    small = [b_qkv, b_out, ln1_gain, ln1_bias, b_up, b_down, ln2_gain, ln2_bias]
    sizes = [item.shape[0] for item in small]
    packed = pack_vectors(small)
    far_packed = fetch_far(packed)
    w_attn = jnp.concatenate([w_qkv, w_out], axis=1)
    far_attn, far_places = fetch_thirds(w_attn, packed)
    attn_places = third_places(far_places, w_attn.shape[0])
    n_attn, n_up, n_down = (fetch_near(item) for item in (w_attn, w_up, w_down))
    p_packed = fetch_rest(fetch_near(packed), far_packed)
    bias_qkv, bias_up, rest = spread_vectors(places, p_packed, sizes, chunk_count)

    segs = segment_ids.reshape(seqs, length)
    member = segs[:, :, None] == jnp.arange(docs, dtype=jnp.int32)[None, None, :]
    span = jnp.sum(jnp.where(member, doc_lengths[:, None, :], 0), axis=2)
    spots = jnp.arange(length, dtype=jnp.int32)[None, :]
    angle = 0.5 * math.pi * spots.astype(F32) / span.astype(F32)
    angle = angle.reshape(tokens, 1)
    seg = (segs + docs * jnp.arange(seqs, dtype=jnp.int32)[:, None]).reshape(tokens).astype(F32)
    segr = seg.reshape(1, tokens)
    tiles = seg.reshape(tokens // TILE, TILE)
    before = jnp.concatenate([jnp.full((1,), -1.0, F32), tiles[:-1, -1]])
    q_on = (tiles == before[:, None]).reshape(tokens, 1)
    k_on = (tiles == tiles[:, -1:]).reshape(tokens, 1)
    lane = jnp.arange(LANE, dtype=jnp.int32)[None, :]
    aux = jnp.zeros((tokens, LANE), F32)
    for index, item in enumerate(
        (seg.reshape(tokens, 1), q_on, k_on, jnp.cos(angle), jnp.sin(angle))
    ):
        aux = jnp.where(lane == index, item.astype(F32), aux)
    x_t = layer_input.T

    aux = lax.optimization_barrier(aux)
    p_attn = fetch_rest(n_attn, far_attn, bias_qkv, aux)
    far_up = fetch_far(w_up, p_attn[-1])
    far_down = fetch_far(w_down, p_attn[-1])
    qf, kf, vp, attn_a, attn_b, rden, wp_qkv = attend(
        attn_places, layer_input, p_attn, bias_qkv, aux, segr
    )
    xhat, rstd, hidden, hidden_t, attn_t, wp_out = join(
        attn_places, attn_a, attn_b, layer_input, p_attn, rest
    )
    p_up = fetch_rest(n_up, far_up, hidden)
    act, slope, wp_up = up_project(places, hidden, p_up, bias_up, chunk_count)
    p_down = fetch_rest(n_down, far_down, act)
    block_out, sums_two, d_hid, up_sums, *messages = ffn(
        places, spot, act, slope, xhat, cotangent, p_down, rest, hidden_t, wp_up, chunk_count
    )
    keeps, sends = messages[:chunk_count], messages[chunk_count:]
    chains = [
        Chain(send, keep, [("halve", 1), ("mx", None)] if i % 2 else [("mx", None), ("halve", 1)])
        for i, (send, keep) in enumerate(zip(sends, keeps))
    ]

    def turn(after, *rounds):
        for picks in rounds:
            live = [chains[i] for i in picks]
            arrived = lax.optimization_barrier((after,) + tuple(item.terms[-1][0] for item in live))
            after = arrived[0]
            for item, array in zip(live, arrived[1:]):
                item.terms[-1] = (array, item.terms[-1][1])
                if item.step(after):
                    after = item.fresh
        return after

    d_hid = gate(d_hid, sends)
    first = chunk_count
    dn, d_res1, keep, send = norm_back(
        spot, d_hid, xhat, rstd, attn_a, attn_b, rden, wp_out, rest, attn_t, sums_two, up_sums
    )
    dn = gate(dn, [turn(d_res1, tuple(range(first)))])
    early, keep, send = group_back(
        spot, qf, kf, vp, dn, aux, segr, x_t, 0, GROUPS - 1, (keep, send)
    )
    chains.append(Chain(send, keep, plan(SPLITS[0])))
    dn = gate(dn, [send, turn(early, tuple(range(first)))])
    late, keep, send = group_back(
        spot, qf, kf, vp, dn, aux, segr, x_t, GROUPS - 1, 1, ()
    )
    chains.append(Chain(send, keep, plan(SPLITS[1])))
    arrived = lax.optimization_barrier(
        (late,) + tuple(chain.terms[-1][0] for chain in chains[:first])
    )
    for chain, array in zip(chains, arrived[1:]):
        chain.terms[-1] = (array, chain.terms[-1][1])
    ffn_part = jnp.concatenate([chain.part(0, chain.rows, 0) for chain in chains[:first]], axis=0)
    ffn_sum = deep_sum(ffn_part)
    chains = chains[first:]
    after = ffn_part
    for kind in ORDER:
        if kind == "I":
            early = gate(early, [send, after])
            after = input_grad = input_back(early, late, wp_qkv, d_res1)
        elif kind == "F":
            after = ffn_sum = gate(ffn_sum, [after])
            ffn_other = flip(ffn_sum, 1)
        else:
            after = turn(after, ("AB".index(kind),))
    attn_halves = [item for chain in chains for item in chain.finish()]
    g_up, g_down = ffn_final(spot, ffn_sum, ffn_other, chunk_count)
    g_out, g_qkv, g_bqkv, g_bout, g_gain1, g_bias1, g_bup, g_bdown, g_gain2, g_bias2 = attn_final(
        spot, attn_halves, sizes, model, chunk_count
    )
    return (
        block_out,
        input_grad,
        g_qkv,
        g_bqkv,
        g_out,
        g_bout,
        g_gain1,
        g_bias1,
        g_up,
        g_bup,
        g_down,
        g_bdown,
        g_gain2,
        g_bias2,
    )


def solution(mesh):
    return jax.shard_map(
        body,
        mesh=mesh,
        in_specs=(
            P(("dp", "mx", "my"), None),
            P("mx", "my"),
            P(("mx", "my")),
            P("mx", "my"),
            P(("mx", "my")),
            P(("mx", "my")),
            P(("mx", "my")),
            P("mx", "my"),
            P(("mx", "my")),
            P("mx", "my"),
            P(("mx", "my")),
            P(("mx", "my")),
            P(("mx", "my")),
            P(("dp", "mx", "my")),
            P(("dp", "mx", "my"), None),
            P(("dp", "mx", "my"), None),
        ),
        out_specs=(
            P(("dp", "mx", "my"), None),
            P(("dp", "mx", "my"), None),
            P("mx", "my"),
            P(("mx", "my")),
            P("mx", "my"),
            P(("mx", "my")),
            P(("mx", "my")),
            P(("mx", "my")),
            P("mx", "my"),
            P(("mx", "my")),
            P("mx", "my"),
            P(("mx", "my")),
            P(("mx", "my")),
            P(("mx", "my")),
        ),
        check_vma=False,
    )
```

```python
import functools
import math

import jax
import jax.numpy as jnp
from jax import lax
from jax.experimental import pallas as pl
from jax.experimental.pallas import tpu as pltpu
from jax.sharding import PartitionSpec as P

HD = 64
LANE = 128
TILE = 256
GROUPS = 3
MIB = 1 << 20
VMEM_MIB = 58
BLOCK = 768
VECTOR_ROWS = 64
SPLITS = (2, 1)
TURNS = (
    ((0,), (1,)),
    ((0,), (1,), (0,), (1,)),
    ((0,), (1,), (0,), (1,), (0,)),
)

BF = jnp.bfloat16
F32 = jnp.float32
norm_eps = 1e-05


def dot(left, right):
    return lax.dot_general(left, right, (((1,), (0,)), ((), ())), preferred_element_type=F32)


def dot_t(left, right):
    return lax.dot_general(left, right, (((1,), (1,)), ((), ())), preferred_element_type=F32)


def t_dot(left, right):
    return lax.dot_general(left, right, (((0,), (0,)), ((), ())), preferred_element_type=F32)


def low_half(shape):
    return lax.broadcasted_iota(jnp.int32, shape, 1) < HD


def params(limit, grid_dims=0):
    return pltpu.CompilerParams(
        dimension_semantics=("arbitrary",) * grid_dims if grid_dims else None,
        vmem_limit_bytes=limit * MIB,
    )


def cost(*_):
    return pl.CostEstimate(flops=1000, bytes_accessed=1000, transcendentals=0)


def hbm(shape, dtype):
    return pltpu.HBM(shape, dtype)


def vmem(shape, dtype):
    return jax.ShapeDtypeStruct(shape, dtype)


def full(shape):
    return pl.BlockSpec(shape, lambda *_: (0,) * len(shape))


ANY = pl.BlockSpec(memory_space=pl.ANY)


def shift(value, axis, step):
    size = lax.axis_size(axis)
    return lax.ppermute(value, axis, [(i, (i + step) % size) for i in range(size)])


def pair_swap(value, axis):
    size = lax.axis_size(axis)
    return lax.ppermute(value, axis, [(i, i ^ 1) for i in range(size)])


def flip(value, bit):
    size = lax.axis_size("dp")
    return lax.ppermute(value, "dp", [(i, i ^ bit) for i in range(size)])


def gate(value, deps):
    return lax.optimization_barrier((value,) + tuple(deps))[0]


def fetch_near(block):
    return [block, pair_swap(block, "my")]


def fetch_far(block, *deps):
    grid_rows = lax.axis_size("mx")
    block = gate(block, deps) if deps else block
    return [shift(block, "mx", step) for step in range(1, grid_rows)]


def fetch_rest(near, far, *deps):
    if deps:
        far = list(lax.optimization_barrier(tuple(far) + deps)[: len(far)])
    return near + far + [pair_swap(item, "my") for item in far]


def fetch_thirds(block, *deps):
    rows = block.shape[0] // 3
    grid_rows = lax.axis_size("mx")
    side = lax.axis_index("dp") % 2
    own = lax.dynamic_slice_in_dim(block, side * rows, rows, axis=0)
    pieces, places = [], []
    for step in range(1, grid_rows):
        first = shift(gate(own, deps), "mx", step)
        row = (lax.axis_index("mx") - step + grid_rows) % grid_rows * 3
        pieces += [first, flip(first, 1), shift(block[2 * rows :], "mx", step)]
        places += [(row + side) * rows, (row + 1 - side) * rows, (row + 2) * rows]
    return pieces, places


def third_places(places, rows):
    row = lax.axis_index("mx") * rows
    col = lax.axis_index("my")
    flat = [row, col, row, 1 - col]
    for c in (col, 1 - col):
        for place in places:
            flat += [place, c]
    return jnp.stack([jnp.asarray(item, jnp.int32) for item in flat])


def piece_places():
    grid_rows = lax.axis_size("mx")
    row = lax.axis_index("mx")
    col = lax.axis_index("my")
    places = [(row, col), (row, 1 - col)]
    for c in (col, 1 - col):
        for step in range(1, grid_rows):
            places.append(((row - step + grid_rows) % grid_rows, c))
    return jnp.stack([jnp.asarray(item, jnp.int32) for place in places for item in place])


def pack_kernel(*refs):
    out_ref = refs[-1]
    for index, ref in enumerate(refs[:-1]):
        size = ref.shape[0]
        out_ref[index : index + 1, 0:size] = ref[...].astype(F32).reshape(1, size)


def pack_vectors(vectors):
    wide = max(item.shape[0] for item in vectors)
    return pl.pallas_call(
        pack_kernel,
        out_shape=jax.ShapeDtypeStruct((len(vectors), wide), F32),
        compiler_params=params(VMEM_MIB),
        name="pack",
    )(*vectors)


def spread_kernel(sizes, grid_rows, chunk_count, places_ref, *refs):
    owners = grid_rows * 2
    qkv_ref, up_ref, rest_ref = refs[owners : owners + 3]
    scr = refs[owners + 3]
    rest = 0
    for index, size in enumerate(sizes):
        total = size * owners
        whole = jnp.zeros((1, total), F32)
        for owner in range(owners):
            place = places_ref[2 * owner] * 2 + places_ref[2 * owner + 1]
            scr[...] = jnp.zeros_like(scr)
            scr[:, 0:size] = refs[owner][index : index + 1, 0:size]
            whole = whole + pltpu.roll(scr[:, 0:total], place * size, 1)
        if index == 0:
            for unit in range(6 * GROUPS):
                part, pair = unit // (2 * GROUPS), unit % (2 * GROUPS)
                lane = (pair % GROUPS) * 6 * LANE + (2 * part + pair // GROUPS) * LANE
                qkv_ref[:, lane : lane + LANE] = whole[:, unit * LANE : (unit + 1) * LANE]
        elif index == 4:
            piece = total // grid_rows // chunk_count
            for i in range(grid_rows):
                for c in range(chunk_count):
                    src, dst = (i * chunk_count + c) * piece, (c * grid_rows + i) * piece
                    up_ref[:, dst : dst + piece] = whole[:, src : src + piece]
        else:
            rest_ref[rest : rest + 1, :] = whole
            rest += 1
    rest_ref[rest:8, :] = jnp.zeros((8 - rest, rest_ref.shape[1]), F32)


def spread_vectors(places, packs, sizes, chunk_count):
    grid_rows = lax.axis_size("mx")
    owners = grid_rows * 2
    wide = max(sizes) * owners
    return pl.pallas_call(
        functools.partial(spread_kernel, sizes, grid_rows, chunk_count),
        grid_spec=pltpu.PrefetchScalarGridSpec(
            num_scalar_prefetch=1,
            grid=(1,),
            in_specs=[full(item.shape) for item in packs],
            out_specs=[
                full((1, sizes[0] * owners)),
                full((1, sizes[4] * owners)),
                full((8, sizes[1] * owners)),
            ],
            scratch_shapes=[pltpu.VMEM((1, wide), F32)],
        ),
        out_shape=[
            jax.ShapeDtypeStruct((1, sizes[0] * owners), F32),
            jax.ShapeDtypeStruct((1, sizes[4] * owners), F32),
            jax.ShapeDtypeStruct((8, sizes[1] * owners), F32),
        ],
        compiler_params=params(VMEM_MIB, 1),
        name="spread",
    )(places, *packs)


def share_vectors(spot_ref, rows, groups, outs, grid_rows, chunk_count):
    owners = grid_rows * 2
    owner = spot_ref[0] * 2 + spot_ref[1]

    def pair(index):
        return [rows[2 * index : 2 * index + 1, :], rows[2 * index + 1 : 2 * index + 2, :]]

    qkv = []
    for unit in range(6 * GROUPS):
        part, place = unit // (2 * GROUPS), unit % (2 * GROUPS)
        lane = 2 * part + place // GROUPS
        row = groups[place % GROUPS][lane // 3 : lane // 3 + 1, :]
        qkv.append(row[:, (lane % 3) * LANE : (lane % 3 + 1) * LANE])
    wide = rows.shape[1]
    piece = outs[4].shape[0] * owners // grid_rows // chunk_count
    ups = []
    for i in range(grid_rows):
        for c in range(chunk_count):
            for part in range(piece // LANE):
                place = (c * grid_rows + i) * piece + part * LANE
                row, lane = 12 + place // wide, place % wide
                ups.append(rows[row : row + 1, lane : lane + LANE])
    for items, out_ref in zip(
        (qkv, pair(0), pair(1), pair(2), ups, pair(3), pair(4), pair(5)), outs
    ):
        size = out_ref.shape[0]
        total = size * owners
        whole = jnp.concatenate(items, axis=1)
        turned = pltpu.roll(whole, lax.rem(total - owner * size, total), 1)
        out_ref[...] = turned[:, 0:size].reshape(size)


def gates(values, dep):
    return list(lax.optimization_barrier(tuple(values) + (dep,))[:-1])


class Chain:
    def __init__(self, send, keep, plan):
        self.plan = plan
        self.stage = 0
        self.fresh = send
        self.terms = [(keep, 0), (pair_swap(send, "my"), 0)]
        self.rows = send.shape[1]
        self.split = True

    def part(self, first, rows, owner=None):
        result = None
        for array, start in self.terms:
            if array.ndim == 3:
                count = array.shape[0] if owner is None else 1
                at = (0 if owner is None else owner, start + first, 0)
                item = lax.dynamic_slice(array, at, (count, rows, array.shape[2]))
                item = item if owner is None else item[0]
            else:
                item = lax.dynamic_slice(array, (start + first, 0), (rows, array.shape[1]))
            if len(self.terms) > 2:
                item = item.astype(F32)
            result = item if result is None else result + item
        return result.astype(BF)

    def step(self, after=None):
        if self.stage == len(self.plan):
            return False
        kind, bit = self.plan[self.stage]
        self.stage += 1
        array, start = self.terms[-1]
        if after is not None:
            self.terms[-1] = (gate(array, [after]), start)
        owner = None if self.split else 0
        if kind == "mx":
            parts = [self.part(0, self.rows, i) for i in range(1, lax.axis_size("mx"))]
            self.fresh = parts[0]
            self.terms += [(shift(part, "mx", i + 1), 0) for i, part in enumerate(parts)]
            self.split = False
        elif kind == "halve":
            side = lax.axis_index("dp") // bit % 2
            self.rows //= 2
            self.fresh = self.part((1 - side) * self.rows, self.rows, owner)
            self.terms = [(array, start + side * self.rows) for array, start in self.terms]
            self.terms.append((flip(self.fresh, bit), 0))
        else:
            if kind == "join" and self.plan[self.stage - 2][0] == "join":
                self.fresh = jnp.concatenate([array for array, _ in self.terms], axis=0)
            else:
                self.fresh = self.part(0, self.rows, owner)
            self.terms = [(self.fresh, 0), (flip(self.fresh, bit), 0)]
        return True

    def finish(self):
        while self.step():
            pass
        return [array for array, _ in self.terms]


def plan(split):
    bits = []
    while 1 << len(bits) < lax.axis_size("dp"):
        bits.append(1 << len(bits))
    return (
        [("mx", None)]
        + [("halve", bit) for bit in bits[:split]]
        + [("whole", bit) for bit in bits[split:]]
        + [("join", bit) for bit in bits[:split][::-1]]
    )


def deep_sum(value):
    size = lax.axis_size("dp")
    groups = [list(range(start, size, 2)) for start in range(2)]
    return lax.psum(value, "dp", axis_index_groups=groups)


def place_copies(places_ref, refs, sems, put):
    copies = []
    for index, ref in enumerate(refs):
        copies += put(places_ref[2 * index], places_ref[2 * index + 1], ref)
    return [
        pltpu.make_async_copy(src, dst, sems.at[index]) for index, (src, dst) in enumerate(copies)
    ]


def aligned(value, size):
    return pl.multiple_of(value, size)


def attend_kernel(pieces, width, places_ref, *refs):
    x_ref = refs[0]
    w_refs = refs[1 : 1 + pieces]
    bias_ref, cs_ref, segc_ref, segr_ref, qm_ref, km_ref = refs[1 + pieces : 7 + pieces]
    qf_ref, kf_ref, vp_ref, out_a, out_b, rden_ref, wp_ref = refs[7 + pieces : 14 + pieces]
    w_scr, mask_scr, sems, out_sem = refs[14 + pieces :]
    step = pl.program_id(0)
    tokens = x_ref.shape[0]
    model = x_ref.shape[1]
    chunks = tokens // TILE
    units = width // LANE

    def put(row, col, ref):
        rows = ref.shape[0]
        start = aligned(row, 16)
        result = []
        for unit in range(units):
            where = col * units + unit
            part = where // (2 * GROUPS)
            pair = where % (2 * GROUPS)
            group = pair % GROUPS
            lane = aligned(part * (2 * LANE) + (pair // GROUPS) * LANE, LANE)
            result.append(
                (
                    ref.at[:, unit * LANE : (unit + 1) * LANE],
                    w_scr.at[group, pl.ds(start, rows), pl.ds(lane, LANE)],
                )
            )
        return result

    out_copy = pltpu.make_async_copy(w_scr, wp_ref, out_sem)

    @pl.when(step == 0)
    def _():
        copies = place_copies(places_ref, w_refs, sems, put)
        for copy in copies:
            copy.start()
        ii = lax.broadcasted_iota(jnp.int32, (TILE, TILE), 0)
        jj = lax.broadcasted_iota(jnp.int32, (TILE, TILE), 1)
        for c in range(chunks):
            rows = slice(c * TILE, (c + 1) * TILE)
            keep = (segc_ref[rows, :] == segr_ref[:, rows]) & (jj <= ii)
            mask_scr[c] = jnp.where(keep, 1.0, 0.0)
        for copy in copies:
            copy.wait()
        out_copy.start()

    low = low_half((TILE, LANE))
    for r in range(chunks):
        rows = slice(r * TILE, (r + 1) * TILE)
        acc = dot(x_ref[rows, :], w_scr[step]) + bias_ref[...]
        cs = cs_ref[rows, :]
        for a in range(2):
            q = jnp.maximum(acc[:, a * LANE : (a + 1) * LANE], 0.0) * 0.125
            k = jnp.maximum(acc[:, (2 + a) * LANE : (3 + a) * LANE], 0.0)
            v = acc[:, (4 + a) * LANE : (5 + a) * LANE]
            q_r = pltpu.roll(q, HD, 1)
            k_r = pltpu.roll(k, HD, 1)
            first = slice(2 * a * LANE, (2 * a + 1) * LANE)
            second = slice((2 * a + 1) * LANE, (2 * a + 2) * LANE)
            qf_ref[rows, first] = (jnp.where(low, q, q_r) * cs).astype(BF)
            qf_ref[rows, second] = (jnp.where(low, q_r, q) * cs).astype(BF)
            kf_ref[rows, first] = (jnp.where(low, k, k_r) * cs).astype(BF)
            kf_ref[rows, second] = (jnp.where(low, k_r, k) * cs).astype(BF)
            vp_ref[rows, first] = jnp.where(low, v, 1.0).astype(BF)
            vp_ref[rows, second] = jnp.where(low, 1.0, v).astype(BF)

    states = [None] * 4
    totals = [None] * 4
    for c in range(chunks):
        rows = slice(c * TILE, (c + 1) * TILE)
        mask = mask_scr[c]
        qm = qm_ref[rows, :]
        km = km_ref[rows, :]
        for a in range(2):
            outs, denoms = [], []
            for h in (2 * a, 2 * a + 1):
                cols = slice(h * LANE, (h + 1) * LANE)
                q = qf_ref[rows, cols]
                k = kf_ref[rows, cols]
                v = vp_ref[rows, cols]
                scores = dot_t(q, k) * mask
                out = dot(scores.astype(BF), v)
                denom = scores[:, :LANE] + scores[:, LANE:]
                if c > 0:
                    out = out + qm * dot(q, states[h].astype(BF))
                    denom = denom + q.astype(F32) * (totals[h] * qm)
                outs.append(out)
                denoms.append(jnp.sum(denom, axis=1, keepdims=True))
                if c < chunks - 1:
                    held = k * km.astype(BF)
                    grown = t_dot(held, v)
                    total = jnp.sum(held.astype(F32), axis=0, keepdims=True)
                    if c > 0:
                        whole = qm[TILE - 1 : TILE, :]
                        grown = grown + states[h] * whole
                        total = total + totals[h] * whole
                    states[h] = grown
                    totals[h] = total
            numer = jnp.where(low, outs[0], outs[1])
            rden = 1.0 / jnp.maximum(jnp.where(low, denoms[0], denoms[1]), 1.0)
            rden_ref[rows, a * LANE : (a + 1) * LANE] = rden
            (out_a, out_b)[a][rows, :] = (numer * rden).astype(BF)

    @pl.when(step == GROUPS - 1)
    def _():
        out_copy.wait()


def attend(places, x, pieces, bias, cs, segc, segr, qm, km):
    tokens, model = x.shape
    count = len(pieces)
    width = 3 * model // 2
    group = 6 * LANE
    spec = pl.BlockSpec((tokens, 4 * LANE), lambda g, p: (0, g))
    half = pl.BlockSpec((tokens, LANE), lambda g, p: (0, g))
    return pl.pallas_call(
        functools.partial(attend_kernel, count, width),
        grid_spec=pltpu.PrefetchScalarGridSpec(
            num_scalar_prefetch=1,
            grid=(GROUPS,),
            in_specs=[full((tokens, model))]
            + [ANY] * count
            + [
                pl.BlockSpec((1, group), lambda g, p: (0, g)),
                full((tokens, LANE)),
                full((tokens, 1)),
                full((1, tokens)),
                full((tokens, LANE)),
                full((tokens, LANE)),
            ],
            out_specs=[
                spec,
                spec,
                spec,
                half,
                half,
                pl.BlockSpec((tokens, 2 * LANE), lambda g, p: (0, g)),
                ANY,
            ],
            scratch_shapes=[
                pltpu.VMEM((GROUPS, model, group), BF),
                pltpu.VMEM((tokens // TILE, TILE, TILE), F32),
                pltpu.SemaphoreType.DMA((count * (width // LANE),)),
                pltpu.SemaphoreType.DMA,
            ],
        ),
        out_shape=[hbm((tokens, GROUPS * 4 * LANE), BF)] * 3
        + [jax.ShapeDtypeStruct((tokens, GROUPS * LANE), BF)] * 2
        + [
            hbm((tokens, model), F32),
            hbm((GROUPS, model, group), BF),
        ],
        compiler_params=params(VMEM_MIB, 1),
        cost_estimate=cost(2 * tokens * model * 3 * model * 1.8, 20 * MIB),
        name="attend",
    )(places, x, *pieces, bias, cs, segc, segr, qm, km)


def rows_put(target, first):
    def put(row, col, ref):
        rows = ref.shape[0]
        width = ref.shape[1] - first
        start = row
        return [
            (
                ref.at[:, first : first + width],
                target.at[pl.ds(aligned(start, 16), rows), pl.ds(aligned(col * width, LANE), width)],
            )
        ]

    return put


def join_kernel(pieces, places_ref, *refs):
    a_ref, b_ref, x_ref = refs[:3]
    w_refs = refs[3 : 3 + pieces]
    rest_ref = refs[3 + pieces]
    xhat_ref, rstd_ref, hb_ref, ht_ref, at_ref, wo_ref = refs[4 + pieces : 10 + pieces]
    w_scr, sems, out_sem = refs[10 + pieces :]
    step = pl.program_id(0)
    out_copy = pltpu.make_async_copy(w_scr, wo_ref, out_sem)

    @pl.when(step == 0)
    def _():
        copies = place_copies(places_ref, w_refs, sems, rows_put(w_scr, 3 * w_scr.shape[1] // 2))
        for copy in copies:
            copy.start()
        for copy in copies:
            copy.wait()
        out_copy.start()

    attn = jnp.concatenate([a_ref[...], b_ref[...]], axis=1)
    resid = x_ref[...].astype(F32) + dot(attn, w_scr[...]) + rest_ref[0:1, :]
    center = resid - jnp.mean(resid, axis=1, keepdims=True)
    rstd = lax.rsqrt(jnp.mean(center * center, axis=1, keepdims=True) + norm_eps)
    xhat = center * rstd
    hidden = xhat * rest_ref[1:2, :] + rest_ref[2:3, :]
    xhat_ref[...] = xhat
    rstd_ref[...] = jnp.broadcast_to(rstd, rstd_ref.shape)
    hb_ref[...] = hidden.astype(BF)
    ht_ref[...] = hidden.T.astype(BF)
    at_ref[...] = attn.astype(F32).T.astype(BF)

    @pl.when(step == pl.num_programs(0) - 1)
    def _():
        out_copy.wait()


def join(places, attn_a, attn_b, x, pieces, rest):
    tokens, model = x.shape
    count = len(pieces)
    row = pl.BlockSpec((TILE, model), lambda r, p: (r, 0))
    half = pl.BlockSpec((TILE, model // 2), lambda r, p: (r, 0))
    flip = pl.BlockSpec((model, TILE), lambda r, p: (0, r))
    return pl.pallas_call(
        functools.partial(join_kernel, count),
        grid_spec=pltpu.PrefetchScalarGridSpec(
            num_scalar_prefetch=1,
            grid=(tokens // TILE,),
            in_specs=[half, half, row] + [ANY] * count + [full((8, model))],
            out_specs=[row, pl.BlockSpec((TILE, LANE), lambda r, p: (r, 0)), row, flip, flip, ANY],
            scratch_shapes=[
                pltpu.VMEM((model, model), BF),
                pltpu.SemaphoreType.DMA((count,)),
                pltpu.SemaphoreType.DMA,
            ],
        ),
        out_shape=[
            hbm((tokens, model), F32),
            hbm((tokens, LANE), F32),
            vmem((tokens, model), BF),
            hbm((model, tokens), BF),
            hbm((model, tokens), BF),
            hbm((model, model), BF),
        ],
        compiler_params=params(VMEM_MIB, 1),
        cost_estimate=cost(2 * tokens * model * model, 14 * MIB),
        name="join",
    )(places, attn_a, attn_b, x, *pieces, rest)


def up_kernel(pieces, chunk_count, places_ref, *refs):
    h_ref = refs[0]
    w_refs = refs[1 : 1 + pieces]
    bias_ref = refs[1 + pieces]
    act_ref, slope_ref, wp_ref = refs[2 + pieces : 5 + pieces]
    w_scr, sems, out_sem = refs[5 + pieces :]
    step = pl.program_id(0)
    wide = w_scr.shape[2]
    out_copy = pltpu.make_async_copy(w_scr, wp_ref, out_sem)

    @pl.when(step == 0)
    def _():
        width = w_refs[0].shape[1]
        piece = wide // lax.axis_size("mx")
        blocks = width // (piece * chunk_count)

        def put(row, col, ref):
            rows = ref.shape[0]
            start = row * rows
            result = []
            for i in range(blocks):
                for c in range(chunk_count):
                    lane = aligned((col * blocks + i) * piece, LANE)
                    src = (i * chunk_count + c) * piece
                    result.append(
                        (
                            ref.at[:, src : src + piece],
                            w_scr.at[c, pl.ds(aligned(start, 16), rows), pl.ds(lane, piece)],
                        )
                    )
            return result

        copies = place_copies(places_ref, w_refs, sems, put)
        for copy in copies:
            copy.start()
        for copy in copies:
            copy.wait()
        out_copy.start()

    tokens = h_ref.shape[0]
    for r in range(tokens // TILE):
        rows = slice(r * TILE, (r + 1) * TILE)
        up = dot(h_ref[rows, :], w_scr[step]) + bias_ref[...]
        phi = lax.erf(up * math.sqrt(0.5)) * 0.5 + 0.5
        bell = jnp.exp(up * up * -0.5) * (1.0 / math.sqrt(2.0 * math.pi))
        act_ref[rows, :] = (up * phi).astype(BF)
        slope_ref[rows, :] = (phi + up * bell).astype(BF)

    @pl.when(step == pl.num_programs(0) - 1)
    def _():
        out_copy.wait()


def up_project(places, hidden, pieces, bias, chunk_count):
    tokens, model = hidden.shape
    count = len(pieces)
    hidden_units = pieces[0].shape[1] * 2
    wide = hidden_units // chunk_count
    piece = wide // lax.axis_size("mx")
    per = pieces[0].shape[1] // piece
    col = pl.BlockSpec((tokens, wide), lambda c, p: (0, c))
    return pl.pallas_call(
        functools.partial(up_kernel, count, chunk_count),
        grid_spec=pltpu.PrefetchScalarGridSpec(
            num_scalar_prefetch=1,
            grid=(chunk_count,),
            in_specs=[full((tokens, model))]
            + [ANY] * count
            + [pl.BlockSpec((1, wide), lambda c, p: (0, c))],
            out_specs=[col, col, ANY],
            scratch_shapes=[
                pltpu.VMEM((chunk_count, model, wide), BF),
                pltpu.SemaphoreType.DMA((count * per,)),
                pltpu.SemaphoreType.DMA,
            ],
        ),
        out_shape=[hbm((tokens, hidden_units), BF)] * 2 + [hbm((chunk_count, model, wide), BF)],
        compiler_params=params(VMEM_MIB, 1),
        cost_estimate=cost(
            2 * tokens * model * hidden_units, 24 * MIB, 2 * tokens * hidden_units
        ),
        name="up",
    )(places, hidden, *pieces, bias)


def once(shape):
    return pl.BlockSpec(shape, lambda *_: (0,) * len(shape), pipeline_mode=pl.Buffered(1))


def ffn_kernel(pieces, chunk_count, grid_rows, piece, tiles, places_ref, spot_ref, *refs):
    rowa_ref, xhat_ref, cot_ref = refs[:3]
    w_refs = refs[3 : 3 + pieces]
    rest_ref, ht_hbm, act_ref, slope_ref, wu_ref = refs[3 + pieces : 8 + pieces]
    outs = refs[8 + pieces :]
    out_ref, sums_ref, dh_ref, bsum_ref = outs[:4]
    keeps = outs[4 : 4 + chunk_count]
    sends = outs[4 + chunk_count : 4 + 2 * chunk_count]
    w_scr, dup_scr, dd_ref, ddt_ref, ht_ref, sems, ht_sem = outs[4 + 2 * chunk_count :]
    row, col = spot_ref[0], spot_ref[1]
    step = pl.program_id(0)
    wide = w_scr.shape[0] // chunk_count
    tokens, block = act_ref.shape
    model = dh_ref.shape[1]
    half, share = model // 2, model // grid_rows
    per = grid_rows // 2
    ht_copy = pltpu.make_async_copy(ht_hbm, ht_ref, ht_sem)

    @pl.when(step == 0)
    def _():
        def put(row, col, ref):
            width = ref.shape[1]
            lane = pl.ds(aligned(col * width, LANE), width)
            return [
                (
                    ref.at[c * piece : (c + 1) * piece, :],
                    w_scr.at[pl.ds(aligned(c * wide + row * piece, 16), piece), lane],
                )
                for c in range(chunk_count)
            ]

        copies = place_copies(places_ref, w_refs, sems, put)
        for copy in copies:
            copy.start()
        ht_copy.start()
        sums_ref[...] = jnp.zeros_like(sums_ref)
        for copy in copies:
            copy.wait()

    @pl.when(step < tiles)
    def _():
        rows = pl.ds(aligned(step * TILE, TILE), TILE)
        hidden = xhat_ref[...] * rest_ref[1:2, :] + rest_ref[2:3, :]
        resid = hidden + dot(rowa_ref[...], w_scr[...]) + rest_ref[3:4, :]
        center = resid - jnp.mean(resid, axis=1, keepdims=True)
        rstd = lax.rsqrt(jnp.mean(center * center, axis=1, keepdims=True) + norm_eps)
        xhat = center * rstd
        out_ref[...] = (xhat * rest_ref[4:5, :] + rest_ref[5:6, :]).astype(BF)
        g = cot_ref[...].astype(F32)
        e = g * rest_ref[4:5, :]
        d_res = rstd * (
            e
            - jnp.mean(e, axis=1, keepdims=True)
            - xhat * jnp.mean(e * xhat, axis=1, keepdims=True)
        )
        dh_ref[rows, :] = d_res
        d_down = d_res.astype(BF)
        dd_ref[rows, :] = d_down
        ddt_ref[:, rows] = d_down.T
        sums_ref[0:1, :] += jnp.sum(g * xhat, axis=0, keepdims=True)
        sums_ref[1:2, :] += jnp.sum(g, axis=0, keepdims=True)
        sums_ref[2:3, :] += jnp.sum(d_down.astype(F32), axis=0, keepdims=True)

    @pl.when(step == tiles)
    def _():
        ht_copy.wait()

    @pl.when(step >= tiles)
    def _():
        turn = step - tiles
        blocks = piece // block
        owner = lax.rem(turn // blocks, grid_rows)
        chunk = turn // (blocks * grid_rows)
        lane = pl.ds(aligned(lax.rem(turn, blocks) * block, LANE), block)
        wd = w_scr.at[pl.ds(aligned(turn * block, 16), block), :]
        total = jnp.zeros((1, block), F32)
        for r in range(tokens // TILE):
            rows = slice(r * TILE, (r + 1) * TILE)
            grad = (dot_t(dd_ref[rows, :], wd[...]) * slope_ref[rows, :].astype(F32)).astype(BF)
            dup_scr[rows, :] = grad
            total = total + jnp.sum(grad.astype(F32), axis=0, keepdims=True)
        bsum_ref[...] = jnp.broadcast_to(total, bsum_ref.shape)
        for r in range(tokens // TILE):
            rows = slice(r * TILE, (r + 1) * TILE)
            dh_ref[rows, :] += dot_t(dup_scr[rows, :], wu_ref[...])
        slot = lax.rem(owner - row + grid_rows, grid_rows)
        place = aligned(half + lax.rem(owner, per) * share, 16)
        down = dot(ddt_ref[pl.ds(aligned(col * half, 16), half), :], act_ref[...]).astype(BF)
        down_far = dot(
            ddt_ref[pl.ds(aligned((1 - col) * half, 16), half), :], act_ref[...]
        ).astype(BF)
        up = dot(ht_ref[...], dup_scr[...]).astype(BF)
        for c in range(chunk_count):

            @pl.when(chunk == c)
            def _():
                keeps[c][slot, 0:half, lane] = down
                sends[c][slot, 0:half, lane] = down_far
                for mine, target in ((True, keeps[c]), (False, sends[c])):

                    @pl.when((owner // per == col) == mine)
                    def _():
                        for i in range(grid_rows):
                            where = lax.rem(i - row + grid_rows, grid_rows)
                            target[where, pl.ds(place, share), lane] = up[
                                i * share : (i + 1) * share, :
                            ]


def ffn(places, spot, act, slope, xhat, cot, pieces, rest, hidden_t, w_up, chunk_count):
    tokens, hidden_units = act.shape
    model = xhat.shape[1]
    count = len(pieces)
    grid_rows = lax.axis_size("mx")
    wide = hidden_units // chunk_count
    piece = wide // grid_rows
    block = min(piece, BLOCK)
    message = (grid_rows, model, piece)
    tiles = tokens // TILE
    inner = wide // block

    def row(width):
        return pl.BlockSpec((TILE, width), lambda s, *_: (jnp.minimum(s, tiles - 1), 0))

    def late(s):
        return jnp.maximum(s - tiles, 0)

    pick = pl.BlockSpec((tokens, block), lambda s, *_: (0, late(s)))
    return pl.pallas_call(
        functools.partial(ffn_kernel, count, chunk_count, grid_rows, piece, tiles),
        grid_spec=pltpu.PrefetchScalarGridSpec(
            num_scalar_prefetch=2,
            grid=(tiles + hidden_units // block,),
            in_specs=[row(hidden_units), row(model), row(model)]
            + [ANY] * count
            + [
                once((8, model)),
                ANY,
                pick,
                pick,
                pl.BlockSpec(
                    (None, model, block), lambda s, *_: (late(s) // inner, 0, late(s) % inner)
                ),
            ],
            out_specs=[
                row(model),
                once((8, model)),
                once((tokens, model)),
                pl.BlockSpec((8, block), lambda s, *_: (0, late(s))),
            ]
            + [once(message)] * (2 * chunk_count),
            scratch_shapes=[
                pltpu.VMEM((hidden_units, model), BF),
                pltpu.VMEM((tokens, block), BF),
                pltpu.VMEM((tokens, model), BF),
                pltpu.VMEM((model, tokens), BF),
                pltpu.VMEM((model, tokens), BF),
                pltpu.SemaphoreType.DMA((count * chunk_count,)),
                pltpu.SemaphoreType.DMA,
            ],
        ),
        out_shape=[
            hbm((tokens, model), BF),
            vmem((8, model), F32),
            hbm((tokens, model), F32),
            vmem((8, hidden_units), F32),
        ]
        + [hbm(message, BF)] * (2 * chunk_count),
        compiler_params=params(VMEM_MIB, 1),
        cost_estimate=cost(),
        name="ffn",
    )(places, spot, act, xhat, cot, *pieces, rest, hidden_t, act, slope, w_up)


def norm_kernel(grid_rows, spot_ref, *refs):
    (
        dres_ref,
        xhat_ref,
        rstd_ref,
        a_ref,
        b_ref,
        rden_ref,
        wo_ref,
        gain_ref,
        at_ref,
        two_ref,
        up_ref,
    ) = refs[:11]
    dn_ref, dr_ref, keep_ref, send_ref, sums_ref, db_scr, msg_scr, ext_scr, sems = refs[11:]
    step = pl.program_id(0)
    model = dres_ref.shape[1]

    @pl.when(step == 0)
    def _():
        sums_ref[...] = jnp.zeros_like(sums_ref)

    d_hidden = dres_ref[...]
    xhat = xhat_ref[...]
    e = d_hidden * gain_ref[1:2, :]
    d_res = rstd_ref[:, 0:1] * (
        e
        - jnp.mean(e, axis=1, keepdims=True)
        - xhat * jnp.mean(e * xhat, axis=1, keepdims=True)
    )
    dr_ref[...] = d_res
    d_branch = d_res.astype(BF)
    db_scr[pl.ds(aligned(step * TILE, TILE), TILE), :] = d_branch
    sums_ref[0:1, :] += jnp.sum(d_hidden * xhat, axis=0, keepdims=True)
    sums_ref[1:2, :] += jnp.sum(d_hidden, axis=0, keepdims=True)
    sums_ref[2:3, :] += jnp.sum(d_branch.astype(F32), axis=0, keepdims=True)
    d_attn = dot_t(d_branch, wo_ref[...])
    low = low_half((TILE, LANE))
    li = lax.broadcasted_iota(jnp.int32, (LANE, LANE), 0) < HD
    lj = lax.broadcasted_iota(jnp.int32, (LANE, LANE), 1) < HD
    swap = jnp.where(li == lj, 0.0, 1.0 / HD).astype(BF)
    front = lax.broadcasted_iota(jnp.int32, (TILE, LANE), 1) % HD < HD // 2
    for pair in range(2 * GROUPS):
        a, g = pair // GROUPS, pair % GROUPS
        d_pair = d_attn[:, pair * LANE : (pair + 1) * LANE]
        attn = (a_ref, b_ref)[a][:, g * LANE : (g + 1) * LANE].astype(F32)
        rden = rden_ref[:, (2 * g + a) * LANE : (2 * g + a + 1) * LANE]
        prod = d_pair * attn
        high = prod.astype(BF)
        rest = (prod - high.astype(F32)).astype(BF)
        other = dot(high, swap) + dot(rest, swap)
        turned = pltpu.roll(rden, HD, 1)
        d_denom = jnp.where(turned < 1.0, -other * turned, 0.0)
        coarse = d_denom.astype(BF).astype(F32)
        d_denom = 2.0 * jnp.where(front, coarse, d_denom - coarse)
        d_numer = d_pair * rden
        place = (4 * g + 2 * a) * LANE
        dn_ref[:, place : place + LANE] = jnp.where(low, d_numer, d_denom).astype(BF)
        dn_ref[:, place + LANE : place + 2 * LANE] = jnp.where(low, d_denom, d_numer).astype(BF)

    @pl.when(step == pl.num_programs(0) - 1)
    def _():
        row, col = spot_ref[0], spot_ref[1]
        half = model // 2
        share = model // grid_rows
        wide = ext_scr.shape[1]
        ext_scr[...] = jnp.zeros_like(ext_scr)
        for index, (ref, line) in enumerate(
            ((sums_ref, 2), (sums_ref, 0), (sums_ref, 1), (two_ref, 2), (two_ref, 0), (two_ref, 1))
        ):
            for part in range(2):
                ext_scr[2 * index + part : 2 * index + part + 1, :] = ref[
                    line : line + 1, part * wide : (part + 1) * wide
                ].astype(BF)
        for part in range(up_ref.shape[1] // wide):
            ext_scr[12 + part : 13 + part, :] = up_ref[
                0:1, part * wide : (part + 1) * wide
            ].astype(BF)
        message_out(
            row, col, grid_rows, at_ref, db_scr, msg_scr, ext_scr, keep_ref, send_ref, 0, 3, 0, sems
        )


def message_out(
    row, col, grid_rows, left_ref, right_ref, msg_scr, ext_scr, keep_ref, send_ref, place, parts,
    line, sems,
):
    share, half = msg_scr.shape[2:]
    count = ext_scr.shape[0]
    copies = []
    for index, (side, target) in enumerate(((1 - col, send_ref), (col, keep_ref))):
        right = right_ref[:, pl.ds(aligned(side * half, LANE), half)]
        grad = dot(left_ref[...], right).astype(BF)
        for i in range(grid_rows):
            slot = lax.rem(i - row + grid_rows, grid_rows)
            msg_scr[index, slot] = grad[i * share : (i + 1) * share, :]
        pairs = [(msg_scr.at[index], target.at[:, pl.ds(aligned(place * share, 8), share), :])]
        lines = pl.ds(aligned(parts * share + line, 8), count)
        pairs += [(ext_scr, target.at[i, lines, :]) for i in range(grid_rows)]
        for src, dst in pairs:
            copy = pltpu.make_async_copy(src, dst, sems.at[len(copies)])
            copy.start()
            copies.append(copy)
    for copy in copies:
        copy.wait()


def norm_back(
    spot, d_hid, xhat, rstd, attn_a, attn_b, rden, w_out, rest, attn_t, sums_two, up_sums
):
    tokens, model = d_hid.shape
    grid_rows = lax.axis_size("mx")
    row = pl.BlockSpec((TILE, model), lambda r, p: (r, 0))
    half = pl.BlockSpec((TILE, model // 2), lambda r, p: (r, 0))
    share = model // grid_rows
    message = (grid_rows, 3 * share + VECTOR_ROWS, model // 2)
    return pl.pallas_call(
        functools.partial(norm_kernel, grid_rows),
        grid_spec=pltpu.PrefetchScalarGridSpec(
            num_scalar_prefetch=1,
            grid=(tokens // TILE,),
            in_specs=[
                row,
                row,
                pl.BlockSpec((TILE, LANE), lambda r, p: (r, 0)),
                half,
                half,
                row,
                once((model, model)),
                once((8, model)),
                once((model, tokens)),
                once(sums_two.shape),
                once(up_sums.shape),
            ],
            out_specs=[pl.BlockSpec((TILE, 2 * model), lambda r, p: (r, 0)), row, ANY, ANY],
            scratch_shapes=[
                pltpu.VMEM((8, model), F32),
                pltpu.VMEM((tokens, model), BF),
                pltpu.VMEM((2, grid_rows, share, model // 2), BF),
                pltpu.VMEM((VECTOR_ROWS, model // 2), BF),
                pltpu.SemaphoreType.DMA((2 * (grid_rows + 1),)),
            ],
        ),
        out_shape=[
            hbm((tokens, 2 * model), BF),
            hbm((tokens, model), F32),
            hbm(message, BF),
            hbm(message, BF),
        ],
        compiler_params=params(VMEM_MIB, 1),
        cost_estimate=cost(),
        name="norm_back",
    )(spot, d_hid, xhat, rstd, attn_a, attn_b, rden, w_out, rest, attn_t, sums_two, up_sums)


def diagonal(pair):
    first, second = (item.astype(BF) for item in pair)
    zero = jnp.zeros_like(first)
    return jnp.concatenate(
        [jnp.concatenate([first, zero], axis=1), jnp.concatenate([zero, second], axis=1)], axis=0
    )


def group_kernel(grid_rows, shared, spot_ref, *refs):
    place, parts, line = shared
    place = place + pl.program_id(0)
    line = line + 8 * pl.program_id(0)
    (
        qf_ref,
        kf_ref,
        vp_ref,
        dn_ref,
        cs_ref,
        segc_ref,
        segr_ref,
        qm_ref,
        km_ref,
        xt_ref,
    ) = refs[:10]
    dp_ref, keep_ref, send_ref, msg_scr, ext_scr, sems = refs[-6:]
    tokens = qf_ref.shape[0]
    model = xt_ref.shape[0]
    chunks = tokens // TILE
    low = low_half((TILE, LANE))
    ii = lax.broadcasted_iota(jnp.int32, (TILE, TILE), 0)
    jj = lax.broadcasted_iota(jnp.int32, (TILE, TILE), 1)
    kept = [[None] * 2 for _ in range(chunks)]
    for a in range(2):
        state = [None, None]
        for c in range(chunks - 1):
            rows = slice(c * TILE, (c + 1) * TILE)
            km = km_ref[rows, :].astype(BF)
            for n in range(2):
                cols = slice((2 * a + n) * LANE, (2 * a + n + 1) * LANE)
                grown = t_dot(kf_ref[rows, cols] * km, vp_ref[rows, cols])
                if c > 0:
                    grown = grown + state[n] * qm_ref[(c + 1) * TILE - 1 : (c + 1) * TILE, :]
                state[n] = grown
            kept[c + 1][a] = diagonal(state)
    back = [[None, None], [None, None]]
    sums = [jnp.zeros((1, LANE), F32) for _ in range(6)]
    for c in range(chunks - 1, -1, -1):
        rows = slice(c * TILE, (c + 1) * TILE)
        same = segc_ref[rows, :] == segr_ref[:, rows]
        lower = jnp.where(same & (jj <= ii), 1.0, 0.0)
        upper = jnp.where(same & (jj >= ii), 1.0, 0.0)
        qm = qm_ref[rows, :]
        km = km_ref[rows, :]
        cs = cs_ref[rows, :]
        scores = []
        for h in range(4):
            cols = slice(h * LANE, (h + 1) * LANE)
            q = qf_ref[rows, cols]
            k = kf_ref[rows, cols]
            v = vp_ref[rows, cols]
            g = dn_ref[rows, cols]
            scores.append(
                (
                    (dot_t(g, v) * lower).astype(BF),
                    None,
                    (dot_t(k, q) * upper).astype(BF),
                )
            )
        for a in range(2):
            wide = slice(2 * a * LANE, (2 * a + 2) * LANE)
            far_q, far_k, far_v = None, None, None
            if c > 0:
                far_q = dot_t(dn_ref[rows, wide], kept[c][a])
            if c < chunks - 1:
                held = diagonal(back[a])
                far_k = dot_t(vp_ref[rows, wide], held)
                far_v = dot(kf_ref[rows, wide], held)
            dqs, dks, dvs, q_on, k_on = [], [], [], [], []
            for n in range(2):
                h = 2 * a + n
                cols = slice(h * LANE, (h + 1) * LANE)
                part = slice(n * LANE, (n + 1) * LANE)
                q = qf_ref[rows, cols]
                k = kf_ref[rows, cols]
                g = dn_ref[rows, cols]
                d_scores, d_scores_t, scores_t = scores[h]
                dq = dot(d_scores, k)
                dk = t_dot(d_scores, q)
                dv = dot(scores_t, g)
                if c > 0:
                    dq = dq + qm * far_q[:, part]
                if c < chunks - 1:
                    dk = dk + km * far_k[:, part]
                    dv = dv + km * far_v[:, part]
                if c > 0:
                    grown = t_dot(q * qm.astype(BF), g)
                    if c < chunks - 1:
                        grown = grown + back[a][n] * km[0:1, :]
                    back[a][n] = grown
                dq = dq * cs
                dk = dk * cs
                dqs.append(dq + pltpu.roll(dq, HD, 1))
                dks.append(dk + pltpu.roll(dk, HD, 1))
                dvs.append(dv)
                q_abs = jnp.abs(q.astype(F32))
                k_abs = jnp.abs(k.astype(F32))
                q_on.append(q_abs + pltpu.roll(q_abs, HD, 1))
                k_on.append(k_abs + pltpu.roll(k_abs, HD, 1))
            dq = jnp.where(low, dqs[0], dqs[1]) * 0.125
            dk = jnp.where(low, dks[0], dks[1])
            dq = jnp.where(jnp.where(low, q_on[0], q_on[1]) > 0.0, dq, 0.0).astype(BF)
            dk = jnp.where(jnp.where(low, k_on[0], k_on[1]) > 0.0, dk, 0.0).astype(BF)
            dv = jnp.where(low, dvs[0], dvs[1]).astype(BF)
            for part, item in enumerate((dq, dk, dv)):
                unit = 2 * part + a
                dp_ref[rows, unit * LANE : (unit + 1) * LANE] = item
                sums[unit] = sums[unit] + jnp.sum(item.astype(F32), axis=0, keepdims=True)
    ext_scr[...] = jnp.zeros_like(ext_scr)
    for unit in range(6):
        lane = (unit % 3) * LANE
        ext_scr[unit // 3 : unit // 3 + 1, lane : lane + LANE] = sums[unit].astype(BF)
    message_out(
        spot_ref[0], spot_ref[1], grid_rows, xt_ref, dp_ref, msg_scr, ext_scr, keep_ref, send_ref,
        place, parts, line, sems,
    )


def group_back(spot, qf, kf, vp, dn, cs, segc, segr, qm, km, x_t, first, count, messages):
    model, tokens = x_t.shape
    grid_rows = lax.axis_size("mx")
    pick = pl.BlockSpec((tokens, 4 * LANE), lambda s, p: (0, first + s))
    lane = once((tokens, LANE))
    share = model // grid_rows
    if messages:
        shared = (1 + first, 3, 24 + 8 * first)
        shape = messages[0].shape
    else:
        shared = (0, 1, 0)
        shape = (grid_rows, share + 16, 3 * LANE)
    lines = 8 if messages else 16
    return pl.pallas_call(
        functools.partial(group_kernel, grid_rows, shared),
        grid_spec=pltpu.PrefetchScalarGridSpec(
            num_scalar_prefetch=1,
            grid=(count,),
            in_specs=[
                pick,
                pick,
                pick,
                pick,
                lane,
                once((tokens, 1)),
                once((1, tokens)),
                lane,
                lane,
                once((model, tokens)),
            ]
            + [ANY] * len(messages),
            out_specs=[
                pl.BlockSpec((None, tokens, 6 * LANE), lambda s, p: (s, 0, 0)),
                ANY,
                ANY,
            ],
            scratch_shapes=[
                pltpu.VMEM((2, grid_rows, share, 3 * LANE), BF),
                pltpu.VMEM((lines, 3 * LANE), BF),
                pltpu.SemaphoreType.DMA((2 * (grid_rows + 1),)),
            ],
        ),
        out_shape=[hbm((count, tokens, 6 * LANE), BF), hbm(shape, BF), hbm(shape, BF)],
        input_output_aliases={11: 1, 12: 2} if messages else {},
        compiler_params=params(VMEM_MIB, 1),
        cost_estimate=cost(),
        name="group%d" % first,
    )(spot, qf, kf, vp, dn, cs, segc, segr, qm, km, x_t, *messages)


def input_kernel(early_ref, late_ref, w_ref, dr_ref, out_ref):
    total = dr_ref[...]
    early = early_ref.shape[0]
    for g in range(GROUPS):
        grad = early_ref[g] if g < early else late_ref[g - early]
        total = total + dot_t(grad, w_ref[g])
    out_ref[...] = total.astype(BF)


def input_back(early, late, w_qkv, d_res):
    tokens, model = d_res.shape
    row = pl.BlockSpec((TILE, model), lambda r: (r, 0))
    return pl.pallas_call(
        input_kernel,
        grid=(tokens // TILE,),
        in_specs=[
            pl.BlockSpec((item.shape[0], TILE, 6 * LANE), lambda r: (0, r, 0))
            for item in (early, late)
        ]
        + [once(w_qkv.shape), row],
        out_specs=row,
        out_shape=hbm((tokens, model), BF),
        compiler_params=params(VMEM_MIB, 1),
        cost_estimate=cost(),
        name="input_back",
    )(early, late, w_qkv, d_res)


def settle(spot_ref, mine_ref, other_ref, target, split):
    side = spot_ref[2]
    rows = mine_ref.shape[0]
    for half, ref in ((side, mine_ref), (1 - side, other_ref)):
        if split == 1:
            target[pl.ds(aligned(half * rows, 8), rows), :] = ref[...].astype(F32)
        else:
            deep = lax.rem(spot_ref[3], 2)
            block = rows // 2
            for quarter, first in ((deep, 0), (1 - deep, block)):
                start = aligned(half * rows + quarter * block, 8)
                target[pl.ds(start, block), :] = ref[first : first + block, :].astype(F32)


def ffn_final_kernel(chunk_count, grid_rows, spot_ref, mine_ref, other_ref, up_ref, down_ref, scr):
    piece = mine_ref.shape[1]
    rows = mine_ref.shape[0] // chunk_count
    per = grid_rows // 2
    half = scr.shape[0] // 2
    share = half // per
    for c in range(chunk_count):
        part = pl.ds(c * rows, rows)
        settle(spot_ref, mine_ref.at[part, :], other_ref.at[part, :], scr, 1)
        down_ref[c * piece : (c + 1) * piece, :] = scr[0:half, :].T
        for n in range(per):
            lane = (n * chunk_count + c) * piece
            up_ref[:, lane : lane + piece] = scr[half + n * share : half + (n + 1) * share, :]


def ffn_final(spot, mine, other, chunk_count):
    grid_rows = lax.axis_size("mx")
    rows, piece = mine.shape
    rows = 2 * rows // chunk_count
    share = rows // 2 // (grid_rows // 2)
    up_shape = (share, piece * chunk_count * (grid_rows // 2))
    down_shape = (piece * chunk_count, rows // 2)
    return pl.pallas_call(
        functools.partial(ffn_final_kernel, chunk_count, grid_rows),
        grid_spec=pltpu.PrefetchScalarGridSpec(
            num_scalar_prefetch=1,
            grid=(1,),
            in_specs=[full(mine.shape), full(other.shape)],
            out_specs=[full(up_shape), full(down_shape)],
            scratch_shapes=[pltpu.VMEM((rows, piece), F32)],
        ),
        out_shape=[hbm(up_shape, F32), hbm(down_shape, F32)],
        compiler_params=params(VMEM_MIB, 1),
        cost_estimate=cost(),
        name="ffn_final",
    )(spot, mine, other)


def attn_final_kernel(grid_rows, chunk_count, spot_ref, *refs):
    halves = refs[:4]
    out_ref, qkv_ref = refs[4:6]
    one_scr, two_scr = refs[-2:]
    share = out_ref.shape[0]
    settle(spot_ref, halves[0], halves[1], one_scr, SPLITS[0])
    settle(spot_ref, halves[2], halves[3], two_scr, SPLITS[1])
    out_ref[...] = one_scr[0:share, :]
    groups = []
    for g in range(GROUPS):
        last = g == GROUPS - 1
        scr, start = (two_scr, 0) if last else (one_scr, (1 + g) * share)
        for t in range(3):
            lane = (3 * t + g) * LANE
            qkv_ref[:, lane : lane + LANE] = scr[start : start + share, t * LANE : (t + 1) * LANE]
        line = share if last else 3 * share + 24 + 8 * g
        groups.append(scr[line : line + 8, :])
    rows = one_scr[3 * share : 3 * share + 24, :]
    share_vectors(spot_ref, rows, groups, refs[6:-2], grid_rows, chunk_count)


def attn_final(spot, halves, sizes, model, chunk_count):
    grid_rows = lax.axis_size("mx")
    share, wide = model // grid_rows, model // 2
    return pl.pallas_call(
        functools.partial(attn_final_kernel, grid_rows, chunk_count),
        grid_spec=pltpu.PrefetchScalarGridSpec(
            num_scalar_prefetch=1,
            grid=(1,),
            in_specs=[full(item.shape) for item in halves],
            out_specs=[full((share, wide)), full((share, 3 * wide))]
            + [full((size,)) for size in sizes],
            scratch_shapes=[
                pltpu.VMEM((2 * halves[0].shape[0], wide), F32),
                pltpu.VMEM((2 * halves[2].shape[0], wide), F32),
            ],
        ),
        out_shape=[hbm((share, wide), F32), hbm((share, 3 * wide), F32)]
        + [jax.ShapeDtypeStruct((size,), F32) for size in sizes],
        compiler_params=params(VMEM_MIB, 1),
        cost_estimate=cost(),
        name="attn_final",
    )(spot, *halves)


def chunks_for(grid_rows, hidden_units):
    for count in (2, 3):
        if hidden_units % (grid_rows * count * LANE) == 0:
            return count
    return 1


def body(
    layer_input,
    w_qkv,
    b_qkv,
    w_out,
    b_out,
    ln1_gain,
    ln1_bias,
    w_up,
    b_up,
    w_down,
    b_down,
    ln2_gain,
    ln2_bias,
    segment_ids,
    doc_lengths,
    cotangent,
):
    tokens, model = layer_input.shape
    seqs, docs = doc_lengths.shape
    length = tokens // seqs
    grid_rows = lax.axis_size("mx")
    hidden_units = 2 * w_up.shape[1]
    chunk_count = chunks_for(grid_rows, hidden_units)
    row = lax.axis_index("mx")
    col = lax.axis_index("my")
    place = lax.axis_index("dp")
    spot = jnp.stack(
        [jnp.asarray(item, jnp.int32) for item in (row, col, place % 2, place // 2)]
    )
    places = piece_places()

    small = [b_qkv, b_out, ln1_gain, ln1_bias, b_up, b_down, ln2_gain, ln2_bias]
    sizes = [item.shape[0] for item in small]
    packed = pack_vectors(small)
    far_packed = fetch_far(packed)
    w_attn = jnp.concatenate([w_qkv, w_out], axis=1)
    far_attn, far_places = fetch_thirds(w_attn, packed)
    attn_places = third_places(far_places, w_attn.shape[0])
    n_attn, n_up, n_down = (fetch_near(item) for item in (w_attn, w_up, w_down))
    p_packed = fetch_rest(fetch_near(packed), far_packed)
    bias_qkv, bias_up, rest = spread_vectors(places, p_packed, sizes, chunk_count)

    segs = segment_ids.reshape(seqs, length)
    member = segs[:, :, None] == jnp.arange(docs, dtype=jnp.int32)[None, None, :]
    span = jnp.sum(jnp.where(member, doc_lengths[:, None, :], 0), axis=2)
    spots = jnp.arange(length, dtype=jnp.int32)[None, :]
    angle = 0.5 * math.pi * spots.astype(F32) / span.astype(F32)
    angle = angle.reshape(tokens, 1)
    lane = jnp.arange(LANE, dtype=jnp.int32)[None, :]
    cs = jnp.where(lane < HD, jnp.cos(angle), jnp.sin(angle))
    seg = (segs + docs * jnp.arange(seqs, dtype=jnp.int32)[:, None]).reshape(tokens)
    segc = seg.reshape(tokens, 1)
    segr = seg.reshape(1, tokens)
    tiles = seg.reshape(tokens // TILE, TILE)
    before = jnp.concatenate([jnp.full((1,), -1, jnp.int32), tiles[:-1, -1]])
    q_on = (tiles == before[:, None]).reshape(tokens, 1)
    k_on = (tiles == tiles[:, -1:]).reshape(tokens, 1)
    qm = jnp.broadcast_to(q_on.astype(F32), (tokens, LANE))
    km = jnp.broadcast_to(k_on.astype(F32), (tokens, LANE))
    x_t = layer_input.T

    cs, segc, qm, km = lax.optimization_barrier((cs, segc, qm, km))
    p_attn = fetch_rest(n_attn, far_attn, bias_qkv, cs, segc, qm, km)
    far_up = fetch_far(w_up, p_attn[-1])
    far_down = fetch_far(w_down, p_attn[-1])
    qf, kf, vp, attn_a, attn_b, rden, wp_qkv = attend(
        attn_places, layer_input, p_attn, bias_qkv, cs, segc, segr, qm, km
    )
    xhat, rstd, hidden, hidden_t, attn_t, wp_out = join(
        attn_places, attn_a, attn_b, layer_input, p_attn, rest
    )
    p_up = fetch_rest(n_up, far_up, hidden)
    act, slope, wp_up = up_project(places, hidden, p_up, bias_up, chunk_count)
    p_down = fetch_rest(n_down, far_down, act)
    block_out, sums_two, d_hid, up_sums, *messages = ffn(
        places, spot, act, slope, xhat, cotangent, p_down, rest, hidden_t, wp_up, chunk_count
    )
    keeps, sends = messages[:chunk_count], messages[chunk_count:]
    chains = [
        Chain(send, keep, [("halve", 1), ("mx", None)] if i % 2 else [("mx", None), ("halve", 1)])
        for i, (send, keep) in enumerate(zip(sends, keeps))
    ]

    def turn(after, *rounds):
        for picks in rounds:
            live = [chains[i] for i in picks]
            arrived = lax.optimization_barrier((after,) + tuple(item.terms[-1][0] for item in live))
            after = arrived[0]
            for item, array in zip(live, arrived[1:]):
                item.terms[-1] = (array, item.terms[-1][1])
                if item.step(after):
                    after = item.fresh
        return after

    d_hid = gate(d_hid, sends)
    first = chunk_count
    dn, d_res1, keep, send = norm_back(
        spot, d_hid, xhat, rstd, attn_a, attn_b, rden, wp_out, rest, attn_t, sums_two, up_sums
    )
    dn = gate(dn, [turn(d_res1, tuple(range(first)))])
    early, keep, send = group_back(
        spot, qf, kf, vp, dn, cs, segc, segr, qm, km, x_t, 0, GROUPS - 1, (keep, send)
    )
    chains.append(Chain(send, keep, plan(SPLITS[0])))
    dn = gate(dn, [send, turn(early, tuple(range(first)))])
    late, keep, send = group_back(
        spot, qf, kf, vp, dn, cs, segc, segr, qm, km, x_t, GROUPS - 1, 1, ()
    )
    chains.append(Chain(send, keep, plan(SPLITS[1])))
    arrived = lax.optimization_barrier(
        (late,) + tuple(chain.terms[-1][0] for chain in chains[:first])
    )
    for chain, array in zip(chains, arrived[1:]):
        chain.terms[-1] = (array, chain.terms[-1][1])
    ffn_part = jnp.concatenate([chain.part(0, chain.rows, 0) for chain in chains[:first]], axis=0)
    ffn_sum = deep_sum(ffn_part)
    chains = chains[first:]
    after = turn(ffn_part, *TURNS[0])
    early = gate(early, [send, after])
    input_grad = input_back(early, late, wp_qkv, d_res1)
    after = turn(input_grad, *TURNS[1])
    ffn_sum = gate(ffn_sum, [after])
    ffn_other = flip(ffn_sum, 1)
    turn(ffn_sum, *TURNS[2])
    attn_halves = [item for chain in chains for item in chain.finish()]
    g_up, g_down = ffn_final(spot, ffn_sum, ffn_other, chunk_count)
    g_out, g_qkv, g_bqkv, g_bout, g_gain1, g_bias1, g_bup, g_bdown, g_gain2, g_bias2 = attn_final(
        spot, attn_halves, sizes, model, chunk_count
    )
    return (
        block_out,
        input_grad,
        g_qkv,
        g_bqkv,
        g_out,
        g_bout,
        g_gain1,
        g_bias1,
        g_up,
        g_bup,
        g_down,
        g_bdown,
        g_gain2,
        g_bias2,
    )


def solution(mesh):
    return jax.shard_map(
        body,
        mesh=mesh,
        in_specs=(
            P(("dp", "mx", "my"), None),
            P("mx", "my"),
            P(("mx", "my")),
            P("mx", "my"),
            P(("mx", "my")),
            P(("mx", "my")),
            P(("mx", "my")),
            P("mx", "my"),
            P(("mx", "my")),
            P("mx", "my"),
            P(("mx", "my")),
            P(("mx", "my")),
            P(("mx", "my")),
            P(("dp", "mx", "my")),
            P(("dp", "mx", "my"), None),
            P(("dp", "mx", "my"), None),
        ),
        out_specs=(
            P(("dp", "mx", "my"), None),
            P(("dp", "mx", "my"), None),
            P("mx", "my"),
            P(("mx", "my")),
            P("mx", "my"),
            P(("mx", "my")),
            P(("mx", "my")),
            P(("mx", "my")),
            P("mx", "my"),
            P(("mx", "my")),
            P("mx", "my"),
            P(("mx", "my")),
            P(("mx", "my")),
            P(("mx", "my")),
        ),
        check_vma=False,
    )
```
